32 devices in a mesh: group: 2 (over x), replica: 16 (over z, y, core).
Axes of the slice: x: 2, y: 2, z: 4, core: 2. Of those that a mesh axis runs over, the one named last changes fastest.
Arguments:
- images: bfloat16 [4, 64, 197, 384], P(None, ('group', 'replica')), may hold values from -6 to 6
- image_count: int32 [4, 32], P(None, ('group', 'replica')), may hold values from 1 to 2, as said below
- cotangent: bfloat16 [4, 64, 197, 384], P(None, ('group', 'replica')), may hold values from -6 to 6
- w_qkv: bfloat16 [384, 1152], P('group'), may hold values from -0.3125 to 0.3125
- b_qv: bfloat16 [768], P('group'), may hold values from -3 to 3
- w_out: bfloat16 [384, 384], P('group'), may hold values from -0.875 to 0.875
- b_out: bfloat16 [384], P('group'), may hold values from -3 to 3
- w_fc1: bfloat16 [384, 1536], P('group'), may hold values from -0.3125 to 0.3125
- b_fc1: bfloat16 [1536], P('group'), may hold values from -3 to 3
- w_fc2: bfloat16 [1536, 384], P('group'), may hold values from -0.15625 to 0.15625
- b_fc2: bfloat16 [384], P('group'), may hold values from -3 to 3
- gain_one: bfloat16 [384], P('group'), may hold values from 0.25 to 1.75
- shift_one: bfloat16 [384], P('group'), may hold values from -3 to 3
- gain_two: bfloat16 [384], P('group'), may hold values from 0.25 to 1.75
- shift_two: bfloat16 [384], P('group'), may hold values from -3 to 3
Outputs:
- outputs: bfloat16 [4, 64, 197, 384], P(None, ('group', 'replica'))
- input_grad: bfloat16 [4, 64, 197, 384], P(None, ('group', 'replica'))
- grad_w_qkv: float32 [384, 1152], P('group')
- grad_b_qv: float32 [768], P('group')
- grad_w_out: float32 [384, 384], P('group')
- grad_b_out: float32 [384], P('group')
- grad_w_fc1: float32 [384, 1536], P('group')
- grad_b_fc1: float32 [1536], P('group')
- grad_w_fc2: float32 [1536, 384], P('group')
- grad_b_fc2: float32 [384], P('group')
- grad_gain_one: float32 [384], P('group')
- grad_shift_one: float32 [384], P('group')
- grad_gain_two: float32 [384], P('group')
- grad_shift_two: float32 [384], P('group')
The draws below stay inside these ranges and needn't reach their ends.
Inputs may be any that keep to these rules, and one draw needn't show every extreme that they name: image_count[m, d] is the number of images in slots 2 d and 2 d + 1 of micro-batch m; slot 2 d always holds one, slot 2 d + 1 only where the entry is 2; each micro-batch has devices with 1 and with 2.
All inputs are finite; a program needn't handle non-finite values.
Results may differ from the reference program's by a relative error of at most 0.012.
Values may be sent and summed in bfloat16 or wider, within the bound.
No kernel may reach another device: no remote copies, remote signals or barrier semaphores. Data moves between devices by JAX's collectives and lax.ppermute only.
A program may use at most 128 MiB of HBM per device.

```python
import jax
import jax.numpy as jnp
from jax import lax

D = 384
HEADS = 6
FF = 1536
SEQ = 197
MICRO = 4
WORKERS = 32
SLOTS = 64


def draw_image_count(key, part):
    first, second = jax.random.split(jax.random.fold_in(key, 11))
    counts = jax.random.randint(first, (MICRO, WORKERS), 1, 3)
    chosen = jax.random.randint(second, (MICRO, 1), 0, WORKERS)
    column = jnp.arange(WORKERS, dtype=jnp.int32)[None, :]
    counts = jnp.where(column == chosen, 2, jnp.where(column == (chosen + 1) % WORKERS, 1, counts))
    return counts.astype(jnp.int32)


def level_of(rng, shape, shards, low, top_value):
    factor_of, own = 1.0, jax.random.fold_in(rng, 6)
    for dim, shards_of in shards:
        draws = jnp.exp(jax.random.uniform(jax.random.fold_in(own, dim), (shards_of,), jnp.float32, low / len(shards), top_value / len(shards)))
        factor_of = factor_of * jnp.repeat(draws, shape[dim] // shards_of).reshape([-1 if axis == dim else 1 for axis in range(len(shape))])
    return factor_of


def noise(own_key, dims, scale, bound, pieces=(), held_as=jnp.bfloat16):
    values = jax.random.normal(own_key, dims, jnp.float32) * scale
    if len(pieces) > 0:
        values = level_of(own_key, dims, pieces, -0.22, 0.18) * values
    return jnp.clip(values, min=-bound, max=bound).astype(held_as)


def setup_inputs(seed: int = 0) -> dict:
    streams_of = jax.random.split(jax.random.key(seed), 16)
    return {
        "images": noise(streams_of[0], (MICRO, SLOTS, SEQ, D), 1.0, 6.0, ((1, 32),)),
        "image_count": draw_image_count(jax.random.fold_in(streams_of[15], 71), 0),
        "cotangent": noise(streams_of[2], (MICRO, SLOTS, SEQ, D), 1.0, 6.0, ((1, 32),)),
        "w_qkv": noise(streams_of[3], (D, 3 * D), D ** -0.5, 0.3125, ((0, 2),)),
        "b_qv": noise(streams_of[4], (2 * D,), 0.5, 3.0, ((0, 2),)),
        "w_out": noise(streams_of[5], (D, D), (D // 8) ** -0.5, 0.875, ((0, 2),)),
        "b_out": noise(streams_of[6], (D,), 0.5, 3.0, ((0, 2),)),
        "w_fc1": noise(streams_of[7], (D, FF), D ** -0.5, 0.3125, ((0, 2),)),
        "b_fc1": noise(streams_of[8], (FF,), 0.5, 3.0, ((0, 2),)),
        "w_fc2": noise(streams_of[9], (FF, D), FF ** -0.5, 0.15625, ((0, 2),)),
        "b_fc2": noise(streams_of[10], (D,), 0.5, 3.0, ((0, 2),)),
        "gain_one": jnp.clip(1.0 + 0.15 * jax.random.normal(streams_of[11], (D,), jnp.float32), 0.25, 1.75).astype(jnp.bfloat16),
        "shift_one": noise(streams_of[12], (D,), 0.5, 3.0, ((0, 2),)),
        "gain_two": jnp.clip(1.0 + 0.15 * jax.random.normal(streams_of[13], (D,), jnp.float32), 0.25, 1.75).astype(jnp.bfloat16),
        "shift_two": noise(streams_of[14], (D,), 0.5, 3.0, ((0, 2),)),
    }


@jax.custom_vjp
def low(v):
    return lax.optimization_barrier(v.astype(jnp.bfloat16)).astype(jnp.float32)

@jax.custom_vjp
def low_back(v):
    return v

def low_keep(v):
    return (low(v), None)

def low_pass(kept, grad):
    return (grad,)

def back_keep(v):
    return (v, None)

def back_low(kept, grad):
    return (low(grad),)
low.defvjp(low_keep, low_pass)
low_back.defvjp(back_keep, back_low)

def layer_norm(values, gain, shift):
    center = values - lax.optimization_barrier(jnp.mean(values, axis=-1, keepdims=True))
    spread = lax.optimization_barrier(jnp.mean(center * center, axis=-1, keepdims=True))
    return center * lax.rsqrt(spread + 1e-06) * gain + shift

def encode(params, tokens, valid):
    w_qkv, b_qv, w_out, b_out, w_fc1, b_fc1, w_fc2, b_fc2, gain_one, shift_one, gain_two, shift_two = params
    highest = lax.Precision.HIGHEST
    count, length, width = tokens.shape
    head_size = width // HEADS
    normed = low(layer_norm(tokens, gain_one, shift_one))
    joined = jnp.einsum('bsd,de->bse', normed, w_qkv, precision=highest)
    bias = jnp.concatenate([b_qv[:width], jnp.zeros_like(b_qv[:width]), b_qv[width:]])
    joined = low(low_back(joined + bias))
    query = joined[..., :width].reshape(count, length, HEADS, head_size)
    keys = joined[..., width:2 * width].reshape(count, length, HEADS, head_size)
    values = joined[..., 2 * width:].reshape(count, length, HEADS, head_size)
    scores = low_back(jnp.einsum('bqhe,bkhe->bhqk', query, keys, precision=highest) * head_size ** (-0.5))
    lse = jax.nn.logsumexp(scores, axis=-1, keepdims=True)
    prob = low(jnp.exp(scores - lse))
    attended = jnp.einsum('bhqk,bkhe->bqhe', prob, values, precision=highest).reshape(count, length, width)
    attended = low(low_back(attended))
    branch = low_back(jnp.einsum('bsd,de->bse', attended, w_out, precision=highest) + b_out)
    middle = tokens + branch
    normed_two = low(layer_norm(middle, gain_two, shift_two))
    pre = low_back(jnp.einsum('bsd,df->bsf', normed_two, w_fc1, precision=highest) + b_fc1)
    act = low(jax.nn.gelu(pre, approximate=False))
    mlp = low_back(jnp.einsum('bsf,fd->bsd', act, w_fc2, precision=highest) + b_fc2)
    return (middle + mlp) * valid[:, None, None]

def reference(images, image_count, cotangent, w_qkv, b_qv, w_out, b_out, w_fc1, b_fc1, w_fc2, b_fc2, gain_one, shift_one, gain_two, shift_two):
    params = tuple((p.astype(jnp.float32) for p in (w_qkv, b_qv, w_out, b_out, w_fc1, b_fc1, w_fc2, b_fc2, gain_one, shift_one, gain_two, shift_two)))
    block_images = 16
    valid = (jnp.arange(2, dtype=jnp.int32)[None, None, :] < image_count[:, :, None]).astype(jnp.float32).reshape(-1, block_images)
    tokens = images.astype(jnp.float32).reshape(-1, block_images, SEQ, D)
    cot_blocks = cotangent.astype(jnp.float32).reshape(-1, block_images, SEQ, D)
    checked = jax.checkpoint(encode)

    def forward(weights, inputs):

        def step(carry, item):
            return (carry, checked(weights, item[0], item[1]))
        unused, result = lax.scan(step, jnp.zeros((), jnp.float32), (inputs, valid))
        return result
    result, pullback = jax.vjp(forward, params, tokens)
    grads, input_grad = pullback(cot_blocks)
    outputs = result.reshape(images.shape).astype(jnp.bfloat16)
    input_grad = input_grad.reshape(images.shape).astype(jnp.bfloat16)
    return (outputs, input_grad, grads[0], grads[1], grads[2], grads[3], grads[4], grads[5], grads[6], grads[7], grads[8], grads[9], grads[10], grads[11])
```

```python
from functools import partial

import jax
import jax.numpy as jnp
from jax import lax
from jax.experimental import pallas as pl
from jax.experimental.pallas import tpu as pltpu
from jax.sharding import PartitionSpec as P

HEADS = 6
ROWS = 208
KEYS = 256
F32 = jnp.float32
BF16 = jnp.bfloat16
NT = (((1,), (1,)), ((), ()))
TN = (((0,), (0,)), ((), ()))


def mm(a, b):
    return jnp.dot(a, b, preferred_element_type=F32)


def mm_nt(a, b):
    return lax.dot_general(a, b, NT, preferred_element_type=F32)


def mm_tn(a, b):
    return lax.dot_general(a, b, TN, preferred_element_type=F32)


def normalize(values):
    center = values - jnp.mean(values, axis=-1, keepdims=True)
    spread = jnp.mean(center * center, axis=-1, keepdims=True)
    rstd = lax.rsqrt(spread + 1e-06)
    return center * rstd, rstd


def norm_back(grad_normed, hat, rstd, gain):
    grad_hat = grad_normed * gain
    first = jnp.mean(grad_hat, axis=-1, keepdims=True)
    second = jnp.mean(grad_hat * hat, axis=-1, keepdims=True)
    return rstd * (grad_hat - first - hat * second)


def gelu_both(pre):
    density = jnp.exp(-0.5 * pre * pre)
    t = 1.0 / (1.0 + (0.3275911 * 0.7071067811865476) * jnp.abs(pre))
    poly = t * (
        0.254829592
        + t * (-0.284496736 + t * (1.421413741 + t * (-1.453152027 + t * 1.061405429)))
    )
    tail = 0.5 * poly * density
    cumulative = jnp.where(pre < 0.0, tail, 1.0 - tail)
    return cumulative, density * 0.3989422804014327


def rows_of(ref):
    return ref[0, 0].astype(F32)


def attention_kernel(x_ref, w_ref, b_ref, g_ref, s_ref, qkv_ref, prob_ref, att_ref, xs, kv):
    seq = x_ref.shape[2]
    width = x_ref.shape[3]

    @pl.when(pl.program_id(0) == 0)
    def _():
        xs[...] = jnp.zeros_like(xs)
        kv[...] = jnp.zeros_like(kv)

    xs[:seq, :] = rows_of(x_ref)
    hat, _ = normalize(xs[...])
    normed = (hat * g_ref[...] + s_ref[...]).astype(BF16)
    qkv = (mm(normed, w_ref[...]) + b_ref[...]).astype(BF16)
    qkv_ref[0] = qkv
    kv[:ROWS, :] = qkv[:, width:]
    low_half = lax.broadcasted_iota(jnp.int32, (1, 128), 1) < 64
    column = lax.broadcasted_iota(jnp.int32, (1, KEYS), 1)
    for pair in range(HEADS // 2):
        lanes = slice(pair * 128, pair * 128 + 128)
        query = qkv[:, lanes] * jnp.array(0.125, BF16)
        keys = kv[:, lanes]
        values = kv[:, width + pair * 128 : width + pair * 128 + 128]
        total = None
        for half in range(2):
            mask = low_half if half == 0 else jnp.logical_not(low_half)
            scores = mm_nt(query, jnp.where(mask, keys, jnp.zeros_like(keys)))
            scores = jnp.where(column < seq, scores, -1e30)
            top = jnp.max(scores, axis=-1, keepdims=True)
            grown = jnp.exp(scores - top)
            prob = (grown * (1.0 / jnp.sum(grown, axis=-1, keepdims=True))).astype(BF16)
            prob_ref[0, 2 * pair + half] = prob
            part = mm(prob, jnp.where(mask, values, jnp.zeros_like(values)))
            total = part if total is None else total + part
        att_ref[0, :, lanes] = total.astype(BF16)


def mlp_kernel(
    count_ref, x_ref, cot_ref, att_ref, wo_ref, bo_ref, w1_ref, b1_ref, w2_ref, b2_ref, g_ref, s_ref,
    out_ref, dx_ref, datt_ref, grads_ref,
    xs, dys, acts, dpres, gw1, gw2, gwo, gb1, gsmall,
):
    step = pl.program_id(0)
    seq = x_ref.shape[2]
    width = x_ref.shape[3]
    hidden = w1_ref.shape[1]

    @pl.when(step == 0)
    def _():
        for ref in (xs, dys, gw1, gw2, gwo, gb1, gsmall):
            ref[...] = jnp.zeros_like(ref)

    valid = (lax.rem(step, 2) < count_ref[lax.div(step, 2), 0]).astype(F32)
    xs[:seq, :] = rows_of(x_ref)
    dys[:seq, :] = rows_of(cot_ref) * valid
    att = att_ref[0]
    middle = xs[...] + mm(att, wo_ref[...]) + bo_ref[...]
    hat, rstd = normalize(middle)
    normed = (hat * g_ref[...] + s_ref[...]).astype(BF16)
    d_out = dys[...]
    d_mlp = d_out.astype(BF16)
    for chunk in range(hidden // 256):
        cols = slice(chunk * 256, chunk * 256 + 256)
        pre = mm(normed, w1_ref[:, cols]) + b1_ref[:, cols]
        d_act = mm_nt(d_mlp, w2_ref[cols, :])
        cumulative, density = gelu_both(pre)
        act = (pre * cumulative).astype(BF16)
        d_pre = (d_act * (cumulative + pre * density)).astype(BF16)
        acts[:, cols] = act
        dpres[:, cols] = d_pre
        gb1[:, cols] += jnp.sum(d_pre.astype(F32).reshape(ROWS // 8, 8, 256), axis=0)
        gw1[:, cols] += mm_tn(normed, d_pre)
        gw2[:, cols] += mm_tn(d_mlp, act)
    result = (middle + mm(acts[...], w2_ref[...]) + b2_ref[...]) * valid
    out_ref[0, 0] = result[:seq].astype(BF16)
    d_normed = mm_nt(dpres[...], w1_ref[...])
    dx = d_out + norm_back(d_normed, hat, rstd, g_ref[...])
    dx_ref[0] = dx
    d_attn = dx.astype(BF16)
    datt_ref[0] = mm_nt(d_attn, wo_ref[...]).astype(BF16)
    gwo[...] += mm_tn(att, d_attn)

    def fold(values):
        return jnp.sum(values.reshape(ROWS // 8, 8, width), axis=0)

    gsmall[0] += fold(d_mlp.astype(F32))
    gsmall[1] += fold(d_attn.astype(F32))
    gsmall[2] += fold(d_normed * hat)
    gsmall[3] += fold(d_normed)

    @pl.when(step == pl.num_programs(0) - 1)
    def _():
        half = width // 2
        quarter = half // 4
        wide = hidden // 2 // 4
        gw2_t = gw2[...].T
        for group in range(2):
            for part in range(4):
                base = group * half + part * quarter
                for col in range(hidden // width):
                    grads_ref[group, part, col * quarter : (col + 1) * quarter, :] = gw1[
                        base : base + quarter, col * width : (col + 1) * width
                    ].astype(BF16)
                top = hidden // width * quarter
                start = group * (hidden // 2) + part * wide
                grads_ref[group, part, top : top + wide, :] = gw2_t[start : start + wide].astype(BF16)
                top += wide
                grads_ref[group, part, top : top + quarter, :] = gwo[base : base + quarter, :].astype(BF16)
                top += quarter
                if part < 2:
                    start = group * (hidden // 2) + part * width
                    row = jnp.sum(gb1[:, start : start + width], axis=0, keepdims=True)
                else:
                    own = slice(group * half, group * half + half)
                    row = jnp.concatenate(
                        [
                            jnp.sum(gsmall[2 * part - 4][:, own], axis=0, keepdims=True),
                            jnp.sum(gsmall[2 * part - 3][:, own], axis=0, keepdims=True),
                        ],
                        axis=1,
                    )
                grads_ref[group, part, top : top + 16, :] = jnp.broadcast_to(row, (16, width)).astype(BF16)


def attention_back_kernel(
    x_ref, qkv_ref, prob_ref, att_ref, datt_ref, dx_ref, w_ref, g_ref, s_ref,
    din_ref, grads_ref,
    xs, kv, dqkv, gw, gb, gsmall,
):
    step = pl.program_id(0)
    seq = x_ref.shape[2]
    width = x_ref.shape[3]

    @pl.when(step == 0)
    def _():
        for ref in (xs, kv, gw, gb, gsmall):
            ref[...] = jnp.zeros_like(ref)

    xs[:seq, :] = rows_of(x_ref)
    hat, rstd = normalize(xs[...])
    normed = (hat * g_ref[...] + s_ref[...]).astype(BF16)
    kv[:ROWS, :] = qkv_ref[0, :, width:]
    low_half = lax.broadcasted_iota(jnp.int32, (1, 128), 1) < 64
    for pair in range(HEADS // 2):
        lanes = slice(pair * 128, pair * 128 + 128)
        query = qkv_ref[0, :, lanes] * jnp.array(0.125, BF16)
        keys = kv[:, lanes] * jnp.array(0.125, BF16)
        values = kv[:, width + pair * 128 : width + pair * 128 + 128]
        d_att = datt_ref[0, :, lanes]
        product = d_att.astype(F32) * att_ref[0, :, lanes].astype(F32)
        dq = dk = dv = None
        for half in range(2):
            mask = low_half if half == 0 else jnp.logical_not(low_half)
            prob = prob_ref[0, 2 * pair + half]
            delta = jnp.sum(jnp.where(mask, product, 0.0), axis=-1, keepdims=True)
            d_prob = mm_nt(d_att, jnp.where(mask, values, jnp.zeros_like(values)))
            d_scores = (prob.astype(F32) * (d_prob - delta)).astype(BF16)
            d_att_h = jnp.where(mask, d_att, jnp.zeros_like(d_att))
            query_h = jnp.where(mask, query, jnp.zeros_like(query))
            keys_h = jnp.where(mask, keys, jnp.zeros_like(keys))
            dv_h = mm_tn(prob, d_att_h)
            dk_h = mm_tn(d_scores, query_h)
            dq_h = mm(d_scores, keys_h)
            dq = dq_h if dq is None else dq + dq_h
            dk = dk_h if dk is None else dk + dk_h
            dv = dv_h if dv is None else dv + dv_h
        dqkv[:, lanes] = dq.astype(BF16)
        dqkv[:, width + pair * 128 : width + pair * 128 + 128] = dk[:ROWS].astype(BF16)
        dqkv[:, 2 * width + pair * 128 : 2 * width + pair * 128 + 128] = dv[:ROWS].astype(BF16)
    d_joined = dqkv[...]
    d_normed = mm_nt(d_joined, w_ref[...])
    gw[...] += mm_tn(normed, d_joined)
    gb[...] += jnp.sum(d_joined.astype(F32).reshape(ROWS // 8, 8, 3 * width), axis=0)
    d_in = dx_ref[0] + norm_back(d_normed, hat, rstd, g_ref[...])
    din_ref[0, 0] = d_in[:seq].astype(BF16)

    def fold(values):
        return jnp.sum(values.reshape(ROWS // 8, 8, width), axis=0)

    gsmall[0] += fold(d_normed * hat)
    gsmall[1] += fold(d_normed)

    @pl.when(step == pl.num_programs(0) - 1)
    def _():
        half = width // 2
        quarter = half // 4
        for group in range(2):
            for part in range(4):
                base = group * half + part * quarter
                for col in range(3):
                    grads_ref[group, part, col * quarter : (col + 1) * quarter, :] = gw[
                        base : base + quarter, col * width : (col + 1) * width
                    ].astype(BF16)
                top = 3 * quarter
                if part == 0:
                    row = jnp.sum(gb[:, 2 * group * width : (2 * group + 1) * width], axis=0, keepdims=True)
                else:
                    own = slice(group * half, group * half + half)
                    row = jnp.concatenate(
                        [
                            jnp.sum(gsmall[0][:, own], axis=0, keepdims=True),
                            jnp.sum(gsmall[1][:, own], axis=0, keepdims=True),
                        ],
                        axis=1,
                    )
                grads_ref[group, part, top : top + 16, :] = jnp.broadcast_to(row, (16, width)).astype(BF16)


def whole(array):
    return pl.BlockSpec(array.shape, lambda i: (0,) * len(array.shape))


def per_image(*shape):
    return pl.BlockSpec((1, *shape), lambda i: (i,) + (0,) * len(shape))


def slot_block(seq, width):
    return pl.BlockSpec((1, 1, seq, width), lambda i: (i // 2, i % 2, 0, 0))


def run_attention(images, w_qkv, bias, gain, shift):
    micro, slots, seq, width = images.shape
    count = micro * slots
    return pl.pallas_call(
        attention_kernel,
        grid=(count,),
        in_specs=[slot_block(seq, width), whole(w_qkv), whole(bias), whole(gain), whole(shift)],
        out_specs=[per_image(ROWS, 3 * width), per_image(HEADS, ROWS, KEYS), per_image(ROWS, width)],
        out_shape=[
            jax.ShapeDtypeStruct((count, ROWS, 3 * width), BF16),
            jax.ShapeDtypeStruct((count, HEADS, ROWS, KEYS), BF16),
            jax.ShapeDtypeStruct((count, ROWS, width), BF16),
        ],
        scratch_shapes=[pltpu.VMEM((ROWS, width), F32), pltpu.VMEM((KEYS, 2 * width), BF16)],
        compiler_params=pltpu.CompilerParams(vmem_limit_bytes=40 << 20),
        cost_estimate=pl.CostEstimate(flops=3 << 30, bytes_accessed=20 << 20, transcendentals=0),
        name="attention_fwd",
    )(images, w_qkv, bias, gain, shift)


def run_mlp(counts, images, cotangent, att, wo, bo, w1, b1, w2, b2, gain, shift):
    micro, slots, seq, width = images.shape
    hidden = w1.shape[1]
    count = micro * slots
    rows = width // 8 * (hidden // width) + hidden // 8 + width // 8 + 16
    return pl.pallas_call(
        mlp_kernel,
        grid=(count,),
        in_specs=[
            pl.BlockSpec(memory_space=pltpu.SMEM),
            slot_block(seq, width),
            slot_block(seq, width),
            per_image(ROWS, width),
        ]
        + [whole(v) for v in (wo, bo, w1, b1, w2, b2, gain, shift)],
        out_specs=[
            slot_block(seq, width),
            per_image(ROWS, width),
            per_image(ROWS, width),
            pl.BlockSpec((2, 4, rows, width), lambda i: (0, 0, 0, 0)),
        ],
        out_shape=[
            jax.ShapeDtypeStruct(images.shape, BF16),
            jax.ShapeDtypeStruct((count, ROWS, width), F32),
            jax.ShapeDtypeStruct((count, ROWS, width), BF16),
            jax.ShapeDtypeStruct((2, 4, rows, width), BF16),
        ],
        scratch_shapes=[
            pltpu.VMEM((ROWS, width), F32),
            pltpu.VMEM((ROWS, width), F32),
            pltpu.VMEM((ROWS, hidden), BF16),
            pltpu.VMEM((ROWS, hidden), BF16),
            pltpu.VMEM((width, hidden), F32),
            pltpu.VMEM((width, hidden), F32),
            pltpu.VMEM((width, width), F32),
            pltpu.VMEM((8, hidden), F32),
            pltpu.VMEM((4, 8, width), F32),
        ],
        compiler_params=pltpu.CompilerParams(vmem_limit_bytes=60 << 20),
        cost_estimate=pl.CostEstimate(flops=12 << 30, bytes_accessed=20 << 20, transcendentals=0),
        name="mlp_fwd_bwd",
    )(counts, images, cotangent, att, wo, bo, w1, b1, w2, b2, gain, shift)


def run_attention_back(images, qkv, prob, att, datt, dx, w_qkv, gain, shift):
    micro, slots, seq, width = images.shape
    count = micro * slots
    rows = width // 8 * 3 + 16
    return pl.pallas_call(
        attention_back_kernel,
        grid=(count,),
        in_specs=[
            slot_block(seq, width),
            per_image(ROWS, 3 * width),
            per_image(HEADS, ROWS, KEYS),
            per_image(ROWS, width),
            per_image(ROWS, width),
            per_image(ROWS, width),
        ]
        + [whole(v) for v in (w_qkv, gain, shift)],
        out_specs=[slot_block(seq, width), pl.BlockSpec((2, 4, rows, width), lambda i: (0, 0, 0, 0))],
        out_shape=[
            jax.ShapeDtypeStruct(images.shape, BF16),
            jax.ShapeDtypeStruct((2, 4, rows, width), BF16),
        ],
        scratch_shapes=[
            pltpu.VMEM((ROWS, width), F32),
            pltpu.VMEM((KEYS, 2 * width), BF16),
            pltpu.VMEM((ROWS, 3 * width), BF16),
            pltpu.VMEM((width, 3 * width), F32),
            pltpu.VMEM((8, 3 * width), F32),
            pltpu.VMEM((2, 8, width), F32),
        ],
        compiler_params=pltpu.CompilerParams(vmem_limit_bytes=60 << 20),
        cost_estimate=pl.CostEstimate(flops=8 << 30, bytes_accessed=20 << 20, transcendentals=0),
        name="attention_bwd",
    )(images, qkv, prob, att, datt, dx, w_qkv, gain, shift)


def flip(value, axis, size, bit):
    return lax.ppermute(value, axis, [(i, i ^ bit) for i in range(size)])


def reduce_grads(grads, replicas):
    group = lax.axis_index("group")
    replica = lax.axis_index("replica")
    core = replica & 1
    side = (replica >> 1) & 1
    take = lambda value, index, size, dim: lax.dynamic_slice_in_dim(value, index * size, size, dim)
    other = flip(take(grads, 1 - core, 2, 1), "replica", replicas, 1)
    grads = take(grads, core, 2, 1) + other
    other = flip(take(grads, 1 - group, 1, 0), "group", 2, 1)
    grads = (take(grads, group, 1, 0) + other)[0]
    other = flip(take(grads, 1 - side, 1, 0), "replica", replicas, 2)
    grads = take(grads, side, 1, 0) + other
    bit = 4
    while bit < replicas:
        grads = grads + flip(grads, "replica", replicas, bit)
        bit *= 2
    other = flip(grads, "replica", replicas, 2)
    grads = jnp.where(side == 0, jnp.concatenate([grads, other]), jnp.concatenate([other, grads]))
    other = flip(grads, "replica", replicas, 1)
    return jnp.where(core == 0, jnp.concatenate([grads, other]), jnp.concatenate([other, grads]))


def local(
    replicas,
    images, image_count, cotangent, w_qkv, b_qv, w_out, b_out, w_fc1, b_fc1, w_fc2, b_fc2,
    gain_one, shift_one, gain_two, shift_two,
):
    group = lax.axis_index("group")

    def full(mine):
        theirs = flip(mine, "group", 2, 1)
        return jnp.where(group == 0, jnp.concatenate([mine, theirs]), jnp.concatenate([theirs, mine]))

    width = images.shape[3]
    hidden = w_fc1.shape[1]
    small = jnp.concatenate([b_qv, b_out, b_fc1, b_fc2, gain_one, shift_one, gain_two, shift_two])
    small = full(small[None]).astype(F32)
    half = width // 2
    offsets = {}
    at = 0
    for name, size in (
        ("b_qv", width), ("b_out", half), ("b_fc1", hidden // 2), ("b_fc2", half),
        ("gain_one", half), ("shift_one", half), ("gain_two", half), ("shift_two", half),
    ):
        offsets[name] = small[:, at : at + size].reshape(1, -1)
        at += size
    bias = offsets["b_qv"]
    bias = jnp.concatenate([bias[:, :width], jnp.zeros_like(bias[:, :width]), bias[:, width:]], axis=1)
    w_qkv_all = full(w_qkv)
    qkv, prob, att = run_attention(images, w_qkv_all, bias, offsets["gain_one"], offsets["shift_one"])
    outputs, dx, datt, grads_b = run_mlp(
        image_count, images, cotangent, att,
        full(w_out), offsets["b_out"], full(w_fc1), offsets["b_fc1"], full(w_fc2), offsets["b_fc2"],
        offsets["gain_two"], offsets["shift_two"],
    )
    input_grad, grads_c = run_attention_back(
        images, qkv, prob, att, datt, dx, w_qkv_all, offsets["gain_one"], offsets["shift_one"]
    )
    sums_b = reduce_grads(grads_b, replicas).astype(F32)
    sums_c = reduce_grads(grads_c, replicas).astype(F32)
    quarter = half // 4
    wide = hidden // 8

    def unfold(block):
        rows = block.shape[1]
        return block.reshape(4, rows // quarter, quarter, width).transpose(0, 2, 1, 3).reshape(half, -1)

    top = hidden // width * quarter
    g_fc1 = unfold(sums_b[:, :top])
    g_fc2 = sums_b[:, top : top + wide].reshape(hidden // 2, width)
    g_out = sums_b[:, top + wide : top + wide + quarter].reshape(half, width)
    rows = sums_b[:, top + wide + quarter]
    g_qkv = unfold(sums_c[:, : 3 * quarter])
    last = sums_c[:, 3 * quarter]
    return (
        outputs, input_grad, g_qkv, last[0], g_out, rows[2, half:], g_fc1, rows[:2].reshape(-1),
        g_fc2, rows[2, :half], last[1, :half], last[1, half:], rows[3, :half], rows[3, half:],
    )


def solution(mesh):
    split = P(None, ("group", "replica"), None, None)
    matrix, vector = P("group", None), P("group")
    return jax.shard_map(
        partial(local, mesh.shape["replica"]),
        mesh=mesh,
        in_specs=(split, P(None, ("group", "replica")), split)
        + (matrix, vector) * 4
        + (vector,) * 4,
        out_specs=(split, split) + (matrix, vector) * 4 + (vector,) * 4,
        check_vma=False,
    )
```

```python
from functools import partial

import jax
import jax.numpy as jnp
from jax import lax
from jax.experimental import pallas as pl
from jax.experimental.layout import Layout, with_layout_constraint
from jax.experimental.pallas import tpu as pltpu
from jax.sharding import PartitionSpec as P


HEADS = 6
ROWS = 208
KEYS = 256
F32 = jnp.float32
BF16 = jnp.bfloat16
NT = (((1,), (1,)), ((), ()))
TN = (((0,), (0,)), ((), ()))


def mm(a, b):
    return jnp.dot(a, b, preferred_element_type=F32)


def mm_nt(a, b):
    return lax.dot_general(a, b, NT, preferred_element_type=F32)


def mm_tn(a, b):
    return lax.dot_general(a, b, TN, preferred_element_type=F32)


def normalize(values):
    center = values - jnp.mean(values, axis=-1, keepdims=True)
    spread = jnp.mean(center * center, axis=-1, keepdims=True)
    rstd = lax.rsqrt(spread + 1e-06)
    return center * rstd, rstd


def norm_back(grad_normed, hat, rstd, gain):
    grad_hat = grad_normed * gain
    first = jnp.mean(grad_hat, axis=-1, keepdims=True)
    second = jnp.mean(grad_hat * hat, axis=-1, keepdims=True)
    return rstd * (grad_hat - first - hat * second)


def gelu_parts(pre, d_act):
    size = jnp.abs(pre)
    density = jnp.exp2(pre * (pre * -0.7213475204444817))
    t = 1.0 / (1.0 + 0.2316418882663604 * size)
    poly = t * (
        0.127414796
        + t * (-0.142248368 + t * (0.7107068705 + t * (-0.7265760135 + t * 0.5307027145)))
    )
    act = jnp.maximum(pre, 0.0) - size * (poly * density)
    edge = density * (poly - 0.3989422804014327 * size)
    slope = jnp.where(pre < 0.0, edge, 1.0 - edge)
    return act.astype(BF16), (d_act * slope).astype(BF16)


def read_image(ref, micro, slot, seq, target, top):
    tiles = target.shape[1] // 128
    for tile in range(tiles):
        start = micro * (seq * tiles * 2) + 2 * tile + slot
        target[top : top + seq, tile * 128 : tile * 128 + 128] = ref[pl.ds(start, seq, stride=2 * tiles), :]


def write_image(ref, micro, slot, seq, value):
    tiles = value.shape[1] // 128
    for tile in range(tiles):
        start = micro * (seq * tiles * 2) + 2 * tile + slot
        ref[pl.ds(start, seq, stride=2 * tiles), :] = value[:seq, tile * 128 : tile * 128 + 128]


def joined(first, second, row, size):
    return jnp.concatenate([first[row : row + 1, :size], second[row : row + 1, :size]], axis=1)


def ordered(idx_ref, mine, theirs):
    low = idx_ref[0] == 0
    mine, theirs = mine.astype(F32), theirs.astype(F32)
    return jnp.where(low, mine, theirs), jnp.where(low, theirs, mine)


def at(start, size):
    return pl.ds(pl.multiple_of(start, 16), size)


VMEM_SPEC = pl.BlockSpec(memory_space=pltpu.VMEM)


def pack_first_kernel(idx_ref, wq_ref, *refs):
    vectors, first_ref, small_ref = refs[:-2], refs[-2], refs[-1]
    part = wq_ref.shape[0]
    small_ref[...] = jnp.zeros_like(small_ref)
    for k, ref in enumerate(vectors):
        size = ref.shape[0]
        small_ref[k : k + 1, :size] = ref[...].reshape(1, size)
    first_ref[:part, :] = wq_ref[...]
    first_ref[part:, :] = jnp.zeros((16, first_ref.shape[1]), BF16)
    first_ref[part : part + 8, : small_ref.shape[1]] = small_ref[...]


def pack_second_kernel(idx_ref, wo_ref, w1_ref, w2_ref, second_ref):
    part, width = wo_ref.shape
    hidden = w1_ref.shape[1]
    second_ref[:, :width] = wo_ref[...]
    second_ref[:, width : width + hidden] = w1_ref[...]
    for k in range(hidden // width):
        second_ref[:, width + hidden + k * width : width + hidden + (k + 1) * width] = w2_ref[
            k * part : (k + 1) * part, :
        ]


def own_rows(rows, columns):
    return pl.BlockSpec((rows, columns), lambda i, idx: (idx[1], 0))


def run_pack_first(idx, w_qkv, vectors):
    half, wide = w_qkv.shape
    longest = max(v.shape[0] for v in vectors)
    shapes = [(half // 2 + 16, wide), (8, longest)]
    return pl.pallas_call(
        pack_first_kernel,
        grid_spec=pltpu.PrefetchScalarGridSpec(
            num_scalar_prefetch=1,
            grid=(1,),
            in_specs=[own_rows(half // 2, wide)] + [pl.BlockSpec(v.shape, lambda i, idx: (0,)) for v in vectors],
            out_specs=[pl.BlockSpec(s, lambda i, idx: (0, 0)) for s in shapes],
        ),
        out_shape=[jax.ShapeDtypeStruct(s, BF16) for s in shapes],
        name="pack_first",
    )(idx, w_qkv, *vectors)


def run_pack_second(idx, w_out, w_fc1, w_fc2):
    half, width = w_out.shape
    hidden = w_fc1.shape[1]
    part = half // 2
    shape = (part, width + 2 * hidden)
    return pl.pallas_call(
        pack_second_kernel,
        grid_spec=pltpu.PrefetchScalarGridSpec(
            num_scalar_prefetch=1,
            grid=(1,),
            in_specs=[own_rows(part, width), own_rows(part, hidden), own_rows(hidden // 4, width)],
            out_specs=pl.BlockSpec(shape, lambda i, idx: (0, 0)),
        ),
        out_shape=jax.ShapeDtypeStruct(shape, BF16),
        name="pack_second",
    )(idx, w_out, w_fc1, w_fc2)


def attention_kernel(
    idx_ref, x_ref, w_ref, near_ref, far_ref, small_ref,
    qkv_ref, prob_ref, att_ref, whole_ref, vec_ref,
    view, xs, kv, bias, scores,
):
    step = pl.program_id(0)
    half, wide = w_ref.shape
    width = wide // 3
    part = half // 2
    pairs = width // 128
    seq = x_ref.shape[0] * 128 // (width * pl.num_programs(0))

    @pl.when(step == 0)
    def _():
        view[...] = x_ref[...].astype(F32)
        xs[...] = jnp.zeros_like(xs)
        kv[...] = jnp.zeros_like(kv)
        group, core = idx_ref[0], idx_ref[1]
        first, second = ordered(idx_ref, small_ref[...], near_ref[part : part + 8, : small_ref.shape[1]])
        vec_ref[0:1, :] = joined(first, second, 4, half)
        vec_ref[1:2, :] = joined(first, second, 5, half)
        other = (1 - group) * half
        for pair in range(pairs):
            for kind in range(3):
                source = slice(kind * width + pair * 128, kind * width + pair * 128 + 128)
                target = slice((3 * pair + kind) * 128, (3 * pair + kind) * 128 + 128)
                whole_ref[at(group * half, half), target] = w_ref[:, source]
                whole_ref[at(other + core * part, part), target] = near_ref[:part, source]
                whole_ref[at(other + (1 - core) * part, part), target] = far_ref[:part, source]
                lanes = slice(pair * 128, pair * 128 + 128)
                piece = (first[0:1, lanes], jnp.zeros((1, 128), F32), second[0:1, lanes])[kind]
                bias[0:1, target] = piece

    read_image(view, lax.div(step, 2), lax.rem(step, 2), seq, xs, 0)
    hat, _ = normalize(xs[...])
    normed = (hat * vec_ref[0:1, :] + vec_ref[1:2, :]).astype(BF16)
    low_half = lax.broadcasted_iota(jnp.int32, (1, 128), 1) < 64
    column = lax.broadcasted_iota(jnp.int32, (1, KEYS), 1)

    def project(pair):
        lanes = slice(pair * 384, pair * 384 + 384)
        qkv = (mm(normed, whole_ref[:, lanes]) + bias[0:1, lanes]).astype(BF16)
        qkv_ref[0, :, lanes] = qkv
        kv[:ROWS, pair * 256 : pair * 256 + 256] = qkv[:, 128:]

    def masked(values, head):
        mask = low_half if head % 2 == 0 else jnp.logical_not(low_half)
        return jnp.where(mask, values, jnp.zeros_like(values))

    def first_part(head):
        pair = head // 2
        query = qkv_ref[0, :, pair * 384 : pair * 384 + 128] * jnp.array(0.125, BF16)
        scores[head % 2] = mm_nt(query, masked(kv[:, pair * 256 : pair * 256 + 128], head))

    def second_part(head):
        for r in range(0, ROWS, 16):
            value = jnp.where(column < seq, scores[head % 2, r : r + 16], -1e30)
            top = jnp.max(value, axis=-1, keepdims=True)
            grown = jnp.exp(value - top)
            prob_ref[0, head, r : r + 16] = (grown * (1.0 / jnp.sum(grown, axis=-1, keepdims=True))).astype(BF16)

    def third_part(head):
        pair = head // 2
        values = kv[:, pair * 256 + 128 : pair * 256 + 256]
        if head % 2 == 1:
            total = mm(prob_ref[0, head - 1], masked(values, 0)) + mm(prob_ref[0, head], masked(values, 1))
            att_ref[0, :, pair * 128 : pair * 128 + 128] = total.astype(BF16)

    project(0)
    for k in range(HEADS + 2):
        if k < HEADS:
            first_part(k)
        if k % 2 == 0 and k // 2 + 1 < pairs:
            project(k // 2 + 1)
        if k >= 2:
            third_part(k - 2)
        if 1 <= k <= HEADS:
            second_part(k - 1)


def mlp_kernel(
    idx_ref, count_ref, x_ref, cot_ref, att_ref, wo_ref, w1_ref, w2_ref, near_ref, far_ref, small_ref, first_ref,
    out_ref, dx_ref, datt_ref, keep_ref, send_ref,
    view_x, view_c, xs, dys, acts, dpres, pres, dacts, wo, w1, w2, wot, w1t, w2t, vec, b1, out_half, dn_half,
    gw1, gw2, gwo, gsmall,
):
    step = pl.program_id(0)
    last = pl.num_programs(0) - 1
    half, width = wo_ref.shape
    hidden = w1_ref.shape[1]
    part = half // 2
    rows = xs.shape[0]
    seq = x_ref.shape[0] * 128 // (width * 2 * pl.num_programs(0))
    core = idx_ref[1]

    @pl.when(step == 0)
    def _():
        view_x[...] = x_ref[...].astype(F32)
        view_c[...] = cot_ref[...].astype(F32)
        for ref in (xs, dys, gw1, gw2, gwo, gsmall):
            ref[...] = jnp.zeros_like(ref)
        group = idx_ref[0]
        wo[at(group * half, half), :] = wo_ref[...]
        w1[at(group * half, half), :] = w1_ref[...]
        w2[at(group * (hidden // 2), hidden // 2), :] = w2_ref[...]
        other = (1 - group) * half
        for ref, which in ((near_ref, core), (far_ref, 1 - core)):
            wo[at(other + which * part, part), :] = ref[:, :width]
            w1[at(other + which * part, part), :] = ref[:, width : width + hidden]
            base = (1 - group) * (hidden // 2) + which * (hidden // 4)
            for k in range(hidden // width):
                w2[at(base + k * part, part), :] = ref[:, width + hidden + k * width : width + hidden + (k + 1) * width]
        wot[...] = wo[...].T
        w1t[...] = w1[...].T
        w2t[...] = w2[...].T
        first, second = ordered(idx_ref, small_ref[...], first_ref[part : part + 8, : small_ref.shape[1]])
        vec[0:1, :] = joined(first, second, 1, half)
        vec[1:2, :] = joined(first, second, 3, half)
        vec[2:3, :] = joined(first, second, 6, half)
        vec[3:4, :] = joined(first, second, 7, half)
        b1[0:1, : hidden // 2] = first[2:3, :]
        b1[0:1, hidden // 2 :] = second[2:3, :]

    second_valid = (1 < count_ref[step, 0]).astype(F32)
    for slot in range(2):
        read_image(view_x, step, slot, seq, xs, slot * ROWS)
        read_image(view_c, step, slot, seq, dys, slot * ROWS)
    row = lax.broadcasted_iota(jnp.int32, (rows, 1), 0)
    valid = jnp.where(row < ROWS, 1.0, second_valid)
    att = att_ref[...].reshape(rows, width)
    middle = xs[...] + mm(att, wo[...]) + vec[0:1, :]
    hat, rstd = normalize(middle)
    gain = vec[2:3, :]
    normed = (hat * gain + vec[3:4, :]).astype(BF16)
    d_out = dys[...] * valid
    d_mlp = d_out.astype(BF16)
    normed_t = jnp.concatenate([normed.T, jnp.ones((16, rows), BF16)], axis=0)
    d_mlp_t = d_mlp.T
    chunks = hidden // 256
    middle_of = hidden // 2

    def first_part(c):
        cols = slice(c * 256, c * 256 + 256)
        pres[c % 2] = mm(normed, w1[:, cols])
        dacts[c % 2] = mm(d_mlp, w2t[:, cols])

    def second_part(c):
        cols = slice(c * 256, c * 256 + 256)
        bias = b1[0:1, cols]
        for r in range(0, rows, 32):
            act, d_pre = gelu_parts(pres[c % 2, r : r + 32] + bias, dacts[c % 2, r : r + 32])
            acts[r : r + 32, cols] = act
            dpres[r : r + 32, cols] = d_pre

    def third_part(c):
        cols = slice(c * 256, c * 256 + 256)
        gw1[:, cols] += mm(normed_t, dpres[:, cols])
        gw2[:, cols] += mm(d_mlp_t, acts[:, cols])

    for k in range(chunks + 2):
        if k < chunks:
            first_part(k)
        if k >= 2:
            third_part(k - 2)
        if k == chunks // 2 + 1:
            out_half[...] = mm(acts[:, :middle_of], w2[:middle_of, :])
            dn_half[...] = mm(dpres[:, :middle_of], w1t[:middle_of, :])
        if 1 <= k <= chunks:
            second_part(k - 1)

    result = (middle + out_half[...] + mm(acts[:, middle_of:], w2[middle_of:, :]) + vec[1:2, :]) * valid
    for slot in range(2):
        write_image(view_x, step, slot, seq, result[slot * ROWS : slot * ROWS + ROWS])
    d_normed = dn_half[...] + mm(dpres[:, middle_of:], w1t[middle_of:, :])
    dx = d_out + norm_back(d_normed, hat, rstd, gain)
    dx_ref[...] = dx.reshape(2, ROWS, width)
    d_attn = dx.astype(BF16)
    datt_ref[...] = mm(d_attn, wot[...]).astype(BF16).reshape(2, ROWS, width)
    gwo[...] += mm_tn(att, d_attn)

    def fold(values):
        return jnp.sum(values.reshape(rows // 8, 8, width), axis=0)

    gsmall[0] += fold(d_out)
    gsmall[1] += fold(d_attn.astype(F32))
    gsmall[2] += fold(d_normed * hat)
    gsmall[3] += fold(d_normed)

    @pl.when(step == last)
    def _():
        out_ref[...] = view_x[...].astype(BF16)
        quarter = half // 4
        wide = hidden // 8
        gw2_t = gw2[...].T
        small_rows = [jnp.sum(gsmall[k], axis=0, keepdims=True) for k in range(4)]

        def emit(group, quad, ref, side):
            base = group * half + quad * quarter
            top = 0
            for col in range(hidden // width):
                ref[group, side, top : top + quarter, :] = gw1[
                    base : base + quarter, col * width : (col + 1) * width
                ].astype(BF16)
                top += quarter
            start = group * (hidden // 2) + quad * wide
            ref[group, side, top : top + wide, :] = gw2_t[start : start + wide].astype(BF16)
            top += wide
            ref[group, side, top : top + quarter, :] = gwo[base : base + quarter, :].astype(BF16)
            top += quarter
            if quad < 2:
                start = group * (hidden // 2) + quad * width
                value = gw1[width : width + 1, start : start + width]
            else:
                own = slice(group * half, group * half + half)
                value = jnp.concatenate(
                    [small_rows[2 * quad - 4][:, own], small_rows[2 * quad - 3][:, own]], axis=1
                )
            ref[group, side, top : top + 16, :] = jnp.broadcast_to(value, (16, width)).astype(BF16)

        split_quads(core, emit, keep_ref, send_ref)


def split_quads(core, emit, keep_ref, send_ref):
    for mine in range(2):

        @pl.when(core == mine)
        def _():
            for group in range(2):
                for side in range(2):
                    emit(group, 2 * mine + side, keep_ref, side)
                    emit(group, 2 * (1 - mine) + side, send_ref, side)


def attention_back_kernel(
    first_image, last, idx_ref, x_ref, qkv_ref, prob_ref, att_ref, datt_ref, w_ref, vec_ref, *refs
):
    carried = 0 if first_image == 0 else 3
    dqkv_ref, total_ref, sums_ref = refs[carried : carried + 3]
    view, xs, kv, hat_t, d_probs, d_scores = refs[-6:]
    step = pl.program_id(0)
    width = w_ref.shape[0]
    seq = x_ref.shape[0] * 128 // (width * qkv_ref.shape[0] * 8)
    image = first_image + step
    pairs = width // 128

    @pl.when(step == 0)
    def _():
        view[...] = x_ref[...].astype(F32)
        xs[...] = jnp.zeros_like(xs)
        kv[...] = jnp.zeros_like(kv)
        total_ref[...] = refs[1][...] if carried else jnp.zeros_like(total_ref)
        sums_ref[...] = refs[2][...] if carried else jnp.zeros_like(sums_ref)

    read_image(view, lax.div(image, 2), lax.rem(image, 2), seq, xs, 0)
    hat, _ = normalize(xs[...])
    hat_t[...] = hat.astype(BF16).T
    for pair in range(pairs):
        kv[:ROWS, pair * 256 : pair * 256 + 256] = qkv_ref[0, :, pair * 384 + 128 : pair * 384 + 384]
    low_half = lax.broadcasted_iota(jnp.int32, (1, 128), 1) < 64

    def masked(values, head):
        mask = low_half if head % 2 == 0 else jnp.logical_not(low_half)
        return jnp.where(mask, values, jnp.zeros_like(values))

    def lanes(head):
        return slice(head // 2 * 128, head // 2 * 128 + 128)

    def first_part(head):
        pair = head // 2
        d_probs[head % 2] = mm_nt(
            datt_ref[0, :, lanes(head)], masked(kv[:, pair * 256 + 128 : pair * 256 + 256], head)
        )

    def second_part(head):
        for r in range(0, ROWS, 16):
            rows = slice(r, r + 16)
            product = datt_ref[0, rows, lanes(head)].astype(F32) * att_ref[0, rows, lanes(head)].astype(F32)
            delta = jnp.sum(masked(product, head), axis=-1, keepdims=True)
            d_scores[head % 4, rows] = (
                prob_ref[0, head, rows].astype(F32) * (d_probs[head % 2, rows] - delta)
            ).astype(BF16)

    def third_part(pair):
        query = qkv_ref[0, :, pair * 384 : pair * 384 + 128] * jnp.array(0.125, BF16)
        keys = kv[:, pair * 256 : pair * 256 + 128] * jnp.array(0.125, BF16)
        d_att = datt_ref[0, :, pair * 128 : pair * 128 + 128]
        dq = dk = dv = 0.0
        for head in (2 * pair, 2 * pair + 1):
            d_score = d_scores[head % 4]
            dv = dv + mm_tn(prob_ref[0, head], masked(d_att, head))
            dk = dk + mm_tn(d_score, masked(query, head))
            dq = dq + mm(d_score, masked(keys, head))
        top = pair * 384
        dqkv_ref[0, :, top : top + 128] = dq.astype(BF16)
        dqkv_ref[0, :, top + 128 : top + 256] = dk[:ROWS].astype(BF16)
        dqkv_ref[0, :, top + 256 : top + 384] = dv[:ROWS].astype(BF16)

    def fourth_part(pair):
        columns = slice(pair * 384, pair * 384 + 384)
        joined_back = dqkv_ref[0, :, columns]
        total_ref[:, columns] += mm(hat_t[...], joined_back)
        sums_ref[:, columns] += jnp.sum(joined_back.astype(F32).reshape(ROWS // 8, 8, 384), axis=0)

    for k in range(HEADS + 3):
        if k < HEADS:
            first_part(k)
        if k >= 3 and k % 2 == 1:
            third_part(k // 2 - 1)
        if k >= 4 and k % 2 == 0:
            fourth_part(k // 2 - 2)
        if 1 <= k <= HEADS:
            second_part(k - 1)

    if last:
        keep_ref, send_ref = refs[carried + 3 : carried + 5]

        @pl.when(step == pl.num_programs(0) - 1)
        def _():
            half = width // 2
            quarter = half // 4
            total_sums = jnp.sum(sums_ref[...], axis=0, keepdims=True)
            weights = w_ref[...].astype(F32)
            d_gain = jnp.sum((weights * total_ref[...]).reshape(width, 3 * width), axis=1, keepdims=True)
            d_shift = jnp.sum(weights * total_sums, axis=1, keepdims=True)
            columns = jnp.concatenate([vec_ref[...], jnp.zeros((120, width), F32)], axis=0).T
            gain, shift = columns[:, 0:1], columns[:, 1:2]
            total_ref[...] = total_ref[...] * gain + shift * total_sums
            lane = lax.broadcasted_iota(jnp.int32, (1, 128), 1)
            both = jnp.where(lane == 0, d_gain, jnp.where(lane == 1, d_shift, 0.0)).T

            def emit(group, quad, ref, side):
                base = group * half + quad * quarter
                for kind in range(3):
                    for pair in range(pairs):
                        source = slice((3 * pair + kind) * 128, (3 * pair + kind) * 128 + 128)
                        ref[group, side, kind * quarter : (kind + 1) * quarter, pair * 128 : pair * 128 + 128] = (
                            total_ref[base : base + quarter, source].astype(BF16)
                        )
                if quad == 0:
                    kind = 2 * group
                    value = jnp.concatenate(
                        [total_sums[:, (3 * p + kind) * 128 : (3 * p + kind) * 128 + 128] for p in range(pairs)], axis=1
                    )
                else:
                    own = slice(group * half, group * half + half)
                    value = jnp.concatenate([both[0:1, own], both[1:2, own]], axis=1)
                ref[group, side, 3 * quarter : 3 * quarter + 16, :] = jnp.broadcast_to(value, (16, width)).astype(BF16)

            split_quads(idx_ref[1], emit, keep_ref, send_ref)


def input_grad_kernel(x_ref, dqkv_ref, dx_ref, w_ref, vec_ref, din_ref, view, outs, xs, wt):
    step = pl.program_id(0)
    width = w_ref.shape[0]
    seq = x_ref.shape[0] * 128 // (width * 2 * pl.num_programs(0))
    rows = xs.shape[0]

    @pl.when(step == 0)
    def _():
        view[...] = x_ref[...].astype(F32)
        wt[...] = w_ref[...].T
        xs[...] = jnp.zeros_like(xs)

    for slot in range(2):
        read_image(view, step, slot, seq, xs, slot * ROWS)
    d_normed = mm(dqkv_ref[...].reshape(rows, 3 * width), wt[...])
    hat, rstd = normalize(xs[...])
    d_in = dx_ref[...].reshape(rows, width) + norm_back(d_normed, hat, rstd, vec_ref[0:1, :])
    for slot in range(2):
        write_image(outs, step, slot, seq, d_in[slot * ROWS : slot * ROWS + ROWS])

    @pl.when(step == pl.num_programs(0) - 1)
    def _():
        din_ref[...] = outs[...].astype(BF16)


def fixed(*shape):
    return pl.BlockSpec(shape, lambda i: (0,) * len(shape))


def per_image(*shape):
    return pl.BlockSpec((1, *shape), lambda i: (i,) + (0,) * len(shape))


SMEM_SPEC = pl.BlockSpec(memory_space=pltpu.SMEM)


def run_attention(count, idx, view, w_qkv, near, far, small):
    width = w_qkv.shape[1] // 3
    return pl.pallas_call(
        attention_kernel,
        grid=(count,),
        in_specs=[SMEM_SPEC] + [VMEM_SPEC] * 5,
        out_specs=[
            per_image(ROWS, 3 * width), per_image(HEADS, ROWS, KEYS), per_image(ROWS, width),
            fixed(width, 3 * width), fixed(8, width),
        ],
        out_shape=[
            pltpu.HBM((count, ROWS, 3 * width), BF16),
            pltpu.HBM((count, HEADS, ROWS, KEYS), BF16),
            pltpu.HBM((count, ROWS, width), BF16),
            jax.ShapeDtypeStruct((width, 3 * width), BF16),
            jax.ShapeDtypeStruct((8, width), F32),
        ],
        scratch_shapes=[
            pltpu.VMEM(view.shape, F32),
            pltpu.VMEM((ROWS, width), F32),
            pltpu.VMEM((KEYS, 2 * width), BF16),
            pltpu.VMEM((8, 3 * width), F32),
            pltpu.VMEM((2, ROWS, KEYS), F32),
        ],
        compiler_params=pltpu.CompilerParams(vmem_limit_bytes=59 << 20),
        cost_estimate=pl.CostEstimate(flops=5 << 30, bytes_accessed=20 << 20, transcendentals=0),
        name="attention_fwd",
    )(idx, view, w_qkv, near, far, small)


def run_mlp(idx, counts, view, cot, att, wo, w1, w2, near, far, small, first):
    width = wo.shape[1]
    hidden = w1.shape[1]
    micro = counts.shape[0]
    rows = 2 * ROWS
    packed = width // 8 * (hidden // width) + hidden // 8 + width // 8 + 16
    two = pl.BlockSpec((2, ROWS, width), lambda i: (i, 0, 0))
    return pl.pallas_call(
        mlp_kernel,
        grid=(micro,),
        in_specs=[SMEM_SPEC, SMEM_SPEC, VMEM_SPEC, VMEM_SPEC, two] + [VMEM_SPEC] * 7,
        out_specs=[VMEM_SPEC, two, two, VMEM_SPEC, VMEM_SPEC],
        out_shape=[
            jax.ShapeDtypeStruct(view.shape, BF16),
            pltpu.HBM(att.shape, F32),
            pltpu.HBM(att.shape, BF16),
            jax.ShapeDtypeStruct((2, 2, packed, width), BF16),
            jax.ShapeDtypeStruct((2, 2, packed, width), BF16),
        ],
        scratch_shapes=[
            pltpu.VMEM(view.shape, F32),
            pltpu.VMEM(view.shape, F32),
            pltpu.VMEM((rows, width), F32),
            pltpu.VMEM((rows, width), F32),
            pltpu.VMEM((rows, hidden), BF16),
            pltpu.VMEM((rows, hidden), BF16),
            pltpu.VMEM((2, rows, 256), F32),
            pltpu.VMEM((2, rows, 256), F32),
            pltpu.VMEM((width, width), BF16),
            pltpu.VMEM((width, hidden), BF16),
            pltpu.VMEM((hidden, width), BF16),
            pltpu.VMEM((width, width), BF16),
            pltpu.VMEM((hidden, width), BF16),
            pltpu.VMEM((width, hidden), BF16),
            pltpu.VMEM((8, width), F32),
            pltpu.VMEM((8, hidden), F32),
            pltpu.VMEM((rows, width), F32),
            pltpu.VMEM((rows, width), F32),
            pltpu.VMEM((width + 16, hidden), F32),
            pltpu.VMEM((width, hidden), F32),
            pltpu.VMEM((width, width), F32),
            pltpu.VMEM((4, 8, width), F32),
        ],
        compiler_params=pltpu.CompilerParams(vmem_limit_bytes=51 << 20),
        cost_estimate=pl.CostEstimate(flops=12 << 30, bytes_accessed=20 << 20, transcendentals=0),
        name="mlp_fwd_bwd",
    )(idx, counts, view, cot, att, wo, w1, w2, near, far, small, first)


def run_attention_back(begin, end, idx, view, qkv, prob, att, datt, w_qkv, vec, carried):
    count = qkv.shape[0]
    width = w_qkv.shape[0]
    packed = width // 8 * 3 + 16
    last = end == count
    block = lambda *shape: pl.BlockSpec((1, *shape), lambda i: (i + begin,) + (0,) * len(shape))
    any_spec = pl.BlockSpec(memory_space=pl.ANY)
    return pl.pallas_call(
        partial(attention_back_kernel, begin, last),
        grid=(end - begin,),
        in_specs=[
            SMEM_SPEC, VMEM_SPEC, block(ROWS, 3 * width), block(HEADS, ROWS, KEYS),
            block(ROWS, width), block(ROWS, width), VMEM_SPEC, VMEM_SPEC,
        ]
        + ([any_spec, VMEM_SPEC, VMEM_SPEC] if carried else []),
        out_specs=[block(ROWS, 3 * width), VMEM_SPEC, VMEM_SPEC] + ([VMEM_SPEC] * 2 if last else []),
        out_shape=[
            pltpu.HBM((count, ROWS, 3 * width), BF16),
            jax.ShapeDtypeStruct((width, 3 * width), F32),
            jax.ShapeDtypeStruct((8, 3 * width), F32),
        ]
        + [jax.ShapeDtypeStruct((2, 2, packed, width), BF16)] * (2 if last else 0),
        scratch_shapes=[
            pltpu.VMEM(view.shape, F32),
            pltpu.VMEM((ROWS, width), F32),
            pltpu.VMEM((KEYS, 2 * width), BF16),
            pltpu.VMEM((width, ROWS), BF16),
            pltpu.VMEM((2, ROWS, KEYS), F32),
            pltpu.VMEM((4, ROWS, KEYS), BF16),
        ],
        input_output_aliases={8: 0} if carried else {},
        compiler_params=pltpu.CompilerParams(vmem_limit_bytes=54 << 20),
        cost_estimate=pl.CostEstimate(flops=(end - begin) << 30, bytes_accessed=20 << 20, transcendentals=0),
    )(idx, view, qkv, prob, att, datt, w_qkv, vec, *carried)


def run_input_grad(view, dqkv, dx, w_qkv, vec):
    count = dqkv.shape[0]
    width = w_qkv.shape[0]
    two = lambda *shape: pl.BlockSpec((2, *shape), lambda i: (i,) + (0,) * len(shape))
    return pl.pallas_call(
        input_grad_kernel,
        grid=(count // 2,),
        in_specs=[VMEM_SPEC, two(ROWS, 3 * width), two(ROWS, width), VMEM_SPEC, VMEM_SPEC],
        out_specs=VMEM_SPEC,
        out_shape=jax.ShapeDtypeStruct(view.shape, BF16),
        scratch_shapes=[
            pltpu.VMEM(view.shape, F32),
            pltpu.VMEM(view.shape, F32),
            pltpu.VMEM((2 * ROWS, width), F32),
            pltpu.VMEM((3 * width, width), BF16),
        ],
        compiler_params=pltpu.CompilerParams(vmem_limit_bytes=57 << 20),
        cost_estimate=pl.CostEstimate(flops=2 << 30, bytes_accessed=20 << 20, transcendentals=0),
        name="input_grad",
    )(view, dqkv, dx, w_qkv, vec)


def merge_kernel(which, idx_ref, a_ref, b_ref, own_ref, other_ref):
    mine = idx_ref[which]
    own_ref[...] = a_ref[mine] + b_ref[mine]
    other_ref[...] = a_ref[1 - mine] + b_ref[1 - mine]


def merge(idx, which, a, b):
    half = jax.ShapeDtypeStruct(a.shape[1:], BF16)
    vmem = pl.BlockSpec(memory_space=pltpu.VMEM)
    return pl.pallas_call(
        partial(merge_kernel, which),
        in_specs=[SMEM_SPEC, vmem, vmem],
        out_specs=[vmem, vmem],
        out_shape=[half, half],
        name="merge",
    )(idx, a, b)


def flip(value, axis, size, bit):
    return lax.ppermute(value, axis, [(i, i ^ bit) for i in range(size)])


def reduce_grads(idx, keep, send, replicas):
    own, other = merge(idx, 0, keep, flip(send, "replica", replicas, 1))
    own, other = merge(idx, 2, own, flip(other, "group", 2, 1))
    own = own + flip(other, "replica", replicas, 2)
    bit = 4
    while bit < replicas:
        own = own + flip(own, "replica", replicas, bit)
        bit *= 2
    side = flip(own, "replica", replicas, 2)
    far_own = flip(own, "replica", replicas, 1)
    return own, side, far_own, flip(side, "replica", replicas, 1)


def unpack_kernel(idx_ref, *refs):
    ins, outs, (mlp, att) = refs[:8], refs[8:20], refs[20:]
    core, side = idx_ref[1], idx_ref[2]
    places = (2 * core + side, 2 * core + 1 - side, 2 * (1 - core) + side, 2 * (1 - core) + 1 - side)
    for k, place in enumerate(places):
        mlp[place] = ins[k][...].astype(F32)
        att[place] = ins[4 + k][...].astype(F32)
    g_qkv, g_bqv, g_out, g_bout, g_fc1, g_bfc1, g_fc2, g_bfc2, g_gone, g_sone, g_gtwo, g_stwo = outs
    half, width = g_out.shape
    hidden = g_fc1.shape[1]
    quarter = half // 4
    wide = hidden // 8
    for quad in range(4):
        rows = slice(quad * quarter, (quad + 1) * quarter)
        top = 0
        for col in range(hidden // width):
            g_fc1[rows, col * width : (col + 1) * width] = mlp[quad, top : top + quarter]
            top += quarter
        g_fc2[quad * wide : (quad + 1) * wide] = mlp[quad, top : top + wide]
        top += wide
        g_out[rows] = mlp[quad, top : top + quarter]
        top += quarter
        value = mlp[quad, top : top + 1]
        if quad < 2:
            g_bfc1[:, quad * width : (quad + 1) * width] = value
        elif quad == 2:
            g_bfc2[...] = value[:, :half]
            g_bout[...] = value[:, half:]
        else:
            g_gtwo[...] = value[:, :half]
            g_stwo[...] = value[:, half:]
        for col in range(3):
            g_qkv[rows, col * width : (col + 1) * width] = att[quad, col * quarter : (col + 1) * quarter]
        value = att[quad, 3 * quarter : 3 * quarter + 1]
        if quad == 0:
            g_bqv[...] = value
        elif quad == 1:
            g_gone[...] = value[:, :half]
            g_sone[...] = value[:, half:]


def run_unpack(idx, mlp, att, shapes):
    vmem = pl.BlockSpec(memory_space=pltpu.VMEM)
    return pl.pallas_call(
        unpack_kernel,
        in_specs=[SMEM_SPEC] + [vmem] * 8,
        out_specs=[vmem] * 12,
        out_shape=[jax.ShapeDtypeStruct(s if len(s) == 2 else (1, *s), F32) for s in shapes],
        scratch_shapes=[pltpu.VMEM((4, *mlp[0].shape), F32), pltpu.VMEM((4, *att[0].shape), F32)],
        compiler_params=pltpu.CompilerParams(vmem_limit_bytes=40 << 20),
        name="unpack",
    )(idx, *mlp, *att)


def interleaved(images):
    micro, slots, seq, width = images.shape
    blocks = images.reshape(micro, slots, seq, width // 128, 128)
    blocks = with_layout_constraint(blocks, Layout(major_to_minor=(0, 2, 3, 1, 4)))
    return blocks.transpose(0, 2, 3, 1, 4).reshape(-1, 128)


def separated(rows, shape):
    micro, slots, seq, width = shape
    blocks = rows.reshape(micro, seq, width // 128, slots, 128).transpose(0, 1, 3, 2, 4)
    return blocks.reshape(micro, seq, slots, width).transpose(0, 2, 1, 3)


SPLITS = ((0, 2), (2, 6), (6, 8))


def local(
    replicas,
    images, image_count, cotangent, w_qkv, b_qv, w_out, b_out, w_fc1, b_fc1, w_fc2, b_fc2,
    gain_one, shift_one, gain_two, shift_two,
):
    replica = lax.axis_index("replica")
    idx = jnp.stack([lax.axis_index("group"), replica & 1, (replica >> 1) & 1]).astype(jnp.int32)
    count = images.shape[0] * images.shape[1]
    vectors = (b_qv, b_out, b_fc1, b_fc2, gain_one, shift_one, gain_two, shift_two)
    first, small = run_pack_first(idx, w_qkv, vectors)
    second = run_pack_second(idx, w_out, w_fc1, w_fc2)
    near_first = flip(first, "group", 2, 1)
    near_second = flip(second, "group", 2, 1)
    far_first = flip(near_first, "replica", replicas, 1)
    far_second = flip(near_second, "replica", replicas, 1)
    view = interleaved(images)
    qkv, prob, att, w_all, vec = run_attention(count, idx, view, w_qkv, near_first, far_first, small)
    out, dx, datt, keep_b, send_b = run_mlp(
        idx, image_count, view, interleaved(cotangent), att, w_out, w_fc1, w_fc2,
        near_second, far_second, small, near_first,
    )
    carried = ()
    for begin, end in SPLITS:
        carried = run_attention_back(begin, end, idx, view, qkv, prob, att, datt, w_all, vec, carried)
    dqkv, _, _, keep_c, send_c = carried
    din = run_input_grad(view, dqkv, dx, w_all, vec)
    mlp = reduce_grads(idx, keep_b, send_b, replicas)
    attention = reduce_grads(idx, keep_c, send_c, replicas)
    shapes = [v.shape for v in (w_qkv, b_qv, w_out, b_out, w_fc1, b_fc1, w_fc2, b_fc2)] + [gain_one.shape] * 4
    grads = run_unpack(idx, mlp, attention, shapes)
    grads = [g.reshape(s) for g, s in zip(grads, shapes)]
    return (separated(out, images.shape), separated(din, images.shape), *grads)


def step(replicas, *args):
    return local(replicas, *args)


def solution(mesh):
    split = P(None, ("group", "replica"), None, None)
    matrix, vector = P("group", None), P("group")
    return jax.shard_map(
        partial(step, mesh.shape["replica"]),
        mesh=mesh,
        in_specs=(split, P(None, ("group", "replica")), split)
        + (matrix, vector) * 4
        + (vector,) * 4,
        out_specs=(split, split) + (matrix, vector) * 4 + (vector,) * 4,
        check_vma=False,
    )
```

```python
from functools import partial

import jax
import jax.numpy as jnp
from jax import lax
from jax.experimental import pallas as pl
from jax.experimental.layout import Layout, with_layout_constraint
from jax.experimental.pallas import tpu as pltpu
from jax.sharding import PartitionSpec as P


HEADS = 6
ROWS = 208
KEYS = 256
F32 = jnp.float32
BF16 = jnp.bfloat16
NT = (((1,), (1,)), ((), ()))
TN = (((0,), (0,)), ((), ()))


def mm(a, b):
    return jnp.dot(a, b, preferred_element_type=F32)


def mm_nt(a, b):
    return lax.dot_general(a, b, NT, preferred_element_type=F32)


def mm_tn(a, b):
    return lax.dot_general(a, b, TN, preferred_element_type=F32)


def normalize(values):
    center = values - jnp.mean(values, axis=-1, keepdims=True)
    spread = jnp.mean(center * center, axis=-1, keepdims=True)
    rstd = lax.rsqrt(spread + 1e-06)
    return center * rstd, rstd


def norm_back(grad_normed, hat, rstd, gain):
    grad_hat = grad_normed * gain
    first = jnp.mean(grad_hat, axis=-1, keepdims=True)
    second = jnp.mean(grad_hat * hat, axis=-1, keepdims=True)
    return rstd * (grad_hat - first - hat * second)


def gelu_parts(pre, d_act):
    size = jnp.abs(pre)
    density = jnp.exp2(pre * (pre * -0.7213475204444817))
    t = 1.0 / (1.0 + 0.2316418882663604 * size)
    poly = t * (
        0.127414796
        + t * (-0.142248368 + t * (0.7107068705 + t * (-0.7265760135 + t * 0.5307027145)))
    )
    act = jnp.maximum(pre, 0.0) - size * (poly * density)
    edge = density * (poly - 0.3989422804014327 * size)
    slope = jnp.where(pre < 0.0, edge, 1.0 - edge)
    return act.astype(BF16), (d_act * slope).astype(BF16)


def read_image(ref, micro, slot, seq, target, top):
    tiles = target.shape[1] // 128
    for tile in range(tiles):
        start = micro * (seq * tiles * 2) + 2 * tile + slot
        target[top : top + seq, tile * 128 : tile * 128 + 128] = ref[pl.ds(start, seq, stride=2 * tiles), :]


def write_image(ref, micro, slot, seq, value):
    tiles = value.shape[1] // 128
    for tile in range(tiles):
        start = micro * (seq * tiles * 2) + 2 * tile + slot
        ref[pl.ds(start, seq, stride=2 * tiles), :] = value[:seq, tile * 128 : tile * 128 + 128]


def joined(first, second, row, size):
    return jnp.concatenate([first[row : row + 1, :size], second[row : row + 1, :size]], axis=1)


def ordered(idx_ref, mine, theirs):
    low = idx_ref[0] == 0
    mine, theirs = mine.astype(F32), theirs.astype(F32)
    return jnp.where(low, mine, theirs), jnp.where(low, theirs, mine)


def fetch(pairs, sem, first, step, steps):
    def copies(k, slot):
        return [
            pltpu.make_async_copy(source.at[pl.ds(2 * (first + k), 2)], target.at[slot], sem.at[n, slot])
            for n, (source, target) in enumerate(pairs)
        ]

    now = lax.rem(step, 2)

    @pl.when(step == 0)
    def _():
        for copy in copies(0, 0):
            copy.start()

    @pl.when(step + 1 < steps)
    def _():
        for copy in copies(step + 1, 1 - now):
            copy.start()

    for copy in copies(step, now):
        copy.wait()
    return [target.at[now] for _, target in pairs]


HBM_SPEC = pl.BlockSpec(memory_space=pltpu.HBM)


def in_hbm(*arrays):
    return [pltpu.with_memory_space_constraint(array, pltpu.HBM) for array in arrays]


def at(start, size):
    return pl.ds(pl.multiple_of(start, 16), size)


VMEM_SPEC = pl.BlockSpec(memory_space=pltpu.VMEM)


def pack_first_kernel(idx_ref, wq_ref, *refs):
    vectors, first_ref, small_ref = refs[:-2], refs[-2], refs[-1]
    part = wq_ref.shape[0]
    small_ref[...] = jnp.zeros_like(small_ref)
    for k, ref in enumerate(vectors):
        size = ref.shape[0]
        small_ref[k : k + 1, :size] = ref[...].reshape(1, size)
    first_ref[:part, :] = wq_ref[...]
    first_ref[part:, :] = jnp.zeros((16, first_ref.shape[1]), BF16)
    first_ref[part : part + 8, : small_ref.shape[1]] = small_ref[...]


def pack_second_kernel(idx_ref, wo_ref, w1_ref, w2_ref, second_ref):
    part, width = wo_ref.shape
    hidden = w1_ref.shape[1]
    second_ref[:, :width] = wo_ref[...]
    second_ref[:, width : width + hidden] = w1_ref[...]
    for k in range(hidden // width):
        second_ref[:, width + hidden + k * width : width + hidden + (k + 1) * width] = w2_ref[
            k * part : (k + 1) * part, :
        ]


def own_rows(rows, columns):
    return pl.BlockSpec((rows, columns), lambda i, idx: (idx[1], 0))


def run_pack_first(idx, w_qkv, vectors):
    half, wide = w_qkv.shape
    longest = max(v.shape[0] for v in vectors)
    shapes = [(half // 2 + 16, wide), (8, longest)]
    return pl.pallas_call(
        pack_first_kernel,
        grid_spec=pltpu.PrefetchScalarGridSpec(
            num_scalar_prefetch=1,
            grid=(1,),
            in_specs=[own_rows(half // 2, wide)] + [pl.BlockSpec(v.shape, lambda i, idx: (0,)) for v in vectors],
            out_specs=[pl.BlockSpec(s, lambda i, idx: (0, 0)) for s in shapes],
        ),
        out_shape=[jax.ShapeDtypeStruct(s, BF16) for s in shapes],
        name="pack_first",
    )(idx, w_qkv, *vectors)


def run_pack_second(idx, w_out, w_fc1, w_fc2):
    half, width = w_out.shape
    hidden = w_fc1.shape[1]
    part = half // 2
    shape = (part, width + 2 * hidden)
    return pl.pallas_call(
        pack_second_kernel,
        grid_spec=pltpu.PrefetchScalarGridSpec(
            num_scalar_prefetch=1,
            grid=(1,),
            in_specs=[own_rows(part, width), own_rows(part, hidden), own_rows(hidden // 4, width)],
            out_specs=pl.BlockSpec(shape, lambda i, idx: (0, 0)),
        ),
        out_shape=jax.ShapeDtypeStruct(shape, BF16),
        name="pack_second",
    )(idx, w_out, w_fc1, w_fc2)


def attention_kernel(
    idx_ref, x_ref, w_ref, near_ref, far_ref, small_ref,
    qkv_ref, prob_ref, att_ref, hat_ref, rstd_ref, whole_ref, vec_ref, b1_ref,
    raw, view, xs, kv, bias, scores, raw_sem,
):
    step = pl.program_id(0)
    half, wide = w_ref.shape
    width = wide // 3
    part = half // 2
    pairs = width // 128
    seq = x_ref.shape[0] * 128 // (width * 2 * pl.num_programs(0))

    @pl.when(step == 0)
    def _():
        load = pltpu.make_async_copy(x_ref, raw, raw_sem)
        load.start()
        xs[...] = jnp.zeros_like(xs)
        kv[...] = jnp.zeros_like(kv)
        group, core = idx_ref[0], idx_ref[1]
        first, second = ordered(idx_ref, small_ref[...], near_ref[part : part + 8, : small_ref.shape[1]])
        for k, row in enumerate((4, 5, 1, 3, 6, 7)):
            vec_ref[k : k + 1, :] = joined(first, second, row, half)
        b1_ref[0:1, :] = jnp.concatenate([first[2:3, :], second[2:3, :]], axis=1)
        other = (1 - group) * half
        for pair in range(pairs):
            for kind in range(3):
                source = slice(kind * width + pair * 128, kind * width + pair * 128 + 128)
                target = slice((3 * pair + kind) * 128, (3 * pair + kind) * 128 + 128)
                whole_ref[at(group * half, half), target] = w_ref[:, source]
                whole_ref[at(other + core * part, part), target] = near_ref[:part, source]
                whole_ref[at(other + (1 - core) * part, part), target] = far_ref[:part, source]
                lanes = slice(pair * 128, pair * 128 + 128)
                piece = (first[0:1, lanes], jnp.zeros((1, 128), F32), second[0:1, lanes])[kind]
                bias[0:1, target] = piece
        load.wait()
        view[...] = raw[...].astype(F32)

    for slot in range(2):
        read_image(view, step, slot, seq, xs, slot * ROWS)
    hat, rstd = normalize(xs[...])
    hat_ref[...] = hat.astype(BF16).reshape(2, ROWS, width)
    rstd_ref[...] = jnp.broadcast_to(rstd, (2 * ROWS, 128)).reshape(2, ROWS, 128)
    normed = (hat * vec_ref[0:1, :] + vec_ref[1:2, :]).astype(BF16)
    low_half = lax.broadcasted_iota(jnp.int32, (1, 128), 1) < 64
    column = lax.broadcasted_iota(jnp.int32, (1, KEYS), 1)

    def project(pair):
        lanes = slice(pair * 384, pair * 384 + 384)
        qkv = (mm(normed, whole_ref[:, lanes]) + bias[0:1, lanes]).astype(BF16)
        for slot in range(2):
            part = qkv[slot * ROWS : slot * ROWS + ROWS]
            qkv_ref[slot, :, lanes] = part
            kv[slot, :ROWS, pair * 256 : pair * 256 + 256] = part[:, 128:]

    def masked(values, head):
        mask = low_half if head % 2 == 0 else jnp.logical_not(low_half)
        return jnp.where(mask, values, jnp.zeros_like(values))

    def first_part(slot, head):
        pair = head // 2
        query = qkv_ref[slot, :, pair * 384 : pair * 384 + 128] * jnp.array(0.125, BF16)
        scores[slot, head % 2] = mm_nt(query, masked(kv[slot, :, pair * 256 : pair * 256 + 128], head))

    def second_part(slot, head):
        for r in range(0, ROWS, 16):
            value = jnp.where(column < seq, scores[slot, head % 2, r : r + 16], -1e30)
            top = jnp.max(value, axis=-1, keepdims=True)
            grown = jnp.exp(value - top)
            prob_ref[slot, head, r : r + 16] = (
                grown * (1.0 / jnp.sum(grown, axis=-1, keepdims=True))
            ).astype(BF16)

    def third_part(slot, head):
        pair = head // 2
        values = kv[slot, :, pair * 256 + 128 : pair * 256 + 256]
        if head % 2 == 1:
            total = mm(prob_ref[slot, head - 1], masked(values, 0)) + mm(prob_ref[slot, head], masked(values, 1))
            att_ref[slot, :, pair * 128 : pair * 128 + 128] = total.astype(BF16)

    project(0)
    for k in range(HEADS + 2):
        for slot in range(2):
            if k < HEADS:
                first_part(slot, k)
            if k >= 2:
                third_part(slot, k - 2)
            if slot == 0 and k % 2 == 0 and k // 2 + 1 < pairs:
                project(k // 2 + 1)
            if 1 <= k <= HEADS:
                second_part(slot, k - 1)


def mlp_kernel(
    idx_ref, count_ref, x_ref, cot_ref, att_hbm, wo_ref, w1_ref, w2_ref, near_ref, far_ref, vec, b1,
    act_ref, middle_ref, dx_ref, datt_ref, w2, keep_ref, send_ref,
    view_x, view_c, xs, dys, acts, dpres, pres, dacts, wo, w1, wot, w1t, w2t, dn_half,
    gw1, gw2, gwo, gsmall, att_buf, raw, att_sem, raw_sem,
):
    step = pl.program_id(0)
    last = pl.num_programs(0) - 1
    half, width = wo_ref.shape
    hidden = w1_ref.shape[1]
    part = half // 2
    rows = xs.shape[0]
    seq = x_ref.shape[0] * 128 // (width * 2 * pl.num_programs(0))
    core = idx_ref[1]

    @pl.when(step == 0)
    def _():
        loads = [pltpu.make_async_copy(ref, raw.at[k], raw_sem.at[k]) for k, ref in enumerate((x_ref, cot_ref))]
        for load in loads:
            load.start()
        for ref in (xs, dys, gw1, gw2, gwo, gsmall):
            ref[...] = jnp.zeros_like(ref)
        group = idx_ref[0]
        wo[at(group * half, half), :] = wo_ref[...]
        w1[at(group * half, half), :] = w1_ref[...]
        w2[at(group * (hidden // 2), hidden // 2), :] = w2_ref[...]
        other = (1 - group) * half
        for ref, which in ((near_ref, core), (far_ref, 1 - core)):
            wo[at(other + which * part, part), :] = ref[:, :width]
            w1[at(other + which * part, part), :] = ref[:, width : width + hidden]
            base = (1 - group) * (hidden // 2) + which * (hidden // 4)
            for k in range(hidden // width):
                w2[at(base + k * part, part), :] = ref[:, width + hidden + k * width : width + hidden + (k + 1) * width]
        wot[...] = wo[...].T
        w1t[...] = w1[...].T
        w2t[...] = w2[...].T
        for load, target, k in zip(loads, (view_x, view_c), range(2)):
            load.wait()
            target[...] = raw[k].astype(F32)

    (att_ref,) = fetch([(att_hbm, att_buf)], att_sem, 0, step, last + 1)
    second_valid = (1 < count_ref[step, 0]).astype(F32)
    for slot in range(2):
        read_image(view_x, step, slot, seq, xs, slot * ROWS)
        read_image(view_c, step, slot, seq, dys, slot * ROWS)
    row = lax.broadcasted_iota(jnp.int32, (rows, 1), 0)
    valid = jnp.where(row < ROWS, 1.0, second_valid)
    att = att_ref[...].reshape(rows, width)
    middle = xs[...] + mm(att, wo[...]) + vec[2:3, :]
    hat, rstd = normalize(middle)
    gain = vec[4:5, :]
    normed = (hat * gain + vec[5:6, :]).astype(BF16)
    d_out = dys[...] * valid
    d_mlp = d_out.astype(BF16)
    normed_t = jnp.concatenate([normed.T, jnp.ones((16, rows), BF16)], axis=0)
    d_mlp_t = d_mlp.T
    chunks = hidden // 256
    middle_of = hidden // 2

    def first_part(c):
        cols = slice(c * 256, c * 256 + 256)
        pres[c % 2] = mm(normed, w1[:, cols])
        dacts[c % 2] = mm(d_mlp, w2t[:, cols])

    def second_part(c):
        cols = slice(c * 256, c * 256 + 256)
        bias = b1[0:1, cols]
        for r in range(0, rows, 32):
            act, d_pre = gelu_parts(pres[c % 2, r : r + 32] + bias, dacts[c % 2, r : r + 32])
            acts[r : r + 32, cols] = act
            act_ref[r // ROWS, r % ROWS : r % ROWS + 16, cols] = act[:16]
            act_ref[(r + 16) // ROWS, (r + 16) % ROWS : (r + 16) % ROWS + 16, cols] = act[16:]
            dpres[r : r + 32, cols] = d_pre

    def third_part(c):
        cols = slice(c * 256, c * 256 + 256)
        gw1[:, cols] += mm(normed_t, dpres[:, cols])
        gw2[:, cols] += mm(d_mlp_t, acts[:, cols])

    for k in range(chunks + 2):
        if k < chunks:
            first_part(k)
        if k >= 2:
            third_part(k - 2)
        if k == chunks // 2 + 1:
            dn_half[...] = mm(dpres[:, :middle_of], w1t[:middle_of, :])
        if 1 <= k <= chunks:
            second_part(k - 1)

    middle_ref[...] = middle.reshape(2, ROWS, width)
    d_normed = dn_half[...] + mm(dpres[:, middle_of:], w1t[middle_of:, :])
    dx = d_out + norm_back(d_normed, hat, rstd, gain)
    d_attn = dx.astype(BF16)
    dx_ref[...] = d_attn.reshape(2, ROWS, width)
    datt_ref[...] = mm(d_attn, wot[...]).astype(BF16).reshape(2, ROWS, width)
    gwo[...] += mm_tn(att, d_attn)

    def fold(values):
        return jnp.sum(values.reshape(rows // 8, 8, width), axis=0)

    gsmall[0] += fold(d_out)
    gsmall[1] += fold(d_attn.astype(F32))
    gsmall[2] += fold(d_normed * hat)
    gsmall[3] += fold(d_normed)

    @pl.when(step == last)
    def _():
        quarter = half // 4
        wide = hidden // 8
        gw2_t = gw2[...].T
        small_rows = [jnp.sum(gsmall[k], axis=0, keepdims=True) for k in range(4)]

        def emit(group, quad, ref, side):
            base = group * half + quad * quarter
            top = 0
            for col in range(hidden // width):
                ref[group, side, top : top + quarter, :] = gw1[
                    base : base + quarter, col * width : (col + 1) * width
                ].astype(BF16)
                top += quarter
            start = group * (hidden // 2) + quad * wide
            ref[group, side, top : top + wide, :] = gw2_t[start : start + wide].astype(BF16)
            top += wide
            ref[group, side, top : top + quarter, :] = gwo[base : base + quarter, :].astype(BF16)
            top += quarter
            if quad < 2:
                start = group * (hidden // 2) + quad * width
                value = gw1[width : width + 1, start : start + width]
            else:
                own = slice(group * half, group * half + half)
                value = jnp.concatenate(
                    [small_rows[2 * quad - 4][:, own], small_rows[2 * quad - 3][:, own]], axis=1
                )
            ref[group, side, top : top + 16, :] = jnp.broadcast_to(value, (16, width)).astype(BF16)

        split_quads(core, emit, keep_ref, send_ref)


def split_quads(core, emit, keep_ref, send_ref):
    for mine in range(2):

        @pl.when(core == mine)
        def _():
            for group in range(2):
                for side in range(2):
                    emit(group, 2 * mine + side, keep_ref, side)
                    emit(group, 2 * (1 - mine) + side, send_ref, side)


def attention_back_kernel(
    first_micro, last, idx_ref, hat_hbm, qkv_hbm, prob_hbm, att_hbm, datt_hbm, w_ref, vec_ref, *refs
):
    carried = 0 if first_micro == 0 else 3
    dqkv_ref, total_ref, sums_ref = refs[carried : carried + 3]
    kv, hat_t, d_probs, d_scores = refs[-10:-6]
    buffers, sem = refs[-6:-1], refs[-1]
    step = pl.program_id(0)
    width = w_ref.shape[0]
    pairs = width // 128
    sources = (hat_hbm, datt_hbm, qkv_hbm, att_hbm, prob_hbm)
    hat_ref, datt_ref, qkv_ref, att_ref, prob_ref = fetch(
        list(zip(sources, buffers)), sem, first_micro, step, pl.num_programs(0)
    )

    @pl.when(step == 0)
    def _():
        kv[...] = jnp.zeros_like(kv)
        if not carried:
            total_ref[...] = jnp.zeros_like(total_ref)
            sums_ref[...] = jnp.zeros_like(sums_ref)

    hat_t[...] = hat_ref[...].reshape(2 * ROWS, width).T
    for pair in range(pairs):
        kv[:, :ROWS, pair * 256 : pair * 256 + 256] = qkv_ref[:, :, pair * 384 + 128 : pair * 384 + 384]
    low_half = lax.broadcasted_iota(jnp.int32, (1, 128), 1) < 64

    def masked(values, head):
        mask = low_half if head % 2 == 0 else jnp.logical_not(low_half)
        return jnp.where(mask, values, jnp.zeros_like(values))

    def lanes(head):
        return slice(head // 2 * 128, head // 2 * 128 + 128)

    def first_part(slot, head):
        pair = head // 2
        d_probs[slot, head % 2] = mm_nt(
            datt_ref[slot, :, lanes(head)], masked(kv[slot, :, pair * 256 + 128 : pair * 256 + 256], head)
        )

    def second_part(slot, head):
        for r in range(0, ROWS, 16):
            rows = slice(r, r + 16)
            product = datt_ref[slot, rows, lanes(head)].astype(F32) * att_ref[slot, rows, lanes(head)].astype(F32)
            delta = jnp.sum(masked(product, head), axis=-1, keepdims=True)
            d_scores[slot, head % 4, rows] = (
                prob_ref[slot, head, rows].astype(F32) * (d_probs[slot, head % 2, rows] - delta)
            ).astype(BF16)

    def third_part(slot, pair):
        query = qkv_ref[slot, :, pair * 384 : pair * 384 + 128] * jnp.array(0.125, BF16)
        keys = kv[slot, :, pair * 256 : pair * 256 + 128] * jnp.array(0.125, BF16)
        d_att = datt_ref[slot, :, pair * 128 : pair * 128 + 128]
        dq = dk = dv = 0.0
        for head in (2 * pair, 2 * pair + 1):
            d_score = d_scores[slot, head % 4]
            dv = dv + mm_tn(prob_ref[slot, head], masked(d_att, head))
            dk = dk + mm_tn(d_score, masked(query, head))
            dq = dq + mm(d_score, masked(keys, head))
        top = pair * 384
        dqkv_ref[slot, :, top : top + 128] = dq.astype(BF16)
        dqkv_ref[slot, :, top + 128 : top + 256] = dk[:ROWS].astype(BF16)
        dqkv_ref[slot, :, top + 256 : top + 384] = dv[:ROWS].astype(BF16)

    def fourth_part(pair):
        columns = slice(pair * 384, pair * 384 + 384)
        joined_back = dqkv_ref[:, :, columns].reshape(2 * ROWS, 384)
        total_ref[:, columns] += mm(hat_t[...], joined_back)
        sums_ref[:, columns] += jnp.sum(joined_back.astype(F32).reshape(ROWS // 4, 8, 384), axis=0)

    for k in range(HEADS + 3):
        for slot in range(2):
            if k < HEADS:
                first_part(slot, k)
            if k >= 3 and k % 2 == 1:
                third_part(slot, k // 2 - 1)
            if slot == 0 and k >= 4 and k % 2 == 0:
                fourth_part(k // 2 - 2)
            if 1 <= k <= HEADS:
                second_part(slot, k - 1)

    if last:
        keep_ref, send_ref = refs[carried + 3 : carried + 5]

        @pl.when(step == pl.num_programs(0) - 1)
        def _():
            half = width // 2
            quarter = half // 4
            total_sums = jnp.sum(sums_ref[...], axis=0, keepdims=True)
            weights = w_ref[...].astype(F32)
            d_gain = jnp.sum((weights * total_ref[...]).reshape(width, 3 * width), axis=1, keepdims=True)
            d_shift = jnp.sum(weights * total_sums, axis=1, keepdims=True)
            columns = jnp.concatenate([vec_ref[...], jnp.zeros((120, width), F32)], axis=0).T
            gain, shift = columns[:, 0:1], columns[:, 1:2]
            total_ref[...] = total_ref[...] * gain + shift * total_sums
            lane = lax.broadcasted_iota(jnp.int32, (1, 128), 1)
            both = jnp.where(lane == 0, d_gain, jnp.where(lane == 1, d_shift, 0.0)).T

            def emit(group, quad, ref, side):
                base = group * half + quad * quarter
                for kind in range(3):
                    for pair in range(pairs):
                        source = slice((3 * pair + kind) * 128, (3 * pair + kind) * 128 + 128)
                        ref[group, side, kind * quarter : (kind + 1) * quarter, pair * 128 : pair * 128 + 128] = (
                            total_ref[base : base + quarter, source].astype(BF16)
                        )
                if quad == 0:
                    kind = 2 * group
                    value = jnp.concatenate(
                        [total_sums[:, (3 * p + kind) * 128 : (3 * p + kind) * 128 + 128] for p in range(pairs)], axis=1
                    )
                else:
                    own = slice(group * half, group * half + half)
                    value = jnp.concatenate([both[0:1, own], both[1:2, own]], axis=1)
                ref[group, side, 3 * quarter : 3 * quarter + 16, :] = jnp.broadcast_to(value, (16, width)).astype(BF16)

            split_quads(idx_ref[1], emit, keep_ref, send_ref)


def input_grad_kernel(hat_hbm, rstd_hbm, dqkv_hbm, dx_hbm, w_ref, vec_ref, din_ref, outs, wt, *refs):
    step = pl.program_id(0)
    width = w_ref.shape[0]
    micros = pl.num_programs(0)
    seq = din_ref.shape[0] * 128 // (width * 2 * micros)
    rows = 2 * ROWS
    sources = (hat_hbm, rstd_hbm, dqkv_hbm, dx_hbm)
    hat_ref, rstd_ref, dqkv_ref, dx_ref = fetch(list(zip(sources, refs[:-1])), refs[-1], 0, step, micros)

    @pl.when(step == 0)
    def _():
        wt[...] = w_ref[...].T

    d_normed = mm(dqkv_ref[...].reshape(rows, 3 * width), wt[...])
    hat = hat_ref[...].reshape(rows, width).astype(F32)
    rstd = rstd_ref[...].reshape(rows, 128)[:, 0:1]
    d_in = dx_ref[...].reshape(rows, width).astype(F32) + norm_back(d_normed, hat, rstd, vec_ref[0:1, :])
    for slot in range(2):
        write_image(outs, step, slot, seq, d_in[slot * ROWS : slot * ROWS + ROWS])

    @pl.when(step == micros - 1)
    def _():
        din_ref[...] = outs[...].astype(BF16)


def outputs_kernel(count_ref, act_hbm, middle_hbm, w2_ref, vec_ref, out_ref, outs, act_buf, middle_buf, sem):
    step = pl.program_id(0)
    hidden, width = w2_ref.shape
    micros = pl.num_programs(0)
    seq = out_ref.shape[0] * 128 // (width * 2 * micros)
    rows = 2 * ROWS
    act_ref, middle_ref = fetch([(act_hbm, act_buf), (middle_hbm, middle_buf)], sem, 0, step, micros)
    row = lax.broadcasted_iota(jnp.int32, (rows, 1), 0)
    valid = jnp.where(row < ROWS, 1.0, (1 < count_ref[step, 0]).astype(F32))
    mlp = mm(act_ref[...].reshape(rows, hidden), w2_ref[...]) + vec_ref[3:4, :]
    result = (middle_ref[...].reshape(rows, width) + mlp) * valid
    for slot in range(2):
        write_image(outs, step, slot, seq, result[slot * ROWS : slot * ROWS + ROWS])

    @pl.when(step == micros - 1)
    def _():
        out_ref[...] = outs[...].astype(BF16)


def per_pair(*shape):
    return pl.BlockSpec((2, *shape), lambda i: (i,) + (0,) * len(shape))


SMEM_SPEC = pl.BlockSpec(memory_space=pltpu.SMEM)


def run_attention(count, idx, view, w_qkv, near, far, small):
    width = w_qkv.shape[1] // 3
    return pl.pallas_call(
        attention_kernel,
        grid=(count // 2,),
        in_specs=[SMEM_SPEC, HBM_SPEC] + [VMEM_SPEC] * 4,
        out_specs=[
            per_pair(ROWS, 3 * width), per_pair(HEADS, ROWS, KEYS), per_pair(ROWS, width),
            per_pair(ROWS, width), per_pair(ROWS, 128), VMEM_SPEC, VMEM_SPEC, VMEM_SPEC,
        ],
        out_shape=[
            pltpu.HBM((count, ROWS, 3 * width), BF16),
            pltpu.HBM((count, HEADS, ROWS, KEYS), BF16),
            pltpu.HBM((count, ROWS, width), BF16),
            pltpu.HBM((count, ROWS, width), BF16),
            pltpu.HBM((count, ROWS, 128), F32),
            jax.ShapeDtypeStruct((width, 3 * width), BF16),
            jax.ShapeDtypeStruct((8, width), F32),
            jax.ShapeDtypeStruct((8, 2 * small.shape[1]), F32),
        ],
        scratch_shapes=[
            pltpu.VMEM(view.shape, BF16),
            pltpu.VMEM(view.shape, F32),
            pltpu.VMEM((2 * ROWS, width), F32),
            pltpu.VMEM((2, KEYS, 2 * width), BF16),
            pltpu.VMEM((8, 3 * width), F32),
            pltpu.VMEM((2, 2, ROWS, KEYS), F32),
            pltpu.SemaphoreType.DMA,
        ],
        compiler_params=pltpu.CompilerParams(vmem_limit_bytes=22 << 20),
        cost_estimate=pl.CostEstimate(flops=5 << 30, bytes_accessed=20 << 20, transcendentals=0),
        name="attention_fwd",
    )(idx, *in_hbm(view), w_qkv, near, far, small)


def run_mlp(idx, counts, view, cot, att, wo, w1, w2, near, far, vec, b1):
    width = wo.shape[1]
    hidden = w1.shape[1]
    micro = counts.shape[0]
    rows = 2 * ROWS
    packed = width // 8 * (hidden // width) + hidden // 8 + width // 8 + 16
    two = pl.BlockSpec((2, ROWS, width), lambda i: (i, 0, 0))
    return pl.pallas_call(
        mlp_kernel,
        grid=(micro,),
        in_specs=[SMEM_SPEC, SMEM_SPEC, HBM_SPEC, HBM_SPEC, HBM_SPEC] + [VMEM_SPEC] * 7,
        out_specs=[per_pair(ROWS, hidden), two, two, two, VMEM_SPEC, VMEM_SPEC, VMEM_SPEC],
        out_shape=[
            pltpu.HBM((2 * micro, ROWS, hidden), BF16),
            pltpu.HBM(att.shape, F32),
            pltpu.HBM(att.shape, BF16),
            pltpu.HBM(att.shape, BF16),
            jax.ShapeDtypeStruct((hidden, width), BF16),
            jax.ShapeDtypeStruct((2, 2, packed, width), BF16),
            jax.ShapeDtypeStruct((2, 2, packed, width), BF16),
        ],
        scratch_shapes=[
            pltpu.VMEM(view.shape, F32),
            pltpu.VMEM(view.shape, F32),
            pltpu.VMEM((rows, width), F32),
            pltpu.VMEM((rows, width), F32),
            pltpu.VMEM((rows, hidden), BF16),
            pltpu.VMEM((rows, hidden), BF16),
            pltpu.VMEM((2, rows, 256), F32),
            pltpu.VMEM((2, rows, 256), F32),
            pltpu.VMEM((width, width), BF16),
            pltpu.VMEM((width, hidden), BF16),
            pltpu.VMEM((width, width), BF16),
            pltpu.VMEM((hidden, width), BF16),
            pltpu.VMEM((width, hidden), BF16),
            pltpu.VMEM((rows, width), F32),
            pltpu.VMEM((width + 16, hidden), F32),
            pltpu.VMEM((width, hidden), F32),
            pltpu.VMEM((width, width), F32),
            pltpu.VMEM((4, 8, width), F32),
            pltpu.VMEM((2, 2, ROWS, width), BF16),
            pltpu.VMEM((2, *view.shape), BF16),
            pltpu.SemaphoreType.DMA((1, 2)),
            pltpu.SemaphoreType.DMA((2,)),
        ],
        compiler_params=pltpu.CompilerParams(vmem_limit_bytes=40 << 20),
        cost_estimate=pl.CostEstimate(flops=12 << 30, bytes_accessed=20 << 20, transcendentals=0),
        name="mlp_fwd_bwd",
    )(idx, counts, *in_hbm(view, cot, att), wo, w1, w2, near, far, vec, b1)


def run_attention_back(begin, end, idx, hat, qkv, prob, att, datt, w_qkv, vec, carried):
    count = qkv.shape[0]
    width = w_qkv.shape[0]
    packed = width // 8 * 3 + 16
    last = 2 * end == count
    block = pl.BlockSpec((2, ROWS, 3 * width), lambda i: (i + begin, 0, 0))
    two = lambda *shape: pltpu.VMEM((2, 2, *shape), BF16)
    return pl.pallas_call(
        partial(attention_back_kernel, begin, last),
        grid=(end - begin,),
        in_specs=[SMEM_SPEC] + [HBM_SPEC] * 5 + [VMEM_SPEC] * 2
        + ([HBM_SPEC, VMEM_SPEC, VMEM_SPEC] if carried else []),
        out_specs=[block, VMEM_SPEC, VMEM_SPEC] + ([VMEM_SPEC] * 2 if last else []),
        out_shape=[
            pltpu.HBM((count, ROWS, 3 * width), BF16),
            jax.ShapeDtypeStruct((width, 3 * width), F32),
            jax.ShapeDtypeStruct((8, 3 * width), F32),
        ]
        + [jax.ShapeDtypeStruct((2, 2, packed, width), BF16)] * (2 if last else 0),
        scratch_shapes=[
            pltpu.VMEM((2, KEYS, 2 * width), BF16),
            pltpu.VMEM((width, 2 * ROWS), BF16),
            pltpu.VMEM((2, 2, ROWS, KEYS), F32),
            pltpu.VMEM((2, 4, ROWS, KEYS), BF16),
            two(ROWS, width), two(ROWS, width), two(ROWS, 3 * width), two(ROWS, width), two(HEADS, ROWS, KEYS),
            pltpu.SemaphoreType.DMA((5, 2)),
        ],
        input_output_aliases={8: 0, 9: 1, 10: 2} if carried else {},
        compiler_params=pltpu.CompilerParams(vmem_limit_bytes=18 << 20),
        cost_estimate=pl.CostEstimate(flops=(end - begin) << 31, bytes_accessed=20 << 20, transcendentals=0),
    )(idx, *in_hbm(hat, qkv, prob, att, datt), w_qkv, vec, *in_hbm(*carried[:1]), *carried[1:])


def run_input_grad(view_shape, hat, rstd, dqkv, dx, w_qkv, vec):
    count = dqkv.shape[0]
    width = w_qkv.shape[0]
    two = lambda dtype, *shape: pltpu.VMEM((2, 2, *shape), dtype)
    return pl.pallas_call(
        input_grad_kernel,
        grid=(count // 2,),
        in_specs=[HBM_SPEC] * 4 + [VMEM_SPEC] * 2,
        out_specs=VMEM_SPEC,
        out_shape=jax.ShapeDtypeStruct(view_shape, BF16),
        scratch_shapes=[
            pltpu.VMEM(view_shape, F32),
            pltpu.VMEM((3 * width, width), BF16),
            two(BF16, ROWS, width), two(F32, ROWS, 128), two(BF16, ROWS, 3 * width), two(BF16, ROWS, width),
            pltpu.SemaphoreType.DMA((4, 2)),
        ],
        compiler_params=pltpu.CompilerParams(vmem_limit_bytes=14 << 20),
        cost_estimate=pl.CostEstimate(flops=2 << 30, bytes_accessed=20 << 20, transcendentals=0),
        name="input_grad",
    )(*in_hbm(hat, rstd, dqkv, dx), w_qkv, vec)


def run_outputs(view_shape, counts, act, middle, w2, vec):
    count, _, hidden = act.shape
    width = w2.shape[1]
    return pl.pallas_call(
        outputs_kernel,
        grid=(count // 2,),
        in_specs=[SMEM_SPEC] + [HBM_SPEC] * 2 + [VMEM_SPEC] * 2,
        out_specs=VMEM_SPEC,
        out_shape=jax.ShapeDtypeStruct(view_shape, BF16),
        scratch_shapes=[
            pltpu.VMEM(view_shape, F32),
            pltpu.VMEM((2, 2, ROWS, hidden), BF16), pltpu.VMEM((2, 2, ROWS, width), F32),
            pltpu.SemaphoreType.DMA((2, 2)),
        ],
        compiler_params=pltpu.CompilerParams(vmem_limit_bytes=14 << 20),
        cost_estimate=pl.CostEstimate(flops=2 << 30, bytes_accessed=20 << 20, transcendentals=0),
        name="layer_outputs",
    )(counts, *in_hbm(act, middle), w2, vec)


def merge_kernel(which, idx_ref, a_ref, b_ref, own_ref, other_ref):
    mine = idx_ref[which]
    own_ref[...] = a_ref[mine] + b_ref[mine]
    other_ref[...] = a_ref[1 - mine] + b_ref[1 - mine]


def merge(idx, which, a, b):
    return pl.pallas_call(
        partial(merge_kernel, which),
        in_specs=[SMEM_SPEC, VMEM_SPEC, VMEM_SPEC],
        out_specs=[VMEM_SPEC, VMEM_SPEC],
        out_shape=[jax.ShapeDtypeStruct(a.shape[1:], BF16)] * 2,
        compiler_params=pltpu.CompilerParams(vmem_limit_bytes=4 << 20),
    )(idx, a, b)


def flip(value, axis, size, bit):
    return lax.ppermute(value, axis, [(i, i ^ bit) for i in range(size)])


def reduce_grads(idx, keep, send, replicas):
    got = flip(send, "replica", replicas, 1)
    own, other = merge(idx, 0, keep, got)
    got = flip(other, "group", 2, 1)
    own, other = merge(idx, 2, own, got)
    got = flip(other, "replica", replicas, 2)
    own = own + got
    bit = 4
    while bit < replicas:
        got = flip(own, "replica", replicas, bit)
        own = own + got
        bit *= 2
    side = flip(own, "replica", replicas, 2)
    far_own = flip(own, "replica", replicas, 1)
    return own, side, far_own, flip(side, "replica", replicas, 1)


def places(idx_ref):
    core, side = idx_ref[1], idx_ref[2]
    return 2 * core + side, 2 * core + 1 - side, 2 * (1 - core) + side, 2 * (1 - core) + 1 - side


def unpack_mlp_kernel(idx_ref, *refs):
    ins, outs, mlp = refs[:4], refs[4:12], refs[12]
    for k, place in enumerate(places(idx_ref)):
        mlp[place] = ins[k][...].astype(F32)
    g_out, g_bout, g_fc1, g_bfc1, g_fc2, g_bfc2, g_gtwo, g_stwo = outs
    half, width = g_out.shape
    hidden = g_fc1.shape[1]
    quarter = half // 4
    wide = hidden // 8
    for quad in range(4):
        rows = slice(quad * quarter, (quad + 1) * quarter)
        top = 0
        for col in range(hidden // width):
            g_fc1[rows, col * width : (col + 1) * width] = mlp[quad, top : top + quarter]
            top += quarter
        g_fc2[quad * wide : (quad + 1) * wide] = mlp[quad, top : top + wide]
        top += wide
        g_out[rows] = mlp[quad, top : top + quarter]
        top += quarter
        value = mlp[quad, top : top + 1]
        if quad < 2:
            g_bfc1[quad * width : (quad + 1) * width] = value.reshape(width)
        elif quad == 2:
            g_bfc2[...] = value[:, :half].reshape(half)
            g_bout[...] = value[:, half:].reshape(half)
        else:
            g_gtwo[...] = value[:, :half].reshape(half)
            g_stwo[...] = value[:, half:].reshape(half)


def unpack_attention_kernel(idx_ref, *refs):
    ins, outs, att = refs[:4], refs[4:8], refs[8]
    for k, place in enumerate(places(idx_ref)):
        att[place] = ins[k][...].astype(F32)
    g_qkv, g_bqv, g_gone, g_sone = outs
    half = g_qkv.shape[0]
    width = 2 * half
    quarter = half // 4
    for quad in range(4):
        rows = slice(quad * quarter, (quad + 1) * quarter)
        for col in range(3):
            g_qkv[rows, col * width : (col + 1) * width] = att[quad, col * quarter : (col + 1) * quarter]
        value = att[quad, 3 * quarter : 3 * quarter + 1]
        if quad == 0:
            g_bqv[...] = value.reshape(width)
        elif quad == 1:
            g_gone[...] = value[:, :half].reshape(half)
            g_sone[...] = value[:, half:].reshape(half)


def run_unpack(kernel, idx, parts, shapes):
    return pl.pallas_call(
        kernel,
        in_specs=[SMEM_SPEC] + [VMEM_SPEC] * 4,
        out_specs=[VMEM_SPEC] * len(shapes),
        out_shape=[jax.ShapeDtypeStruct(s, F32) for s in shapes],
        scratch_shapes=[pltpu.VMEM((4, *parts[0].shape), F32)],
        compiler_params=pltpu.CompilerParams(vmem_limit_bytes=8 << 20),
    )(idx, *parts)


def interleaved(images):
    micro, slots, seq, width = images.shape
    blocks = images.reshape(micro, slots, seq, width // 128, 128)
    blocks = with_layout_constraint(blocks, Layout(major_to_minor=(0, 2, 3, 1, 4)))
    return blocks.transpose(0, 2, 3, 1, 4).reshape(-1, 128)


def separated(rows, shape):
    micro, slots, seq, width = shape
    blocks = rows.reshape(micro, seq, width // 128, slots, 128).transpose(0, 1, 3, 2, 4)
    return blocks.reshape(micro, seq, slots, width).transpose(0, 2, 1, 3)


SPLITS = ((0, 1), (1, 4))


def local(
    replicas,
    images, image_count, cotangent, w_qkv, b_qv, w_out, b_out, w_fc1, b_fc1, w_fc2, b_fc2,
    gain_one, shift_one, gain_two, shift_two,
):
    replica = lax.axis_index("replica")
    idx = jnp.stack([lax.axis_index("group"), replica & 1, (replica >> 1) & 1]).astype(jnp.int32)
    count = images.shape[0] * images.shape[1]
    vectors = (b_qv, b_out, b_fc1, b_fc2, gain_one, shift_one, gain_two, shift_two)
    first, small = run_pack_first(idx, w_qkv, vectors)
    second = run_pack_second(idx, w_out, w_fc1, w_fc2)
    near_first = flip(first, "group", 2, 1)
    near_second = flip(second, "group", 2, 1)
    far_first = flip(near_first, "replica", replicas, 1)
    far_second = flip(near_second, "replica", replicas, 1)
    view = interleaved(images)
    qkv, prob, att, hat, rstd, w_all, vec, b1 = run_attention(count, idx, view, w_qkv, near_first, far_first, small)
    act, middle, dx, datt, w_two, keep_b, send_b = run_mlp(
        idx, image_count, view, interleaved(cotangent), att, w_out, w_fc1, w_fc2,
        near_second, far_second, vec, b1,
    )
    carried = ()
    for begin, end in SPLITS:
        carried = run_attention_back(begin, end, idx, hat, qkv, prob, att, datt, w_all, vec, carried)
    dqkv, _, _, keep_c, send_c = carried
    din = run_input_grad(view.shape, hat, rstd, dqkv, dx, w_all, vec)
    out = run_outputs(view.shape, image_count, act, middle, w_two, vec)
    mlp = reduce_grads(idx, keep_b, send_b, replicas)
    attention = reduce_grads(idx, keep_c, send_c, replicas)
    shape_of = lambda *arrays: [v.shape for v in arrays]
    g_out, g_bout, g_fc1, g_bfc1, g_fc2, g_bfc2, g_gtwo, g_stwo = run_unpack(
        unpack_mlp_kernel, idx, mlp,
        shape_of(w_out, b_out, w_fc1, b_fc1, w_fc2, b_fc2, gain_two, shift_two),
    )
    g_qkv, g_bqv, g_gone, g_sone = run_unpack(
        unpack_attention_kernel, idx, attention, shape_of(w_qkv, b_qv, gain_one, shift_one)
    )
    return (
        separated(out, images.shape), separated(din, images.shape),
        g_qkv, g_bqv, g_out, g_bout, g_fc1, g_bfc1, g_fc2, g_bfc2, g_gone, g_sone, g_gtwo, g_stwo,
    )


def step(replicas, *args):
    return local(replicas, *args)


def solution(mesh):
    split = P(None, ("group", "replica"), None, None)
    matrix, vector = P("group", None), P("group")
    return jax.shard_map(
        partial(step, mesh.shape["replica"]),
        mesh=mesh,
        in_specs=(split, P(None, ("group", "replica")), split)
        + (matrix, vector) * 4
        + (vector,) * 4,
        out_specs=(split, split) + (matrix, vector) * 4 + (vector,) * 4,
        check_vma=False,
    )
```

```python
from functools import partial

import jax
import jax.numpy as jnp
from jax import lax
from jax.experimental import pallas as pl
from jax.experimental.layout import Layout, with_layout_constraint
from jax.experimental.pallas import tpu as pltpu
from jax.sharding import PartitionSpec as P


HEADS = 6
ROWS = 208
KEYS = 256
F32 = jnp.float32
BF16 = jnp.bfloat16
NT = (((1,), (1,)), ((), ()))
TN = (((0,), (0,)), ((), ()))


def mm(a, b):
    return jnp.dot(a, b, preferred_element_type=F32)


def mm_nt(a, b):
    return lax.dot_general(a, b, NT, preferred_element_type=F32)


def mm_tn(a, b):
    return lax.dot_general(a, b, TN, preferred_element_type=F32)


def normalize(values):
    center = values - jnp.mean(values, axis=-1, keepdims=True)
    spread = jnp.mean(center * center, axis=-1, keepdims=True)
    rstd = lax.rsqrt(spread + 1e-06)
    return center * rstd, rstd


def norm_back(grad_normed, hat, rstd, gain):
    grad_hat = grad_normed * gain
    first = jnp.mean(grad_hat, axis=-1, keepdims=True)
    second = jnp.mean(grad_hat * hat, axis=-1, keepdims=True)
    return rstd * (grad_hat - first - hat * second)


def gelu_parts(pre, d_act):
    size = jnp.abs(pre)
    density = jnp.exp2(pre * (pre * -0.7213475204444817))
    t = 1.0 / (1.0 + 0.2316418882663604 * size)
    poly = t * (
        0.127414796
        + t * (-0.142248368 + t * (0.7107068705 + t * (-0.7265760135 + t * 0.5307027145)))
    )
    act = jnp.maximum(pre, 0.0) - size * (poly * density)
    edge = density * (poly - 0.3989422804014327 * size)
    slope = jnp.where(pre < 0.0, edge, 1.0 - edge)
    return act.astype(BF16), (d_act * slope).astype(BF16)


def read_image(ref, micro, slot, seq, target, top):
    tiles = target.shape[1] // 128
    for tile in range(tiles):
        start = micro * (seq * tiles * 2) + 2 * tile + slot
        target[top : top + seq, tile * 128 : tile * 128 + 128] = ref[pl.ds(start, seq, stride=2 * tiles), :]


def write_image(ref, micro, slot, seq, value):
    tiles = value.shape[1] // 128
    for tile in range(tiles):
        start = micro * (seq * tiles * 2) + 2 * tile + slot
        ref[pl.ds(start, seq, stride=2 * tiles), :] = value[:seq, tile * 128 : tile * 128 + 128]


def joined(first, second, row, size):
    return jnp.concatenate([first[row : row + 1, :size], second[row : row + 1, :size]], axis=1)


def ordered(idx_ref, mine, theirs):
    low = idx_ref[0] == 0
    mine, theirs = mine.astype(F32), theirs.astype(F32)
    return jnp.where(low, mine, theirs), jnp.where(low, theirs, mine)


def fetch(pairs, sem, first, step, steps):
    def copies(k, slot):
        return [
            pltpu.make_async_copy(source.at[pl.ds(2 * (first + k), 2)], target.at[slot], sem.at[n, slot])
            for n, (source, target) in enumerate(pairs)
        ]

    now = lax.rem(step, 2)

    @pl.when(step == 0)
    def _():
        for copy in copies(0, 0):
            copy.start()

    @pl.when(step + 1 < steps)
    def _():
        for copy in copies(step + 1, 1 - now):
            copy.start()

    for copy in copies(step, now):
        copy.wait()
    return [target.at[now] for _, target in pairs]


HBM_SPEC = pl.BlockSpec(memory_space=pltpu.HBM)


def in_hbm(*arrays):
    return [pltpu.with_memory_space_constraint(array, pltpu.HBM) for array in arrays]


def at(start, size):
    return pl.ds(pl.multiple_of(start, 16), size)


VMEM_SPEC = pl.BlockSpec(memory_space=pltpu.VMEM)


def pack_first_kernel(idx_ref, wq_ref, *refs):
    vectors, first_ref, small_ref = refs[:-2], refs[-2], refs[-1]
    part = wq_ref.shape[0]
    small_ref[...] = jnp.zeros_like(small_ref)
    for k, ref in enumerate(vectors):
        size = ref.shape[0]
        small_ref[k : k + 1, :size] = ref[...].reshape(1, size)
    first_ref[:part, :] = wq_ref[...]
    first_ref[part:, :] = jnp.zeros((16, first_ref.shape[1]), BF16)
    first_ref[part : part + 8, : small_ref.shape[1]] = small_ref[...]


def pack_second_kernel(idx_ref, wo_ref, w1_ref, w2_ref, second_ref):
    part, width = wo_ref.shape
    hidden = w1_ref.shape[1]
    second_ref[:, :width] = wo_ref[...]
    second_ref[:, width : width + hidden] = w1_ref[...]
    for k in range(hidden // width):
        second_ref[:, width + hidden + k * width : width + hidden + (k + 1) * width] = w2_ref[
            k * part : (k + 1) * part, :
        ]


def own_rows(rows, columns):
    return pl.BlockSpec((rows, columns), lambda i, idx: (idx[1], 0))


def run_pack_first(idx, w_qkv, vectors):
    half, wide = w_qkv.shape
    longest = max(v.shape[0] for v in vectors)
    shapes = [(half // 2 + 16, wide), (8, longest)]
    return pl.pallas_call(
        pack_first_kernel,
        grid_spec=pltpu.PrefetchScalarGridSpec(
            num_scalar_prefetch=1,
            grid=(1,),
            in_specs=[own_rows(half // 2, wide)] + [pl.BlockSpec(v.shape, lambda i, idx: (0,)) for v in vectors],
            out_specs=[pl.BlockSpec(s, lambda i, idx: (0, 0)) for s in shapes],
        ),
        out_shape=[jax.ShapeDtypeStruct(s, BF16) for s in shapes],
        name="pack_first",
    )(idx, w_qkv, *vectors)


def run_pack_second(idx, w_out, w_fc1, w_fc2):
    half, width = w_out.shape
    hidden = w_fc1.shape[1]
    part = half // 2
    shape = (part, width + 2 * hidden)
    return pl.pallas_call(
        pack_second_kernel,
        grid_spec=pltpu.PrefetchScalarGridSpec(
            num_scalar_prefetch=1,
            grid=(1,),
            in_specs=[own_rows(part, width), own_rows(part, hidden), own_rows(hidden // 4, width)],
            out_specs=pl.BlockSpec(shape, lambda i, idx: (0, 0)),
        ),
        out_shape=jax.ShapeDtypeStruct(shape, BF16),
        name="pack_second",
    )(idx, w_out, w_fc1, w_fc2)


def attention_kernel(
    idx_ref, x_ref, w_ref, near_ref, far_ref, small_ref,
    qkv_ref, prob_ref, att_ref, hat_ref, rstd_ref, whole_ref, vec_ref, b1_ref,
    raw, view, xs, kv, bias, scores, raw_sem,
):
    step = pl.program_id(0)
    half, wide = w_ref.shape
    width = wide // 3
    part = half // 2
    pairs = width // 128
    seq = x_ref.shape[0] * 128 // (width * 2 * pl.num_programs(0))

    @pl.when(step == 0)
    def _():
        load = pltpu.make_async_copy(x_ref, raw, raw_sem)
        load.start()
        xs[...] = jnp.zeros_like(xs)
        kv[...] = jnp.zeros_like(kv)
        group, core = idx_ref[0], idx_ref[1]
        first, second = ordered(idx_ref, small_ref[...], near_ref[part : part + 8, : small_ref.shape[1]])
        for k, row in enumerate((4, 5, 1, 3, 6, 7)):
            vec_ref[k : k + 1, :] = joined(first, second, row, half)
        b1_ref[0:1, :] = jnp.concatenate([first[2:3, :], second[2:3, :]], axis=1)
        other = (1 - group) * half
        for pair in range(pairs):
            for kind in range(3):
                source = slice(kind * width + pair * 128, kind * width + pair * 128 + 128)
                target = slice((3 * pair + kind) * 128, (3 * pair + kind) * 128 + 128)
                whole_ref[at(group * half, half), target] = w_ref[:, source]
                whole_ref[at(other + core * part, part), target] = near_ref[:part, source]
                whole_ref[at(other + (1 - core) * part, part), target] = far_ref[:part, source]
                lanes = slice(pair * 128, pair * 128 + 128)
                piece = (first[0:1, lanes], jnp.zeros((1, 128), F32), second[0:1, lanes])[kind]
                bias[0:1, target] = piece
        load.wait()
        view[...] = raw[...].astype(F32)

    for slot in range(2):
        read_image(view, step, slot, seq, xs, slot * ROWS)
    hat, rstd = normalize(xs[...])
    hat_ref[...] = hat.astype(BF16).reshape(2, ROWS, width)
    rstd_ref[...] = jnp.broadcast_to(rstd, (2 * ROWS, 128)).reshape(2, ROWS, 128)
    normed = (hat * vec_ref[0:1, :] + vec_ref[1:2, :]).astype(BF16)
    low_half = lax.broadcasted_iota(jnp.int32, (1, 128), 1) < 64
    column = lax.broadcasted_iota(jnp.int32, (1, KEYS), 1)

    def project(pair):
        lanes = slice(pair * 384, pair * 384 + 384)
        qkv = (mm(normed, whole_ref[:, lanes]) + bias[0:1, lanes]).astype(BF16)
        for slot in range(2):
            part = qkv[slot * ROWS : slot * ROWS + ROWS]
            qkv_ref[slot, :, lanes] = part
            kv[slot, :ROWS, pair * 256 : pair * 256 + 256] = part[:, 128:]

    def masked(values, head):
        mask = low_half if head % 2 == 0 else jnp.logical_not(low_half)
        return jnp.where(mask, values, jnp.zeros_like(values))

    def first_part(slot, head):
        pair = head // 2
        query = qkv_ref[slot, :, pair * 384 : pair * 384 + 128] * jnp.array(0.125, BF16)
        scores[slot, head % 2] = mm_nt(query, masked(kv[slot, :, pair * 256 : pair * 256 + 128], head))

    def second_part(slot, head):
        for r in range(0, ROWS, 16):
            value = jnp.where(column < seq, scores[slot, head % 2, r : r + 16], -1e30)
            top = jnp.max(value, axis=-1, keepdims=True)
            grown = jnp.exp(value - top)
            prob_ref[slot, head, r : r + 16] = (
                grown * (1.0 / jnp.sum(grown, axis=-1, keepdims=True))
            ).astype(BF16)

    def third_part(slot, head):
        pair = head // 2
        values = kv[slot, :, pair * 256 + 128 : pair * 256 + 256]
        if head % 2 == 1:
            total = mm(prob_ref[slot, head - 1], masked(values, 0)) + mm(prob_ref[slot, head], masked(values, 1))
            att_ref[slot, :, pair * 128 : pair * 128 + 128] = total.astype(BF16)

    project(0)
    for k in range(HEADS + 2):
        for slot in range(2):
            if k < HEADS:
                first_part(slot, k)
            if k >= 2:
                third_part(slot, k - 2)
            if slot == 0 and k % 2 == 0 and k // 2 + 1 < pairs:
                project(k // 2 + 1)
            if 1 <= k <= HEADS:
                second_part(slot, k - 1)


def mlp_kernel(
    idx_ref, count_ref, x_ref, cot_ref, att_hbm, wo_ref, w1_ref, w2_ref, near_ref, far_ref, vec, b1,
    act_ref, middle_ref, dx_ref, datt_ref, w2, keep_ref, send_ref,
    view_x, view_c, xs, dys, acts, dpres, pres, dacts, wo, w1, wot, w1t, w2t, dn_half,
    gw1, gw2, gwo, gsmall, att_buf, raw, att_sem, raw_sem,
):
    step = pl.program_id(0)
    last = pl.num_programs(0) - 1
    half, width = wo_ref.shape
    hidden = w1_ref.shape[1]
    part = half // 2
    rows = xs.shape[0]
    seq = x_ref.shape[0] * 128 // (width * 2 * pl.num_programs(0))
    core = idx_ref[1]

    @pl.when(step == 0)
    def _():
        loads = [pltpu.make_async_copy(ref, raw.at[k], raw_sem.at[k]) for k, ref in enumerate((x_ref, cot_ref))]
        for load in loads:
            load.start()
        for ref in (xs, dys, gw1, gw2, gwo, gsmall):
            ref[...] = jnp.zeros_like(ref)
        group = idx_ref[0]
        wo[at(group * half, half), :] = wo_ref[...]
        w1[at(group * half, half), :] = w1_ref[...]
        w2[at(group * (hidden // 2), hidden // 2), :] = w2_ref[...]
        other = (1 - group) * half
        for ref, which in ((near_ref, core), (far_ref, 1 - core)):
            wo[at(other + which * part, part), :] = ref[:, :width]
            w1[at(other + which * part, part), :] = ref[:, width : width + hidden]
            base = (1 - group) * (hidden // 2) + which * (hidden // 4)
            for k in range(hidden // width):
                w2[at(base + k * part, part), :] = ref[:, width + hidden + k * width : width + hidden + (k + 1) * width]
        wot[...] = wo[...].T
        w1t[...] = w1[...].T
        w2t[...] = w2[...].T
        for load, target, k in zip(loads, (view_x, view_c), range(2)):
            load.wait()
            target[...] = raw[k].astype(F32)

    (att_ref,) = fetch([(att_hbm, att_buf)], att_sem, 0, step, last + 1)
    second_valid = (1 < count_ref[step, 0]).astype(F32)
    for slot in range(2):
        read_image(view_x, step, slot, seq, xs, slot * ROWS)
        read_image(view_c, step, slot, seq, dys, slot * ROWS)
    row = lax.broadcasted_iota(jnp.int32, (rows, 1), 0)
    valid = jnp.where(row < ROWS, 1.0, second_valid)
    att = att_ref[...].reshape(rows, width)
    middle = xs[...] + mm(att, wo[...]) + vec[2:3, :]
    hat, rstd = normalize(middle)
    gain = vec[4:5, :]
    normed = (hat * gain + vec[5:6, :]).astype(BF16)
    d_out = dys[...] * valid
    d_mlp = d_out.astype(BF16)
    normed_t = jnp.concatenate([normed.T, jnp.ones((16, rows), BF16)], axis=0)
    d_mlp_t = d_mlp.T
    chunks = hidden // 256
    middle_of = hidden // 2

    def first_part(c):
        cols = slice(c * 256, c * 256 + 256)
        pres[c % 2] = mm(normed, w1[:, cols])
        dacts[c % 2] = mm(d_mlp, w2t[:, cols])

    def second_part(c):
        cols = slice(c * 256, c * 256 + 256)
        bias = b1[0:1, cols]
        for r in range(0, rows, 32):
            act, d_pre = gelu_parts(pres[c % 2, r : r + 32] + bias, dacts[c % 2, r : r + 32])
            acts[r : r + 32, cols] = act
            act_ref[r // ROWS, r % ROWS : r % ROWS + 16, cols] = act[:16]
            act_ref[(r + 16) // ROWS, (r + 16) % ROWS : (r + 16) % ROWS + 16, cols] = act[16:]
            dpres[r : r + 32, cols] = d_pre

    def third_part(c):
        cols = slice(c * 256, c * 256 + 256)
        gw1[:, cols] += mm(normed_t, dpres[:, cols])
        gw2[:, cols] += mm(d_mlp_t, acts[:, cols])

    for k in range(chunks + 2):
        if k < chunks:
            first_part(k)
        if k >= 2:
            third_part(k - 2)
        if k == chunks // 2 + 1:
            dn_half[...] = mm(dpres[:, :middle_of], w1t[:middle_of, :])
        if 1 <= k <= chunks:
            second_part(k - 1)

    middle_ref[...] = middle.reshape(2, ROWS, width)
    d_normed = dn_half[...] + mm(dpres[:, middle_of:], w1t[middle_of:, :])
    dx = d_out + norm_back(d_normed, hat, rstd, gain)
    d_attn = dx.astype(BF16)
    dx_ref[...] = d_attn.reshape(2, ROWS, width)
    datt_ref[...] = mm(d_attn, wot[...]).astype(BF16).reshape(2, ROWS, width)
    gwo[...] += mm_tn(att, d_attn)

    def fold(values):
        return jnp.sum(values.reshape(rows // 8, 8, width), axis=0)

    gsmall[0] += fold(d_out)
    gsmall[1] += fold(d_attn.astype(F32))
    gsmall[2] += fold(d_normed * hat)
    gsmall[3] += fold(d_normed)

    @pl.when(step == last)
    def _():
        quarter = half // 4
        wide = hidden // 8
        gw2_t = gw2[...].T
        small_rows = [jnp.sum(gsmall[k], axis=0, keepdims=True) for k in range(4)]

        def emit(group, quad, ref, side):
            base = group * half + quad * quarter
            top = 0
            for col in range(hidden // width):
                ref[group, side, top : top + quarter, :] = gw1[
                    base : base + quarter, col * width : (col + 1) * width
                ].astype(BF16)
                top += quarter
            start = group * (hidden // 2) + quad * wide
            ref[group, side, top : top + wide, :] = gw2_t[start : start + wide].astype(BF16)
            top += wide
            ref[group, side, top : top + quarter, :] = gwo[base : base + quarter, :].astype(BF16)
            top += quarter
            if quad < 2:
                start = group * (hidden // 2) + quad * width
                value = gw1[width : width + 1, start : start + width]
            else:
                own = slice(group * half, group * half + half)
                value = jnp.concatenate(
                    [small_rows[2 * quad - 4][:, own], small_rows[2 * quad - 3][:, own]], axis=1
                )
            ref[group, side, top : top + 16, :] = jnp.broadcast_to(value, (16, width)).astype(BF16)

        split_quads(core, emit, keep_ref, send_ref)


def split_quads(core, emit, keep_ref, send_ref):
    for mine in range(2):

        @pl.when(core == mine)
        def _():
            for group in range(2):
                for side in range(2):
                    emit(group, 2 * mine + side, keep_ref, side)
                    emit(group, 2 * (1 - mine) + side, send_ref, side)


def attention_back_kernel(
    first_micro, last, idx_ref, hat_hbm, qkv_hbm, prob_hbm, att_hbm, datt_hbm, w_ref, vec_ref, *refs
):
    carried = 0 if first_micro == 0 else 3
    dqkv_ref, total_ref, sums_ref = refs[carried : carried + 3]
    kv, hat_t, d_probs, d_scores = refs[-10:-6]
    buffers, sem = refs[-6:-1], refs[-1]
    step = pl.program_id(0)
    width = w_ref.shape[0]
    pairs = width // 128
    sources = (hat_hbm, datt_hbm, qkv_hbm, att_hbm, prob_hbm)
    hat_ref, datt_ref, qkv_ref, att_ref, prob_ref = fetch(
        list(zip(sources, buffers)), sem, first_micro, step, pl.num_programs(0)
    )

    @pl.when(step == 0)
    def _():
        kv[...] = jnp.zeros_like(kv)
        if not carried:
            total_ref[...] = jnp.zeros_like(total_ref)
            sums_ref[...] = jnp.zeros_like(sums_ref)

    hat_t[...] = hat_ref[...].reshape(2 * ROWS, width).T
    for pair in range(pairs):
        kv[:, :ROWS, pair * 256 : pair * 256 + 256] = qkv_ref[:, :, pair * 384 + 128 : pair * 384 + 384]
    low_half = lax.broadcasted_iota(jnp.int32, (1, 128), 1) < 64

    def masked(values, head):
        mask = low_half if head % 2 == 0 else jnp.logical_not(low_half)
        return jnp.where(mask, values, jnp.zeros_like(values))

    def lanes(head):
        return slice(head // 2 * 128, head // 2 * 128 + 128)

    def first_part(slot, head):
        pair = head // 2
        d_probs[slot, head % 2] = mm_nt(
            datt_ref[slot, :, lanes(head)], masked(kv[slot, :, pair * 256 + 128 : pair * 256 + 256], head)
        )

    def second_part(slot, head):
        for r in range(0, ROWS, 16):
            rows = slice(r, r + 16)
            product = datt_ref[slot, rows, lanes(head)].astype(F32) * att_ref[slot, rows, lanes(head)].astype(F32)
            delta = jnp.sum(masked(product, head), axis=-1, keepdims=True)
            d_scores[slot, head % 4, rows] = (
                prob_ref[slot, head, rows].astype(F32) * (d_probs[slot, head % 2, rows] - delta)
            ).astype(BF16)

    def third_part(slot, pair):
        query = qkv_ref[slot, :, pair * 384 : pair * 384 + 128] * jnp.array(0.125, BF16)
        keys = kv[slot, :, pair * 256 : pair * 256 + 128] * jnp.array(0.125, BF16)
        d_att = datt_ref[slot, :, pair * 128 : pair * 128 + 128]
        dq = dk = dv = 0.0
        for head in (2 * pair, 2 * pair + 1):
            d_score = d_scores[slot, head % 4]
            dv = dv + mm_tn(prob_ref[slot, head], masked(d_att, head))
            dk = dk + mm_tn(d_score, masked(query, head))
            dq = dq + mm(d_score, masked(keys, head))
        top = pair * 384
        dqkv_ref[slot, :, top : top + 128] = dq.astype(BF16)
        dqkv_ref[slot, :, top + 128 : top + 256] = dk[:ROWS].astype(BF16)
        dqkv_ref[slot, :, top + 256 : top + 384] = dv[:ROWS].astype(BF16)

    def fourth_part(pair):
        columns = slice(pair * 384, pair * 384 + 384)
        joined_back = dqkv_ref[:, :, columns].reshape(2 * ROWS, 384)
        total_ref[:, columns] += mm(hat_t[...], joined_back)
        sums_ref[:, columns] += jnp.sum(joined_back.astype(F32).reshape(ROWS // 4, 8, 384), axis=0)

    for k in range(HEADS + 3):
        for slot in range(2):
            if k < HEADS:
                first_part(slot, k)
            if k >= 3 and k % 2 == 1:
                third_part(slot, k // 2 - 1)
            if slot == 0 and k >= 4 and k % 2 == 0:
                fourth_part(k // 2 - 2)
            if 1 <= k <= HEADS:
                second_part(slot, k - 1)

    if last:
        keep_ref, send_ref = refs[carried + 3 : carried + 5]

        @pl.when(step == pl.num_programs(0) - 1)
        def _():
            half = width // 2
            quarter = half // 4
            total_sums = jnp.sum(sums_ref[...], axis=0, keepdims=True)
            weights = w_ref[...].astype(F32)
            d_gain = jnp.sum((weights * total_ref[...]).reshape(width, 3 * width), axis=1, keepdims=True)
            d_shift = jnp.sum(weights * total_sums, axis=1, keepdims=True)
            columns = jnp.concatenate([vec_ref[...], jnp.zeros((120, width), F32)], axis=0).T
            gain, shift = columns[:, 0:1], columns[:, 1:2]
            total_ref[...] = total_ref[...] * gain + shift * total_sums
            lane = lax.broadcasted_iota(jnp.int32, (1, 128), 1)
            both = jnp.where(lane == 0, d_gain, jnp.where(lane == 1, d_shift, 0.0)).T

            def emit(group, quad, ref, side):
                base = group * half + quad * quarter
                for kind in range(3):
                    for pair in range(pairs):
                        source = slice((3 * pair + kind) * 128, (3 * pair + kind) * 128 + 128)
                        ref[group, side, kind * quarter : (kind + 1) * quarter, pair * 128 : pair * 128 + 128] = (
                            total_ref[base : base + quarter, source].astype(BF16)
                        )
                if quad == 0:
                    kind = 2 * group
                    value = jnp.concatenate(
                        [total_sums[:, (3 * p + kind) * 128 : (3 * p + kind) * 128 + 128] for p in range(pairs)], axis=1
                    )
                else:
                    own = slice(group * half, group * half + half)
                    value = jnp.concatenate([both[0:1, own], both[1:2, own]], axis=1)
                ref[group, side, 3 * quarter : 3 * quarter + 16, :] = jnp.broadcast_to(value, (16, width)).astype(BF16)

            split_quads(idx_ref[1], emit, keep_ref, send_ref)


def input_grad_kernel(hat_hbm, rstd_hbm, dqkv_hbm, dx_hbm, w_ref, vec_ref, din_ref, outs, wt, *refs):
    step = pl.program_id(0)
    width = w_ref.shape[0]
    micros = pl.num_programs(0)
    seq = din_ref.shape[0] * 128 // (width * 2 * micros)
    rows = 2 * ROWS
    sources = (hat_hbm, rstd_hbm, dqkv_hbm, dx_hbm)
    hat_ref, rstd_ref, dqkv_ref, dx_ref = fetch(list(zip(sources, refs[:-1])), refs[-1], 0, step, micros)

    @pl.when(step == 0)
    def _():
        wt[...] = w_ref[...].T

    d_normed = mm(dqkv_ref[...].reshape(rows, 3 * width), wt[...])
    hat = hat_ref[...].reshape(rows, width).astype(F32)
    rstd = rstd_ref[...].reshape(rows, 128)[:, 0:1]
    d_in = dx_ref[...].reshape(rows, width).astype(F32) + norm_back(d_normed, hat, rstd, vec_ref[0:1, :])
    for slot in range(2):
        write_image(outs, step, slot, seq, d_in[slot * ROWS : slot * ROWS + ROWS])

    @pl.when(step == micros - 1)
    def _():
        din_ref[...] = outs[...].astype(BF16)


def outputs_kernel(count_ref, act_hbm, middle_hbm, w2_ref, vec_ref, out_ref, outs, act_buf, middle_buf, sem):
    step = pl.program_id(0)
    hidden, width = w2_ref.shape
    micros = pl.num_programs(0)
    seq = out_ref.shape[0] * 128 // (width * 2 * micros)
    rows = 2 * ROWS
    act_ref, middle_ref = fetch([(act_hbm, act_buf), (middle_hbm, middle_buf)], sem, 0, step, micros)
    row = lax.broadcasted_iota(jnp.int32, (rows, 1), 0)
    valid = jnp.where(row < ROWS, 1.0, (1 < count_ref[step, 0]).astype(F32))
    mlp = mm(act_ref[...].reshape(rows, hidden), w2_ref[...]) + vec_ref[3:4, :]
    result = (middle_ref[...].reshape(rows, width) + mlp) * valid
    for slot in range(2):
        write_image(outs, step, slot, seq, result[slot * ROWS : slot * ROWS + ROWS])

    @pl.when(step == micros - 1)
    def _():
        out_ref[...] = outs[...].astype(BF16)


def per_pair(*shape):
    return pl.BlockSpec((2, *shape), lambda i: (i,) + (0,) * len(shape))


SMEM_SPEC = pl.BlockSpec(memory_space=pltpu.SMEM)


def run_attention(count, idx, view, w_qkv, near, far, small):
    width = w_qkv.shape[1] // 3
    return pl.pallas_call(
        attention_kernel,
        grid=(count // 2,),
        in_specs=[SMEM_SPEC, HBM_SPEC] + [VMEM_SPEC] * 4,
        out_specs=[
            per_pair(ROWS, 3 * width), per_pair(HEADS, ROWS, KEYS), per_pair(ROWS, width),
            per_pair(ROWS, width), per_pair(ROWS, 128), VMEM_SPEC, VMEM_SPEC, VMEM_SPEC,
        ],
        out_shape=[
            pltpu.HBM((count, ROWS, 3 * width), BF16),
            pltpu.HBM((count, HEADS, ROWS, KEYS), BF16),
            pltpu.HBM((count, ROWS, width), BF16),
            pltpu.HBM((count, ROWS, width), BF16),
            pltpu.HBM((count, ROWS, 128), F32),
            jax.ShapeDtypeStruct((width, 3 * width), BF16),
            jax.ShapeDtypeStruct((8, width), F32),
            jax.ShapeDtypeStruct((8, 2 * small.shape[1]), F32),
        ],
        scratch_shapes=[
            pltpu.VMEM(view.shape, BF16),
            pltpu.VMEM(view.shape, F32),
            pltpu.VMEM((2 * ROWS, width), F32),
            pltpu.VMEM((2, KEYS, 2 * width), BF16),
            pltpu.VMEM((8, 3 * width), F32),
            pltpu.VMEM((2, 2, ROWS, KEYS), F32),
            pltpu.SemaphoreType.DMA,
        ],
        compiler_params=pltpu.CompilerParams(vmem_limit_bytes=22 << 20),
        cost_estimate=pl.CostEstimate(flops=5 << 30, bytes_accessed=20 << 20, transcendentals=0),
        name="attention_fwd",
    )(idx, *in_hbm(view), w_qkv, near, far, small)


def run_mlp(idx, counts, view, cot, att, wo, w1, w2, near, far, vec, b1):
    width = wo.shape[1]
    hidden = w1.shape[1]
    micro = counts.shape[0]
    rows = 2 * ROWS
    packed = width // 8 * (hidden // width) + hidden // 8 + width // 8 + 16
    two = pl.BlockSpec((2, ROWS, width), lambda i: (i, 0, 0))
    return pl.pallas_call(
        mlp_kernel,
        grid=(micro,),
        in_specs=[SMEM_SPEC, SMEM_SPEC, HBM_SPEC, HBM_SPEC, HBM_SPEC] + [VMEM_SPEC] * 7,
        out_specs=[per_pair(ROWS, hidden), two, two, two, VMEM_SPEC, VMEM_SPEC, VMEM_SPEC],
        out_shape=[
            pltpu.HBM((2 * micro, ROWS, hidden), BF16),
            pltpu.HBM(att.shape, F32),
            pltpu.HBM(att.shape, BF16),
            pltpu.HBM(att.shape, BF16),
            jax.ShapeDtypeStruct((hidden, width), BF16),
            jax.ShapeDtypeStruct((2, 2, packed, width), BF16),
            jax.ShapeDtypeStruct((2, 2, packed, width), BF16),
        ],
        scratch_shapes=[
            pltpu.VMEM(view.shape, F32),
            pltpu.VMEM(view.shape, F32),
            pltpu.VMEM((rows, width), F32),
            pltpu.VMEM((rows, width), F32),
            pltpu.VMEM((rows, hidden), BF16),
            pltpu.VMEM((rows, hidden), BF16),
            pltpu.VMEM((2, rows, 256), F32),
            pltpu.VMEM((2, rows, 256), F32),
            pltpu.VMEM((width, width), BF16),
            pltpu.VMEM((width, hidden), BF16),
            pltpu.VMEM((width, width), BF16),
            pltpu.VMEM((hidden, width), BF16),
            pltpu.VMEM((width, hidden), BF16),
            pltpu.VMEM((rows, width), F32),
            pltpu.VMEM((width + 16, hidden), F32),
            pltpu.VMEM((width, hidden), F32),
            pltpu.VMEM((width, width), F32),
            pltpu.VMEM((4, 8, width), F32),
            pltpu.VMEM((2, 2, ROWS, width), BF16),
            pltpu.VMEM((2, *view.shape), BF16),
            pltpu.SemaphoreType.DMA((1, 2)),
            pltpu.SemaphoreType.DMA((2,)),
        ],
        compiler_params=pltpu.CompilerParams(vmem_limit_bytes=40 << 20),
        cost_estimate=pl.CostEstimate(flops=12 << 30, bytes_accessed=20 << 20, transcendentals=0),
        name="mlp_fwd_bwd",
    )(idx, counts, *in_hbm(view, cot, att), wo, w1, w2, near, far, vec, b1)


def run_attention_back(begin, end, idx, hat, qkv, prob, att, datt, w_qkv, vec, carried):
    count = qkv.shape[0]
    width = w_qkv.shape[0]
    packed = width // 8 * 3 + 16
    last = 2 * end == count
    block = pl.BlockSpec((2, ROWS, 3 * width), lambda i: (i + begin, 0, 0))
    two = lambda *shape: pltpu.VMEM((2, 2, *shape), BF16)
    return pl.pallas_call(
        partial(attention_back_kernel, begin, last),
        grid=(end - begin,),
        in_specs=[SMEM_SPEC] + [HBM_SPEC] * 5 + [VMEM_SPEC] * 2
        + ([HBM_SPEC, VMEM_SPEC, VMEM_SPEC] if carried else []),
        out_specs=[block, VMEM_SPEC, VMEM_SPEC] + ([VMEM_SPEC] * 2 if last else []),
        out_shape=[
            pltpu.HBM((count, ROWS, 3 * width), BF16),
            jax.ShapeDtypeStruct((width, 3 * width), F32),
            jax.ShapeDtypeStruct((8, 3 * width), F32),
        ]
        + [jax.ShapeDtypeStruct((2, 2, packed, width), BF16)] * (2 if last else 0),
        scratch_shapes=[
            pltpu.VMEM((2, KEYS, 2 * width), BF16),
            pltpu.VMEM((width, 2 * ROWS), BF16),
            pltpu.VMEM((2, 2, ROWS, KEYS), F32),
            pltpu.VMEM((2, 4, ROWS, KEYS), BF16),
            two(ROWS, width), two(ROWS, width), two(ROWS, 3 * width), two(ROWS, width), two(HEADS, ROWS, KEYS),
            pltpu.SemaphoreType.DMA((5, 2)),
        ],
        input_output_aliases={8: 0, 9: 1, 10: 2} if carried else {},
        compiler_params=pltpu.CompilerParams(vmem_limit_bytes=18 << 20),
        cost_estimate=pl.CostEstimate(flops=(end - begin) << 31, bytes_accessed=20 << 20, transcendentals=0),
    )(idx, *in_hbm(hat, qkv, prob, att, datt), w_qkv, vec, *in_hbm(*carried[:1]), *carried[1:])


def run_input_grad(view_shape, hat, rstd, dqkv, dx, w_qkv, vec):
    count = dqkv.shape[0]
    width = w_qkv.shape[0]
    two = lambda dtype, *shape: pltpu.VMEM((2, 2, *shape), dtype)
    return pl.pallas_call(
        input_grad_kernel,
        grid=(count // 2,),
        in_specs=[HBM_SPEC] * 4 + [VMEM_SPEC] * 2,
        out_specs=VMEM_SPEC,
        out_shape=jax.ShapeDtypeStruct(view_shape, BF16),
        scratch_shapes=[
            pltpu.VMEM(view_shape, F32),
            pltpu.VMEM((3 * width, width), BF16),
            two(BF16, ROWS, width), two(F32, ROWS, 128), two(BF16, ROWS, 3 * width), two(BF16, ROWS, width),
            pltpu.SemaphoreType.DMA((4, 2)),
        ],
        compiler_params=pltpu.CompilerParams(vmem_limit_bytes=14 << 20),
        cost_estimate=pl.CostEstimate(flops=2 << 30, bytes_accessed=20 << 20, transcendentals=0),
        name="input_grad",
    )(*in_hbm(hat, rstd, dqkv, dx), w_qkv, vec)


def run_outputs(view_shape, counts, act, middle, w2, vec):
    count, _, hidden = act.shape
    width = w2.shape[1]
    return pl.pallas_call(
        outputs_kernel,
        grid=(count // 2,),
        in_specs=[SMEM_SPEC] + [HBM_SPEC] * 2 + [VMEM_SPEC] * 2,
        out_specs=VMEM_SPEC,
        out_shape=jax.ShapeDtypeStruct(view_shape, BF16),
        scratch_shapes=[
            pltpu.VMEM(view_shape, F32),
            pltpu.VMEM((2, 2, ROWS, hidden), BF16), pltpu.VMEM((2, 2, ROWS, width), F32),
            pltpu.SemaphoreType.DMA((2, 2)),
        ],
        compiler_params=pltpu.CompilerParams(vmem_limit_bytes=14 << 20),
        cost_estimate=pl.CostEstimate(flops=2 << 30, bytes_accessed=20 << 20, transcendentals=0),
        name="layer_outputs",
    )(counts, *in_hbm(act, middle), w2, vec)


def merge_kernel(which, idx_ref, a_ref, b_ref, own_ref, other_ref):
    mine = idx_ref[which]
    own_ref[...] = a_ref[mine] + b_ref[mine]
    other_ref[...] = a_ref[1 - mine] + b_ref[1 - mine]


def merge(idx, which, a, b):
    return pl.pallas_call(
        partial(merge_kernel, which),
        in_specs=[SMEM_SPEC, VMEM_SPEC, VMEM_SPEC],
        out_specs=[VMEM_SPEC, VMEM_SPEC],
        out_shape=[jax.ShapeDtypeStruct(a.shape[1:], BF16)] * 2,
        compiler_params=pltpu.CompilerParams(vmem_limit_bytes=4 << 20),
    )(idx, a, b)


def flip(value, axis, size, bit):
    return lax.ppermute(value, axis, [(i, i ^ bit) for i in range(size)])


def exchange(own, replicas, bit):
    while bit < replicas:
        got = flip(own, "replica", replicas, bit)
        own = own + got
        bit *= 2
    return own


def reduce_grads(idx, keep, send, replicas):
    own, other = merge(idx, 0, keep, flip(send, "replica", replicas, 1))
    own, other = merge(idx, 2, own, flip(other, "group", 2, 1))
    got = flip(other, "replica", replicas, 2)
    own = own + got
    own = exchange(own, replicas, 4)
    side = flip(own, "replica", replicas, 2)
    far_own = flip(own, "replica", replicas, 1)
    return own, side, far_own, flip(side, "replica", replicas, 1)


def reduce_large_grads(idx, keep, send, replicas):
    own, other = merge(idx, 0, keep, flip(send, "replica", replicas, 1))
    own, other = merge(idx, 2, own, flip(other, "group", 2, 1))
    halves = (2, own.shape[0] // 2, own.shape[1])
    got = flip(other, "replica", replicas, 2)
    own, other = merge(idx, 3, own.reshape(halves), got.reshape(halves))
    got = flip(other, "replica", replicas, 4)
    own = own + got
    own = exchange(own, replicas, 8)
    next_own = flip(own, "replica", replicas, 4)
    side = flip(own, "replica", replicas, 2)
    next_side = flip(next_own, "replica", replicas, 2)
    parts = (own, next_own, side, next_side)
    far = [flip(part, "replica", replicas, 1) for part in parts]
    return (*parts, *far)


def places(idx_ref):
    core, side = idx_ref[1], idx_ref[2]
    return 2 * core + side, 2 * core + 1 - side, 2 * (1 - core) + side, 2 * (1 - core) + 1 - side


def unpack_mlp_kernel(idx_ref, *refs):
    ins, outs, mlp = refs[:8], refs[8:16], refs[16]
    low = idx_ref[3]
    lines = ins[0].shape[0]
    for k, place in enumerate(places(idx_ref)):
        mlp[place, at(low * lines, lines)] = ins[2 * k][...].astype(F32)
        mlp[place, at((1 - low) * lines, lines)] = ins[2 * k + 1][...].astype(F32)
    g_out, g_bout, g_fc1, g_bfc1, g_fc2, g_bfc2, g_gtwo, g_stwo = outs
    half, width = g_out.shape
    hidden = g_fc1.shape[1]
    quarter = half // 4
    wide = hidden // 8
    for quad in range(4):
        rows = slice(quad * quarter, (quad + 1) * quarter)
        top = 0
        for col in range(hidden // width):
            g_fc1[rows, col * width : (col + 1) * width] = mlp[quad, top : top + quarter]
            top += quarter
        g_fc2[quad * wide : (quad + 1) * wide] = mlp[quad, top : top + wide]
        top += wide
        g_out[rows] = mlp[quad, top : top + quarter]
        top += quarter
        value = mlp[quad, top : top + 1]
        if quad < 2:
            g_bfc1[quad * width : (quad + 1) * width] = value.reshape(width)
        elif quad == 2:
            g_bfc2[...] = value[:, :half].reshape(half)
            g_bout[...] = value[:, half:].reshape(half)
        else:
            g_gtwo[...] = value[:, :half].reshape(half)
            g_stwo[...] = value[:, half:].reshape(half)


def unpack_attention_kernel(idx_ref, *refs):
    ins, outs, att = refs[:4], refs[4:8], refs[8]
    for k, place in enumerate(places(idx_ref)):
        att[place] = ins[k][...].astype(F32)
    g_qkv, g_bqv, g_gone, g_sone = outs
    half = g_qkv.shape[0]
    width = 2 * half
    quarter = half // 4
    for quad in range(4):
        rows = slice(quad * quarter, (quad + 1) * quarter)
        for col in range(3):
            g_qkv[rows, col * width : (col + 1) * width] = att[quad, col * quarter : (col + 1) * quarter]
        value = att[quad, 3 * quarter : 3 * quarter + 1]
        if quad == 0:
            g_bqv[...] = value.reshape(width)
        elif quad == 1:
            g_gone[...] = value[:, :half].reshape(half)
            g_sone[...] = value[:, half:].reshape(half)


def run_unpack(kernel, idx, parts, shapes):
    return pl.pallas_call(
        kernel,
        in_specs=[SMEM_SPEC] + [VMEM_SPEC] * len(parts),
        out_specs=[VMEM_SPEC] * len(shapes),
        out_shape=[jax.ShapeDtypeStruct(s, F32) for s in shapes],
        scratch_shapes=[pltpu.VMEM((4, parts[0].shape[0] * len(parts) // 4, parts[0].shape[1]), F32)],
        compiler_params=pltpu.CompilerParams(vmem_limit_bytes=8 << 20),
    )(idx, *parts)


def interleaved(images):
    micro, slots, seq, width = images.shape
    blocks = images.reshape(micro, slots, seq, width // 128, 128)
    blocks = with_layout_constraint(blocks, Layout(major_to_minor=(0, 2, 3, 1, 4)))
    return blocks.transpose(0, 2, 3, 1, 4).reshape(-1, 128)


def separated(rows, shape):
    micro, slots, seq, width = shape
    blocks = rows.reshape(micro, seq, width // 128, slots, 128).transpose(0, 1, 3, 2, 4)
    return blocks.reshape(micro, seq, slots, width).transpose(0, 2, 1, 3)


SPLITS = ((0, 1), (1, 4))


def local(
    replicas,
    images, image_count, cotangent, w_qkv, b_qv, w_out, b_out, w_fc1, b_fc1, w_fc2, b_fc2,
    gain_one, shift_one, gain_two, shift_two,
):
    replica = lax.axis_index("replica")
    idx = jnp.stack([lax.axis_index("group"), replica & 1, (replica >> 1) & 1, (replica >> 2) & 1]).astype(jnp.int32)
    count = images.shape[0] * images.shape[1]
    vectors = (b_qv, b_out, b_fc1, b_fc2, gain_one, shift_one, gain_two, shift_two)
    first, small = run_pack_first(idx, w_qkv, vectors)
    second = run_pack_second(idx, w_out, w_fc1, w_fc2)
    near_first = flip(first, "group", 2, 1)
    near_second = flip(second, "group", 2, 1)
    far_first = flip(near_first, "replica", replicas, 1)
    far_second = flip(near_second, "replica", replicas, 1)
    view = interleaved(images)
    qkv, prob, att, hat, rstd, w_all, vec, b1 = run_attention(count, idx, view, w_qkv, near_first, far_first, small)
    act, middle, dx, datt, w_two, keep_b, send_b = run_mlp(
        idx, image_count, view, interleaved(cotangent), att, w_out, w_fc1, w_fc2,
        near_second, far_second, vec, b1,
    )
    carried = ()
    for begin, end in SPLITS:
        carried = run_attention_back(begin, end, idx, hat, qkv, prob, att, datt, w_all, vec, carried)
    dqkv, _, _, keep_c, send_c = carried
    din = run_input_grad(view.shape, hat, rstd, dqkv, dx, w_all, vec)
    out = run_outputs(view.shape, image_count, act, middle, w_two, vec)
    mlp = reduce_large_grads(idx, keep_b, send_b, replicas)
    attention = reduce_grads(idx, keep_c, send_c, replicas)
    shape_of = lambda *arrays: [v.shape for v in arrays]
    g_out, g_bout, g_fc1, g_bfc1, g_fc2, g_bfc2, g_gtwo, g_stwo = run_unpack(
        unpack_mlp_kernel, idx, mlp,
        shape_of(w_out, b_out, w_fc1, b_fc1, w_fc2, b_fc2, gain_two, shift_two),
    )
    g_qkv, g_bqv, g_gone, g_sone = run_unpack(
        unpack_attention_kernel, idx, attention, shape_of(w_qkv, b_qv, gain_one, shift_one)
    )
    return (
        separated(out, images.shape), separated(din, images.shape),
        g_qkv, g_bqv, g_out, g_bout, g_fc1, g_bfc1, g_fc2, g_bfc2, g_gone, g_sone, g_gtwo, g_stwo,
    )


def step(replicas, *args):
    return local(replicas, *args)


def solution(mesh):
    split = P(None, ("group", "replica"), None, None)
    matrix, vector = P("group", None), P("group")
    return jax.shard_map(
        partial(step, mesh.shape["replica"]),
        mesh=mesh,
        in_specs=(split, P(None, ("group", "replica")), split)
        + (matrix, vector) * 4
        + (vector,) * 4,
        out_specs=(split, split) + (matrix, vector) * 4 + (vector,) * 4,
        check_vma=False,
    )
```

```python
from functools import partial

import jax
import jax.numpy as jnp
from jax import lax
from jax.experimental import pallas as pl
from jax.experimental.layout import Layout, with_layout_constraint
from jax.experimental.pallas import tpu as pltpu
from jax.sharding import PartitionSpec as P


HEADS = 6
ROWS = 208
KEYS = 256
F32 = jnp.float32
BF16 = jnp.bfloat16
NT = (((1,), (1,)), ((), ()))
TN = (((0,), (0,)), ((), ()))


def mm(a, b):
    return jnp.dot(a, b, preferred_element_type=F32)


def mm_nt(a, b):
    return lax.dot_general(a, b, NT, preferred_element_type=F32)


def mm_tn(a, b):
    return lax.dot_general(a, b, TN, preferred_element_type=F32)


def normalize(values):
    center = values - jnp.mean(values, axis=-1, keepdims=True)
    spread = jnp.mean(center * center, axis=-1, keepdims=True)
    rstd = lax.rsqrt(spread + 1e-06)
    return center * rstd, rstd


def norm_back(grad_normed, hat, rstd, gain):
    grad_hat = grad_normed * gain
    first = jnp.mean(grad_hat, axis=-1, keepdims=True)
    second = jnp.mean(grad_hat * hat, axis=-1, keepdims=True)
    return rstd * (grad_hat - first - hat * second)


def gelu_parts(pre, d_act):
    size = jnp.abs(pre)
    density = jnp.exp2(pre * (pre * -0.7213475204444817))
    t = 1.0 / (1.0 + 0.2316418882663604 * size)
    poly = t * (
        0.127414796
        + t * (-0.142248368 + t * (0.7107068705 + t * (-0.7265760135 + t * 0.5307027145)))
    )
    act = jnp.maximum(pre, 0.0) - size * (poly * density)
    edge = density * (poly - 0.3989422804014327 * size)
    slope = jnp.where(pre < 0.0, edge, 1.0 - edge)
    return act.astype(BF16), (d_act * slope).astype(BF16)


def read_image(ref, micro, slot, seq, target, top):
    tiles = target.shape[1] // 128
    for tile in range(tiles):
        start = micro * (seq * tiles * 2) + 2 * tile + slot
        target[top : top + seq, tile * 128 : tile * 128 + 128] = ref[pl.ds(start, seq, stride=2 * tiles), :]


def write_image(ref, micro, slot, seq, value):
    tiles = value.shape[1] // 128
    for tile in range(tiles):
        start = micro * (seq * tiles * 2) + 2 * tile + slot
        ref[pl.ds(start, seq, stride=2 * tiles), :] = value[:seq, tile * 128 : tile * 128 + 128]


def joined(first, second, row, size):
    return jnp.concatenate([first[row : row + 1, :size], second[row : row + 1, :size]], axis=1)


def ordered(idx_ref, mine, theirs):
    low = idx_ref[0] == 0
    mine, theirs = mine.astype(F32), theirs.astype(F32)
    return jnp.where(low, mine, theirs), jnp.where(low, theirs, mine)


def fetch(pairs, sem, first, step, steps):
    def copies(k, slot):
        return [
            pltpu.make_async_copy(source.at[pl.ds(2 * (first + k), 2)], target.at[slot], sem.at[n, slot])
            for n, (source, target) in enumerate(pairs)
        ]

    now = lax.rem(step, 2)

    @pl.when(step == 0)
    def _():
        for copy in copies(0, 0):
            copy.start()

    @pl.when(step + 1 < steps)
    def _():
        for copy in copies(step + 1, 1 - now):
            copy.start()

    for copy in copies(step, now):
        copy.wait()
    return [target.at[now] for _, target in pairs]


HBM_SPEC = pl.BlockSpec(memory_space=pltpu.HBM)


def in_hbm(*arrays):
    return [pltpu.with_memory_space_constraint(array, pltpu.HBM) for array in arrays]


def at(start, size):
    return pl.ds(pl.multiple_of(start, 16), size)


VMEM_SPEC = pl.BlockSpec(memory_space=pltpu.VMEM)


def pack_first_kernel(idx_ref, wq_ref, *refs):
    vectors, first_ref, small_ref = refs[:-2], refs[-2], refs[-1]
    part = wq_ref.shape[0]
    small_ref[...] = jnp.zeros_like(small_ref)
    for k, ref in enumerate(vectors):
        size = ref.shape[0]
        small_ref[k : k + 1, :size] = ref[...].reshape(1, size)
    first_ref[:part, :] = wq_ref[...]
    first_ref[part:, :] = jnp.zeros((16, first_ref.shape[1]), BF16)
    first_ref[part : part + 8, : small_ref.shape[1]] = small_ref[...]


def pack_second_kernel(idx_ref, wo_ref, w1_ref, w2_ref, second_ref):
    part, width = wo_ref.shape
    hidden = w1_ref.shape[1]
    second_ref[:, :width] = wo_ref[...]
    second_ref[:, width : width + hidden] = w1_ref[...]
    for k in range(hidden // width):
        second_ref[:, width + hidden + k * width : width + hidden + (k + 1) * width] = w2_ref[
            k * part : (k + 1) * part, :
        ]


def own_rows(rows, columns):
    return pl.BlockSpec((rows, columns), lambda i, idx: (idx[1], 0))


def run_pack_first(idx, w_qkv, vectors):
    half, wide = w_qkv.shape
    longest = max(v.shape[0] for v in vectors)
    shapes = [(half // 2 + 16, wide), (8, longest)]
    return pl.pallas_call(
        pack_first_kernel,
        grid_spec=pltpu.PrefetchScalarGridSpec(
            num_scalar_prefetch=1,
            grid=(1,),
            in_specs=[own_rows(half // 2, wide)] + [pl.BlockSpec(v.shape, lambda i, idx: (0,)) for v in vectors],
            out_specs=[pl.BlockSpec(s, lambda i, idx: (0, 0)) for s in shapes],
        ),
        out_shape=[jax.ShapeDtypeStruct(s, BF16) for s in shapes],
        name="pack_first",
    )(idx, w_qkv, *vectors)


def run_pack_second(idx, w_out, w_fc1, w_fc2):
    half, width = w_out.shape
    hidden = w_fc1.shape[1]
    part = half // 2
    shape = (part, width + 2 * hidden)
    return pl.pallas_call(
        pack_second_kernel,
        grid_spec=pltpu.PrefetchScalarGridSpec(
            num_scalar_prefetch=1,
            grid=(1,),
            in_specs=[own_rows(part, width), own_rows(part, hidden), own_rows(hidden // 4, width)],
            out_specs=pl.BlockSpec(shape, lambda i, idx: (0, 0)),
        ),
        out_shape=jax.ShapeDtypeStruct(shape, BF16),
        name="pack_second",
    )(idx, w_out, w_fc1, w_fc2)


def load_view(source, raw, view, sem):
    load = pltpu.make_async_copy(source, raw, sem)
    load.start()
    load.wait()
    view[...] = raw[...].astype(F32)


def prepare_images_kernel(x_hbm, low_ref, hat_ref, rstd_ref, raw, view, xs, sem):
    step = pl.program_id(0)
    width = xs.shape[1]
    seq = x_hbm.shape[0] * 128 // (width * 2 * pl.num_programs(0))

    @pl.when(step == 0)
    def _():
        xs[...] = jnp.zeros_like(xs)
        load_view(x_hbm, raw, view, sem)

    for slot in range(2):
        read_image(view, step, slot, seq, xs, slot * ROWS)
    value = xs[...]
    hat, rstd = normalize(value)
    low_ref[...] = value.astype(BF16).reshape(2, ROWS, width)
    hat_ref[...] = hat.reshape(2, ROWS, width)
    rstd_ref[...] = jnp.broadcast_to(rstd, (2 * ROWS, 128)).reshape(2, ROWS, 128)


def prepare_cotangent_kernel(x_hbm, low_ref, raw, view, xs, sem):
    step = pl.program_id(0)
    width = xs.shape[1]
    seq = x_hbm.shape[0] * 128 // (width * 2 * pl.num_programs(0))

    @pl.when(step == 0)
    def _():
        xs[...] = jnp.zeros_like(xs)
        load_view(x_hbm, raw, view, sem)

    for slot in range(2):
        read_image(view, step, slot, seq, xs, slot * ROWS)
    low_ref[...] = xs[...].astype(BF16).reshape(2, ROWS, width)


def run_prepare(kernel, view, count, width, outs):
    return pl.pallas_call(
        kernel,
        grid=(count // 2,),
        in_specs=[HBM_SPEC],
        out_specs=[per_pair(ROWS, columns) for columns, _ in outs],
        out_shape=[pltpu.HBM((count, ROWS, columns), dtype) for columns, dtype in outs],
        scratch_shapes=[
            pltpu.VMEM(view.shape, BF16), pltpu.VMEM(view.shape, F32), pltpu.VMEM((2 * ROWS, width), F32),
            pltpu.SemaphoreType.DMA,
        ],
        compiler_params=pltpu.CompilerParams(vmem_limit_bytes=14 << 20),
        cost_estimate=pl.CostEstimate(flops=1 << 28, bytes_accessed=8 << 20, transcendentals=0),
    )(*in_hbm(view))


def attention_kernel(
    seq, idx_ref, hat_hbm, w_ref, near_ref, far_ref, small_ref,
    qkv_ref, prob_ref, att_ref, whole_ref, vec_ref, b1_ref,
    kv, bias, scores, hat_buf, hat_sem,
):
    step = pl.program_id(0)
    half, wide = w_ref.shape
    width = wide // 3
    part = half // 2
    pairs = width // 128
    (hat_ref,) = fetch([(hat_hbm, hat_buf)], hat_sem, 0, step, pl.num_programs(0))

    @pl.when(step == 0)
    def _():
        kv[...] = jnp.zeros_like(kv)
        group, core = idx_ref[0], idx_ref[1]
        first, second = ordered(idx_ref, small_ref[...], near_ref[part : part + 8, : small_ref.shape[1]])
        for k, row in enumerate((4, 5, 1, 3, 6, 7)):
            vec_ref[k : k + 1, :] = joined(first, second, row, half)
        b1_ref[0:1, :] = jnp.concatenate([first[2:3, :], second[2:3, :]], axis=1)
        other = (1 - group) * half
        for pair in range(pairs):
            for kind in range(3):
                source = slice(kind * width + pair * 128, kind * width + pair * 128 + 128)
                target = slice((3 * pair + kind) * 128, (3 * pair + kind) * 128 + 128)
                whole_ref[at(group * half, half), target] = w_ref[:, source]
                whole_ref[at(other + core * part, part), target] = near_ref[:part, source]
                whole_ref[at(other + (1 - core) * part, part), target] = far_ref[:part, source]
                lanes = slice(pair * 128, pair * 128 + 128)
                piece = (first[0:1, lanes], jnp.zeros((1, 128), F32), second[0:1, lanes])[kind]
                bias[0:1, target] = piece

    hat = hat_ref[...].reshape(2 * ROWS, width)
    normed = (hat * vec_ref[0:1, :] + vec_ref[1:2, :]).astype(BF16)
    low_half = lax.broadcasted_iota(jnp.int32, (1, 128), 1) < 64
    column = lax.broadcasted_iota(jnp.int32, (1, KEYS), 1)

    def project(pair):
        lanes = slice(pair * 384, pair * 384 + 384)
        qkv = (mm(normed, whole_ref[:, lanes]) + bias[0:1, lanes]).astype(BF16)
        for slot in range(2):
            part = qkv[slot * ROWS : slot * ROWS + ROWS]
            qkv_ref[slot, :, lanes] = part
            kv[slot, :ROWS, pair * 256 : pair * 256 + 256] = part[:, 128:]

    def masked(values, head):
        mask = low_half if head % 2 == 0 else jnp.logical_not(low_half)
        return jnp.where(mask, values, jnp.zeros_like(values))

    def first_part(slot, head):
        pair = head // 2
        query = qkv_ref[slot, :, pair * 384 : pair * 384 + 128] * jnp.array(0.125, BF16)
        scores[slot, head % 2] = mm_nt(query, masked(kv[slot, :, pair * 256 : pair * 256 + 128], head))

    def second_part(slot, head):
        for r in range(0, ROWS, 16):
            value = jnp.where(column < seq, scores[slot, head % 2, r : r + 16], -1e30)
            top = jnp.max(value, axis=-1, keepdims=True)
            grown = jnp.exp(value - top)
            prob_ref[slot, head, r : r + 16] = (
                grown * (1.0 / jnp.sum(grown, axis=-1, keepdims=True))
            ).astype(BF16)

    def third_part(slot, head):
        pair = head // 2
        values = kv[slot, :, pair * 256 + 128 : pair * 256 + 256]
        if head % 2 == 1:
            total = mm(prob_ref[slot, head - 1], masked(values, 0)) + mm(prob_ref[slot, head], masked(values, 1))
            att_ref[slot, :, pair * 128 : pair * 128 + 128] = total.astype(BF16)

    project(0)
    for k in range(HEADS + 2):
        for slot in range(2):
            if k < HEADS:
                first_part(slot, k)
            if k >= 2:
                third_part(slot, k - 2)
            if slot == 0 and k % 2 == 0 and k // 2 + 1 < pairs:
                project(k // 2 + 1)
            if 1 <= k <= HEADS:
                second_part(slot, k - 1)


def mlp_kernel(
    idx_ref, count_ref, x_hbm, cot_hbm, att_hbm, wo_ref, w1_ref, w2_ref, near_ref, far_ref, vec, b1,
    act_ref, middle_ref, dx_ref, datt_ref, w2, keep_ref, send_ref,
    acts, dpres, pres, dacts, wo, w1, wot, w1t, w2t, dn_half,
    gw1, gw2, gwo, gsmall, x_buf, cot_buf, att_buf, sem,
):
    step = pl.program_id(0)
    last = pl.num_programs(0) - 1
    half, width = wo_ref.shape
    hidden = w1_ref.shape[1]
    part = half // 2
    rows = 2 * ROWS
    core = idx_ref[1]

    @pl.when(step == 0)
    def _():
        for ref in (gw1, gw2, gwo, gsmall):
            ref[...] = jnp.zeros_like(ref)
        group = idx_ref[0]
        wo[at(group * half, half), :] = wo_ref[...]
        w1[at(group * half, half), :] = w1_ref[...]
        w2[at(group * (hidden // 2), hidden // 2), :] = w2_ref[...]
        other = (1 - group) * half
        for ref, which in ((near_ref, core), (far_ref, 1 - core)):
            wo[at(other + which * part, part), :] = ref[:, :width]
            w1[at(other + which * part, part), :] = ref[:, width : width + hidden]
            base = (1 - group) * (hidden // 2) + which * (hidden // 4)
            for k in range(hidden // width):
                w2[at(base + k * part, part), :] = ref[:, width + hidden + k * width : width + hidden + (k + 1) * width]
        wot[...] = wo[...].T
        w1t[...] = w1[...].T
        w2t[...] = w2[...].T

    x_ref, cot_ref, att_ref = fetch(
        [(x_hbm, x_buf), (cot_hbm, cot_buf), (att_hbm, att_buf)], sem, 0, step, last + 1
    )
    second_valid = (1 < count_ref[step, 0]).astype(F32)
    row = lax.broadcasted_iota(jnp.int32, (rows, 1), 0)
    valid = jnp.where(row < ROWS, 1.0, second_valid)
    att = att_ref[...].reshape(rows, width)
    middle = x_ref[...].reshape(rows, width).astype(F32) + mm(att, wo[...]) + vec[2:3, :]
    hat, rstd = normalize(middle)
    gain = vec[4:5, :]
    normed = (hat * gain + vec[5:6, :]).astype(BF16)
    d_out = cot_ref[...].reshape(rows, width).astype(F32) * valid
    d_mlp = d_out.astype(BF16)
    normed_t = jnp.concatenate([normed.T, jnp.ones((16, rows), BF16)], axis=0)
    d_mlp_t = d_mlp.T
    chunks = hidden // 256
    middle_of = hidden // 2

    def first_part(c):
        cols = slice(c * 256, c * 256 + 256)
        pres[c % 2] = mm(normed, w1[:, cols])
        dacts[c % 2] = mm(d_mlp, w2t[:, cols])

    def second_part(c):
        cols = slice(c * 256, c * 256 + 256)
        bias = b1[0:1, cols]
        for r in range(0, rows, 32):
            act, d_pre = gelu_parts(pres[c % 2, r : r + 32] + bias, dacts[c % 2, r : r + 32])
            acts[r : r + 32, cols] = act
            act_ref[r // ROWS, r % ROWS : r % ROWS + 16, cols] = act[:16]
            act_ref[(r + 16) // ROWS, (r + 16) % ROWS : (r + 16) % ROWS + 16, cols] = act[16:]
            dpres[r : r + 32, cols] = d_pre

    def third_part(c):
        cols = slice(c * 256, c * 256 + 256)
        gw1[:, cols] += mm(normed_t, dpres[:, cols])
        gw2[:, cols] += mm(d_mlp_t, acts[:, cols])

    for k in range(chunks + 2):
        if k < chunks:
            first_part(k)
        if k >= 2:
            third_part(k - 2)
        if k == chunks // 2 + 1:
            dn_half[...] = mm(dpres[:, :middle_of], w1t[:middle_of, :])
        if 1 <= k <= chunks:
            second_part(k - 1)

    middle_ref[...] = middle.reshape(2, ROWS, width)
    d_normed = dn_half[...] + mm(dpres[:, middle_of:], w1t[middle_of:, :])
    dx = d_out + norm_back(d_normed, hat, rstd, gain)
    d_attn = dx.astype(BF16)
    dx_ref[...] = d_attn.reshape(2, ROWS, width)
    datt_ref[...] = mm(d_attn, wot[...]).astype(BF16).reshape(2, ROWS, width)
    gwo[...] += mm_tn(att, d_attn)

    def fold(values):
        return jnp.sum(values.reshape(rows // 8, 8, width), axis=0)

    gsmall[0] += fold(d_out)
    gsmall[1] += fold(d_attn.astype(F32))
    gsmall[2] += fold(d_normed * hat)
    gsmall[3] += fold(d_normed)

    @pl.when(step == last)
    def _():
        quarter = half // 4
        wide = hidden // 8
        gw2_t = gw2[...].T
        small_rows = [jnp.sum(gsmall[k], axis=0, keepdims=True) for k in range(4)]

        def emit(group, quad, ref, side):
            base = group * half + quad * quarter
            top = 0
            for col in range(hidden // width):
                ref[group, side, top : top + quarter, :] = gw1[
                    base : base + quarter, col * width : (col + 1) * width
                ].astype(BF16)
                top += quarter
            start = group * (hidden // 2) + quad * wide
            ref[group, side, top : top + wide, :] = gw2_t[start : start + wide].astype(BF16)
            top += wide
            ref[group, side, top : top + quarter, :] = gwo[base : base + quarter, :].astype(BF16)
            top += quarter
            if quad < 2:
                start = group * (hidden // 2) + quad * width
                value = gw1[width : width + 1, start : start + width]
            else:
                own = slice(group * half, group * half + half)
                value = jnp.concatenate(
                    [small_rows[2 * quad - 4][:, own], small_rows[2 * quad - 3][:, own]], axis=1
                )
            ref[group, side, top : top + 16, :] = jnp.broadcast_to(value, (16, width)).astype(BF16)

        split_quads(core, emit, keep_ref, send_ref)


def split_quads(core, emit, keep_ref, send_ref):
    for mine in range(2):

        @pl.when(core == mine)
        def _():
            for group in range(2):
                for side in range(2):
                    emit(group, 2 * mine + side, keep_ref, side)
                    emit(group, 2 * (1 - mine) + side, send_ref, side)


def attention_back_kernel(
    first_micro, last, idx_ref, hat_hbm, qkv_hbm, prob_hbm, att_hbm, datt_hbm, w_ref, vec_ref, *refs
):
    carried = 0 if first_micro == 0 else 3
    dqkv_ref, total_ref, sums_ref = refs[carried : carried + 3]
    kv, hat_t, d_probs, d_scores = refs[-10:-6]
    buffers, sem = refs[-6:-1], refs[-1]
    step = pl.program_id(0)
    width = w_ref.shape[0]
    pairs = width // 128
    sources = (hat_hbm, datt_hbm, qkv_hbm, att_hbm, prob_hbm)
    hat_ref, datt_ref, qkv_ref, att_ref, prob_ref = fetch(
        list(zip(sources, buffers)), sem, first_micro, step, pl.num_programs(0)
    )

    @pl.when(step == 0)
    def _():
        kv[...] = jnp.zeros_like(kv)
        if not carried:
            total_ref[...] = jnp.zeros_like(total_ref)
            sums_ref[...] = jnp.zeros_like(sums_ref)

    hat_t[...] = hat_ref[...].reshape(2 * ROWS, width).astype(BF16).T
    for pair in range(pairs):
        kv[:, :ROWS, pair * 256 : pair * 256 + 256] = qkv_ref[:, :, pair * 384 + 128 : pair * 384 + 384]
    low_half = lax.broadcasted_iota(jnp.int32, (1, 128), 1) < 64

    def masked(values, head):
        mask = low_half if head % 2 == 0 else jnp.logical_not(low_half)
        return jnp.where(mask, values, jnp.zeros_like(values))

    def lanes(head):
        return slice(head // 2 * 128, head // 2 * 128 + 128)

    def first_part(slot, head):
        pair = head // 2
        d_probs[slot, head % 2] = mm_nt(
            datt_ref[slot, :, lanes(head)], masked(kv[slot, :, pair * 256 + 128 : pair * 256 + 256], head)
        )

    def second_part(slot, head):
        for r in range(0, ROWS, 16):
            rows = slice(r, r + 16)
            product = datt_ref[slot, rows, lanes(head)].astype(F32) * att_ref[slot, rows, lanes(head)].astype(F32)
            delta = jnp.sum(masked(product, head), axis=-1, keepdims=True)
            d_scores[slot, head % 4, rows] = (
                prob_ref[slot, head, rows].astype(F32) * (d_probs[slot, head % 2, rows] - delta)
            ).astype(BF16)

    def third_part(slot, pair):
        query = qkv_ref[slot, :, pair * 384 : pair * 384 + 128] * jnp.array(0.125, BF16)
        keys = kv[slot, :, pair * 256 : pair * 256 + 128] * jnp.array(0.125, BF16)
        d_att = datt_ref[slot, :, pair * 128 : pair * 128 + 128]
        dq = dk = dv = 0.0
        for head in (2 * pair, 2 * pair + 1):
            d_score = d_scores[slot, head % 4]
            dv = dv + mm_tn(prob_ref[slot, head], masked(d_att, head))
            dk = dk + mm_tn(d_score, masked(query, head))
            dq = dq + mm(d_score, masked(keys, head))
        top = pair * 384
        dqkv_ref[slot, :, top : top + 128] = dq.astype(BF16)
        dqkv_ref[slot, :, top + 128 : top + 256] = dk[:ROWS].astype(BF16)
        dqkv_ref[slot, :, top + 256 : top + 384] = dv[:ROWS].astype(BF16)

    def fourth_part(pair):
        columns = slice(pair * 384, pair * 384 + 384)
        joined_back = dqkv_ref[:, :, columns].reshape(2 * ROWS, 384)
        total_ref[:, columns] += mm(hat_t[...], joined_back)
        sums_ref[:, columns] += jnp.sum(joined_back.astype(F32).reshape(ROWS // 4, 8, 384), axis=0)

    for k in range(HEADS + 3):
        for slot in range(2):
            if k < HEADS:
                first_part(slot, k)
            if k >= 3 and k % 2 == 1:
                third_part(slot, k // 2 - 1)
            if slot == 0 and k >= 4 and k % 2 == 0:
                fourth_part(k // 2 - 2)
            if 1 <= k <= HEADS:
                second_part(slot, k - 1)

    if last:
        keep_ref, send_ref = refs[carried + 3 : carried + 5]

        @pl.when(step == pl.num_programs(0) - 1)
        def _():
            half = width // 2
            quarter = half // 4
            total_sums = jnp.sum(sums_ref[...], axis=0, keepdims=True)
            weights = w_ref[...].astype(F32)
            d_gain = jnp.sum((weights * total_ref[...]).reshape(width, 3 * width), axis=1, keepdims=True)
            d_shift = jnp.sum(weights * total_sums, axis=1, keepdims=True)
            columns = jnp.concatenate([vec_ref[...], jnp.zeros((120, width), F32)], axis=0).T
            gain, shift = columns[:, 0:1], columns[:, 1:2]
            total_ref[...] = total_ref[...] * gain + shift * total_sums
            lane = lax.broadcasted_iota(jnp.int32, (1, 128), 1)
            both = jnp.where(lane == 0, d_gain, jnp.where(lane == 1, d_shift, 0.0)).T

            def emit(group, quad, ref, side):
                base = group * half + quad * quarter
                for kind in range(3):
                    for pair in range(pairs):
                        source = slice((3 * pair + kind) * 128, (3 * pair + kind) * 128 + 128)
                        ref[group, side, kind * quarter : (kind + 1) * quarter, pair * 128 : pair * 128 + 128] = (
                            total_ref[base : base + quarter, source].astype(BF16)
                        )
                if quad == 0:
                    kind = 2 * group
                    value = jnp.concatenate(
                        [total_sums[:, (3 * p + kind) * 128 : (3 * p + kind) * 128 + 128] for p in range(pairs)], axis=1
                    )
                else:
                    own = slice(group * half, group * half + half)
                    value = jnp.concatenate([both[0:1, own], both[1:2, own]], axis=1)
                ref[group, side, 3 * quarter : 3 * quarter + 16, :] = jnp.broadcast_to(value, (16, width)).astype(BF16)

            split_quads(idx_ref[1], emit, keep_ref, send_ref)


def input_grad_kernel(hat_hbm, rstd_hbm, dqkv_hbm, dx_hbm, w_ref, vec_ref, din_ref, outs, wt, *refs):
    step = pl.program_id(0)
    width = w_ref.shape[0]
    micros = pl.num_programs(0)
    seq = din_ref.shape[0] * 128 // (width * 2 * micros)
    rows = 2 * ROWS
    sources = (hat_hbm, rstd_hbm, dqkv_hbm, dx_hbm)
    hat_ref, rstd_ref, dqkv_ref, dx_ref = fetch(list(zip(sources, refs[:-1])), refs[-1], 0, step, micros)

    @pl.when(step == 0)
    def _():
        wt[...] = w_ref[...].T

    d_normed = mm(dqkv_ref[...].reshape(rows, 3 * width), wt[...])
    hat = hat_ref[...].reshape(rows, width)
    rstd = rstd_ref[...].reshape(rows, 128)[:, 0:1]
    d_in = dx_ref[...].reshape(rows, width).astype(F32) + norm_back(d_normed, hat, rstd, vec_ref[0:1, :])
    for slot in range(2):
        write_image(outs, step, slot, seq, d_in[slot * ROWS : slot * ROWS + ROWS])

    @pl.when(step == micros - 1)
    def _():
        din_ref[...] = outs[...].astype(BF16)


def outputs_kernel(count_ref, act_hbm, middle_hbm, w2_ref, vec_ref, out_ref, outs, act_buf, middle_buf, sem):
    step = pl.program_id(0)
    hidden, width = w2_ref.shape
    micros = pl.num_programs(0)
    seq = out_ref.shape[0] * 128 // (width * 2 * micros)
    rows = 2 * ROWS
    act_ref, middle_ref = fetch([(act_hbm, act_buf), (middle_hbm, middle_buf)], sem, 0, step, micros)
    row = lax.broadcasted_iota(jnp.int32, (rows, 1), 0)
    valid = jnp.where(row < ROWS, 1.0, (1 < count_ref[step, 0]).astype(F32))
    mlp = mm(act_ref[...].reshape(rows, hidden), w2_ref[...]) + vec_ref[3:4, :]
    result = (middle_ref[...].reshape(rows, width) + mlp) * valid
    for slot in range(2):
        write_image(outs, step, slot, seq, result[slot * ROWS : slot * ROWS + ROWS])

    @pl.when(step == micros - 1)
    def _():
        out_ref[...] = outs[...].astype(BF16)


def per_pair(*shape):
    return pl.BlockSpec((2, *shape), lambda i: (i,) + (0,) * len(shape))


SMEM_SPEC = pl.BlockSpec(memory_space=pltpu.SMEM)


def run_attention(seq, idx, hat, w_qkv, near, far, small):
    count = hat.shape[0]
    width = w_qkv.shape[1] // 3
    return pl.pallas_call(
        partial(attention_kernel, seq),
        grid=(count // 2,),
        in_specs=[SMEM_SPEC, HBM_SPEC] + [VMEM_SPEC] * 4,
        out_specs=[
            per_pair(ROWS, 3 * width), per_pair(HEADS, ROWS, KEYS), per_pair(ROWS, width),
            VMEM_SPEC, VMEM_SPEC, VMEM_SPEC,
        ],
        out_shape=[
            pltpu.HBM((count, ROWS, 3 * width), BF16),
            pltpu.HBM((count, HEADS, ROWS, KEYS), BF16),
            pltpu.HBM((count, ROWS, width), BF16),
            jax.ShapeDtypeStruct((width, 3 * width), BF16),
            jax.ShapeDtypeStruct((8, width), F32),
            jax.ShapeDtypeStruct((8, 2 * small.shape[1]), F32),
        ],
        scratch_shapes=[
            pltpu.VMEM((2, KEYS, 2 * width), BF16),
            pltpu.VMEM((8, 3 * width), F32),
            pltpu.VMEM((2, 2, ROWS, KEYS), F32),
            pltpu.VMEM((2, 2, ROWS, width), F32),
            pltpu.SemaphoreType.DMA((1, 2)),
        ],
        compiler_params=pltpu.CompilerParams(vmem_limit_bytes=22 << 20),
        cost_estimate=pl.CostEstimate(flops=5 << 30, bytes_accessed=20 << 20, transcendentals=0),
        name="attention_fwd",
    )(idx, *in_hbm(hat), w_qkv, near, far, small)


def run_mlp(idx, counts, images, cot, att, wo, w1, w2, near, far, vec, b1):
    width = wo.shape[1]
    hidden = w1.shape[1]
    micro = counts.shape[0]
    rows = 2 * ROWS
    packed = width // 8 * (hidden // width) + hidden // 8 + width // 8 + 16
    two = pl.BlockSpec((2, ROWS, width), lambda i: (i, 0, 0))
    return pl.pallas_call(
        mlp_kernel,
        grid=(micro,),
        in_specs=[SMEM_SPEC, SMEM_SPEC, HBM_SPEC, HBM_SPEC, HBM_SPEC] + [VMEM_SPEC] * 7,
        out_specs=[per_pair(ROWS, hidden), two, two, two, VMEM_SPEC, VMEM_SPEC, VMEM_SPEC],
        out_shape=[
            pltpu.HBM((2 * micro, ROWS, hidden), BF16),
            pltpu.HBM(att.shape, F32),
            pltpu.HBM(att.shape, BF16),
            pltpu.HBM(att.shape, BF16),
            jax.ShapeDtypeStruct((hidden, width), BF16),
            jax.ShapeDtypeStruct((2, 2, packed, width), BF16),
            jax.ShapeDtypeStruct((2, 2, packed, width), BF16),
        ],
        scratch_shapes=[
            pltpu.VMEM((rows, hidden), BF16),
            pltpu.VMEM((rows, hidden), BF16),
            pltpu.VMEM((2, rows, 256), F32),
            pltpu.VMEM((2, rows, 256), F32),
            pltpu.VMEM((width, width), BF16),
            pltpu.VMEM((width, hidden), BF16),
            pltpu.VMEM((width, width), BF16),
            pltpu.VMEM((hidden, width), BF16),
            pltpu.VMEM((width, hidden), BF16),
            pltpu.VMEM((rows, width), F32),
            pltpu.VMEM((width + 16, hidden), F32),
            pltpu.VMEM((width, hidden), F32),
            pltpu.VMEM((width, width), F32),
            pltpu.VMEM((4, 8, width), F32),
            pltpu.VMEM((2, 2, ROWS, width), BF16),
            pltpu.VMEM((2, 2, ROWS, width), BF16),
            pltpu.VMEM((2, 2, ROWS, width), BF16),
            pltpu.SemaphoreType.DMA((3, 2)),
        ],
        compiler_params=pltpu.CompilerParams(vmem_limit_bytes=40 << 20),
        cost_estimate=pl.CostEstimate(flops=12 << 30, bytes_accessed=20 << 20, transcendentals=0),
        name="mlp_fwd_bwd",
    )(idx, counts, *in_hbm(images, cot, att), wo, w1, w2, near, far, vec, b1)


def run_attention_back(begin, end, idx, hat, qkv, prob, att, datt, w_qkv, vec, carried):
    count = qkv.shape[0]
    width = w_qkv.shape[0]
    packed = width // 8 * 3 + 16
    last = 2 * end == count
    block = pl.BlockSpec((2, ROWS, 3 * width), lambda i: (i + begin, 0, 0))
    two = lambda *shape: pltpu.VMEM((2, 2, *shape), BF16)
    return pl.pallas_call(
        partial(attention_back_kernel, begin, last),
        grid=(end - begin,),
        in_specs=[SMEM_SPEC] + [HBM_SPEC] * 5 + [VMEM_SPEC] * 2
        + ([HBM_SPEC, VMEM_SPEC, VMEM_SPEC] if carried else []),
        out_specs=[block, VMEM_SPEC, VMEM_SPEC] + ([VMEM_SPEC] * 2 if last else []),
        out_shape=[
            pltpu.HBM((count, ROWS, 3 * width), BF16),
            jax.ShapeDtypeStruct((width, 3 * width), F32),
            jax.ShapeDtypeStruct((8, 3 * width), F32),
        ]
        + [jax.ShapeDtypeStruct((2, 2, packed, width), BF16)] * (2 if last else 0),
        scratch_shapes=[
            pltpu.VMEM((2, KEYS, 2 * width), BF16),
            pltpu.VMEM((width, 2 * ROWS), BF16),
            pltpu.VMEM((2, 2, ROWS, KEYS), F32),
            pltpu.VMEM((2, 4, ROWS, KEYS), BF16),
            pltpu.VMEM((2, 2, ROWS, width), F32),
            two(ROWS, width), two(ROWS, 3 * width), two(ROWS, width), two(HEADS, ROWS, KEYS),
            pltpu.SemaphoreType.DMA((5, 2)),
        ],
        input_output_aliases={8: 0, 9: 1, 10: 2} if carried else {},
        compiler_params=pltpu.CompilerParams(vmem_limit_bytes=18 << 20),
        cost_estimate=pl.CostEstimate(flops=(end - begin) << 31, bytes_accessed=20 << 20, transcendentals=0),
    )(idx, *in_hbm(hat, qkv, prob, att, datt), w_qkv, vec, *in_hbm(*carried[:1]), *carried[1:])


def run_input_grad(view_shape, hat, rstd, dqkv, dx, w_qkv, vec):
    count = dqkv.shape[0]
    width = w_qkv.shape[0]
    two = lambda dtype, *shape: pltpu.VMEM((2, 2, *shape), dtype)
    return pl.pallas_call(
        input_grad_kernel,
        grid=(count // 2,),
        in_specs=[HBM_SPEC] * 4 + [VMEM_SPEC] * 2,
        out_specs=VMEM_SPEC,
        out_shape=jax.ShapeDtypeStruct(view_shape, BF16),
        scratch_shapes=[
            pltpu.VMEM(view_shape, F32),
            pltpu.VMEM((3 * width, width), BF16),
            two(F32, ROWS, width), two(F32, ROWS, 128), two(BF16, ROWS, 3 * width), two(BF16, ROWS, width),
            pltpu.SemaphoreType.DMA((4, 2)),
        ],
        compiler_params=pltpu.CompilerParams(vmem_limit_bytes=14 << 20),
        cost_estimate=pl.CostEstimate(flops=2 << 30, bytes_accessed=20 << 20, transcendentals=0),
        name="input_grad",
    )(*in_hbm(hat, rstd, dqkv, dx), w_qkv, vec)


def run_outputs(view_shape, counts, act, middle, w2, vec):
    count, _, hidden = act.shape
    width = w2.shape[1]
    return pl.pallas_call(
        outputs_kernel,
        grid=(count // 2,),
        in_specs=[SMEM_SPEC] + [HBM_SPEC] * 2 + [VMEM_SPEC] * 2,
        out_specs=VMEM_SPEC,
        out_shape=jax.ShapeDtypeStruct(view_shape, BF16),
        scratch_shapes=[
            pltpu.VMEM(view_shape, F32),
            pltpu.VMEM((2, 2, ROWS, hidden), BF16), pltpu.VMEM((2, 2, ROWS, width), F32),
            pltpu.SemaphoreType.DMA((2, 2)),
        ],
        compiler_params=pltpu.CompilerParams(vmem_limit_bytes=14 << 20),
        cost_estimate=pl.CostEstimate(flops=2 << 30, bytes_accessed=20 << 20, transcendentals=0),
        name="layer_outputs",
    )(counts, *in_hbm(act, middle), w2, vec)


def merge_kernel(which, idx_ref, a_ref, b_ref, own_ref, other_ref):
    mine = idx_ref[which]
    own_ref[...] = a_ref[mine] + b_ref[mine]
    other_ref[...] = a_ref[1 - mine] + b_ref[1 - mine]


def merge(idx, which, a, b):
    return pl.pallas_call(
        partial(merge_kernel, which),
        in_specs=[SMEM_SPEC, VMEM_SPEC, VMEM_SPEC],
        out_specs=[VMEM_SPEC, VMEM_SPEC],
        out_shape=[jax.ShapeDtypeStruct(a.shape[1:], BF16)] * 2,
        compiler_params=pltpu.CompilerParams(vmem_limit_bytes=4 << 20),
    )(idx, a, b)


def flip(value, axis, size, bit):
    return lax.ppermute(value, axis, [(i, i ^ bit) for i in range(size)])


def exchange(own, replicas, bit):
    while bit < replicas:
        got = flip(own, "replica", replicas, bit)
        own = own + got
        bit *= 2
    return own


def reduce_grads(idx, keep, send, replicas):
    own, other = merge(idx, 0, keep, flip(send, "replica", replicas, 1))
    own, other = merge(idx, 2, own, flip(other, "group", 2, 1))
    got = flip(other, "replica", replicas, 2)
    own = own + got
    own = exchange(own, replicas, 4)
    side = flip(own, "replica", replicas, 2)
    far_own = flip(own, "replica", replicas, 1)
    return own, side, far_own, flip(side, "replica", replicas, 1)


def reduce_large_grads(idx, keep, send, replicas):
    own, other = merge(idx, 0, keep, flip(send, "replica", replicas, 1))
    own, other = merge(idx, 2, own, flip(other, "group", 2, 1))
    halves = (2, own.shape[0] // 2, own.shape[1])
    got = flip(other, "replica", replicas, 2)
    own, other = merge(idx, 3, own.reshape(halves), got.reshape(halves))
    got = flip(other, "replica", replicas, 4)
    own = own + got
    own = exchange(own, replicas, 8)
    next_own = flip(own, "replica", replicas, 4)
    side = flip(own, "replica", replicas, 2)
    next_side = flip(next_own, "replica", replicas, 2)
    parts = (own, next_own, side, next_side)
    far = [flip(part, "replica", replicas, 1) for part in parts]
    return (*parts, *far)


def places(idx_ref):
    core, side = idx_ref[1], idx_ref[2]
    return 2 * core + side, 2 * core + 1 - side, 2 * (1 - core) + side, 2 * (1 - core) + 1 - side


def unpack_mlp_kernel(idx_ref, *refs):
    ins, outs, mlp = refs[:8], refs[8:16], refs[16]
    low = idx_ref[3]
    lines = ins[0].shape[0]
    for k, place in enumerate(places(idx_ref)):
        mlp[place, at(low * lines, lines)] = ins[2 * k][...].astype(F32)
        mlp[place, at((1 - low) * lines, lines)] = ins[2 * k + 1][...].astype(F32)
    g_out, g_bout, g_fc1, g_bfc1, g_fc2, g_bfc2, g_gtwo, g_stwo = outs
    half, width = g_out.shape
    hidden = g_fc1.shape[1]
    quarter = half // 4
    wide = hidden // 8
    for quad in range(4):
        rows = slice(quad * quarter, (quad + 1) * quarter)
        top = 0
        for col in range(hidden // width):
            g_fc1[rows, col * width : (col + 1) * width] = mlp[quad, top : top + quarter]
            top += quarter
        g_fc2[quad * wide : (quad + 1) * wide] = mlp[quad, top : top + wide]
        top += wide
        g_out[rows] = mlp[quad, top : top + quarter]
        top += quarter
        value = mlp[quad, top : top + 1]
        if quad < 2:
            g_bfc1[quad * width : (quad + 1) * width] = value.reshape(width)
        elif quad == 2:
            g_bfc2[...] = value[:, :half].reshape(half)
            g_bout[...] = value[:, half:].reshape(half)
        else:
            g_gtwo[...] = value[:, :half].reshape(half)
            g_stwo[...] = value[:, half:].reshape(half)


def unpack_attention_kernel(idx_ref, *refs):
    ins, outs, att = refs[:4], refs[4:8], refs[8]
    for k, place in enumerate(places(idx_ref)):
        att[place] = ins[k][...].astype(F32)
    g_qkv, g_bqv, g_gone, g_sone = outs
    half = g_qkv.shape[0]
    width = 2 * half
    quarter = half // 4
    for quad in range(4):
        rows = slice(quad * quarter, (quad + 1) * quarter)
        for col in range(3):
            g_qkv[rows, col * width : (col + 1) * width] = att[quad, col * quarter : (col + 1) * quarter]
        value = att[quad, 3 * quarter : 3 * quarter + 1]
        if quad == 0:
            g_bqv[...] = value.reshape(width)
        elif quad == 1:
            g_gone[...] = value[:, :half].reshape(half)
            g_sone[...] = value[:, half:].reshape(half)


def run_unpack(kernel, idx, parts, shapes):
    return pl.pallas_call(
        kernel,
        in_specs=[SMEM_SPEC] + [VMEM_SPEC] * len(parts),
        out_specs=[VMEM_SPEC] * len(shapes),
        out_shape=[jax.ShapeDtypeStruct(s, F32) for s in shapes],
        scratch_shapes=[pltpu.VMEM((4, parts[0].shape[0] * len(parts) // 4, parts[0].shape[1]), F32)],
        compiler_params=pltpu.CompilerParams(vmem_limit_bytes=8 << 20),
    )(idx, *parts)


def interleaved(images):
    micro, slots, seq, width = images.shape
    blocks = images.reshape(micro, slots, seq, width // 128, 128)
    blocks = with_layout_constraint(blocks, Layout(major_to_minor=(0, 2, 3, 1, 4)))
    return blocks.transpose(0, 2, 3, 1, 4).reshape(-1, 128)


def separated(rows, shape):
    micro, slots, seq, width = shape
    blocks = rows.reshape(micro, seq, width // 128, slots, 128).transpose(0, 1, 3, 2, 4)
    return blocks.reshape(micro, seq, slots, width).transpose(0, 2, 1, 3)


SPLITS = ((0, 1), (1, 4))


def local(
    replicas,
    images, image_count, cotangent, w_qkv, b_qv, w_out, b_out, w_fc1, b_fc1, w_fc2, b_fc2,
    gain_one, shift_one, gain_two, shift_two,
):
    replica = lax.axis_index("replica")
    idx = jnp.stack([lax.axis_index("group"), replica & 1, (replica >> 1) & 1, (replica >> 2) & 1]).astype(jnp.int32)
    count = images.shape[0] * images.shape[1]
    width = images.shape[3]
    vectors = (b_qv, b_out, b_fc1, b_fc2, gain_one, shift_one, gain_two, shift_two)
    first, small = run_pack_first(idx, w_qkv, vectors)
    second = run_pack_second(idx, w_out, w_fc1, w_fc2)
    near_first = flip(first, "group", 2, 1)
    near_second = flip(second, "group", 2, 1)
    far_first = flip(near_first, "replica", replicas, 1)
    far_second = flip(near_second, "replica", replicas, 1)
    view = interleaved(images)
    image_rows, hat, rstd = run_prepare(
        prepare_images_kernel, view, count, width, ((width, BF16), (width, F32), (128, F32))
    )
    (cot_rows,) = run_prepare(prepare_cotangent_kernel, interleaved(cotangent), count, width, ((width, BF16),))
    qkv, prob, att, w_all, vec, b1 = run_attention(
        images.shape[2], idx, hat, w_qkv, near_first, far_first, small
    )
    act, middle, dx, datt, w_two, keep_b, send_b = run_mlp(
        idx, image_count, image_rows, cot_rows, att, w_out, w_fc1, w_fc2, near_second, far_second, vec, b1
    )
    carried = ()
    for begin, end in SPLITS:
        carried = run_attention_back(begin, end, idx, hat, qkv, prob, att, datt, w_all, vec, carried)
    dqkv, _, _, keep_c, send_c = carried
    din = run_input_grad(view.shape, hat, rstd, dqkv, dx, w_all, vec)
    out = run_outputs(view.shape, image_count, act, middle, w_two, vec)
    mlp = reduce_large_grads(idx, keep_b, send_b, replicas)
    attention = reduce_grads(idx, keep_c, send_c, replicas)
    shape_of = lambda *arrays: [v.shape for v in arrays]
    g_out, g_bout, g_fc1, g_bfc1, g_fc2, g_bfc2, g_gtwo, g_stwo = run_unpack(
        unpack_mlp_kernel, idx, mlp,
        shape_of(w_out, b_out, w_fc1, b_fc1, w_fc2, b_fc2, gain_two, shift_two),
    )
    g_qkv, g_bqv, g_gone, g_sone = run_unpack(
        unpack_attention_kernel, idx, attention, shape_of(w_qkv, b_qv, gain_one, shift_one)
    )
    return (
        separated(out, images.shape), separated(din, images.shape),
        g_qkv, g_bqv, g_out, g_bout, g_fc1, g_bfc1, g_fc2, g_bfc2, g_gone, g_sone, g_gtwo, g_stwo,
    )


def step(replicas, *args):
    return local(replicas, *args)


def solution(mesh):
    split = P(None, ("group", "replica"), None, None)
    matrix, vector = P("group", None), P("group")
    return jax.shard_map(
        partial(step, mesh.shape["replica"]),
        mesh=mesh,
        in_specs=(split, P(None, ("group", "replica")), split)
        + (matrix, vector) * 4
        + (vector,) * 4,
        out_specs=(split, split) + (matrix, vector) * 4 + (vector,) * 4,
        check_vma=False,
    )
```

```python
from functools import partial

import jax
import jax.numpy as jnp
from jax import lax
from jax.experimental import pallas as pl
from jax.experimental.layout import Layout, with_layout_constraint
from jax.experimental.pallas import tpu as pltpu
from jax.sharding import PartitionSpec as P


HEADS = 6
ROWS = 208
KEYS = 256
F32 = jnp.float32
BF16 = jnp.bfloat16
NT = (((1,), (1,)), ((), ()))
TN = (((0,), (0,)), ((), ()))


def mm(a, b):
    return jnp.dot(a, b, preferred_element_type=F32)


def mm_nt(a, b):
    return lax.dot_general(a, b, NT, preferred_element_type=F32)


def mm_tn(a, b):
    return lax.dot_general(a, b, TN, preferred_element_type=F32)


def normalize(values):
    center = values - jnp.mean(values, axis=-1, keepdims=True)
    spread = jnp.mean(center * center, axis=-1, keepdims=True)
    rstd = lax.rsqrt(spread + 1e-06)
    return center * rstd, rstd


def norm_back(grad_normed, hat, rstd, gain):
    grad_hat = grad_normed * gain
    first = jnp.mean(grad_hat, axis=-1, keepdims=True)
    second = jnp.mean(grad_hat * hat, axis=-1, keepdims=True)
    return rstd * (grad_hat - first - hat * second)


def gelu_parts(pre, d_act):
    size = jnp.abs(pre)
    density = jnp.exp2(pre * (pre * -0.7213475204444817))
    t = 1.0 / (1.0 + 0.2316418882663604 * size)
    poly = t * (
        0.127414796
        + t * (-0.142248368 + t * (0.7107068705 + t * (-0.7265760135 + t * 0.5307027145)))
    )
    act = jnp.maximum(pre, 0.0) - size * (poly * density)
    edge = density * (poly - 0.3989422804014327 * size)
    slope = jnp.where(pre < 0.0, edge, 1.0 - edge)
    return act.astype(BF16), (d_act * slope).astype(BF16)


def read_image(ref, micro, slot, seq, target, top):
    tiles = target.shape[1] // 128
    for tile in range(tiles):
        start = micro * (seq * tiles * 2) + 2 * tile + slot
        target[top : top + seq, tile * 128 : tile * 128 + 128] = ref[pl.ds(start, seq, stride=2 * tiles), :]


def write_image(ref, micro, slot, seq, value):
    tiles = value.shape[1] // 128
    for tile in range(tiles):
        start = micro * (seq * tiles * 2) + 2 * tile + slot
        ref[pl.ds(start, seq, stride=2 * tiles), :] = value[:seq, tile * 128 : tile * 128 + 128]


def joined(first, second, row, size):
    return jnp.concatenate([first[row : row + 1, :size], second[row : row + 1, :size]], axis=1)


def ordered(idx_ref, mine, theirs):
    low = idx_ref[0] == 0
    mine, theirs = mine.astype(F32), theirs.astype(F32)
    return jnp.where(low, mine, theirs), jnp.where(low, theirs, mine)


def fetch(pairs, sem, first, step, steps):
    def copies(k, slot):
        return [
            pltpu.make_async_copy(source.at[pl.ds(2 * (first + k), 2)], target.at[slot], sem.at[n, slot])
            for n, (source, target) in enumerate(pairs)
        ]

    now = lax.rem(step, 2)

    @pl.when(step == 0)
    def _():
        for copy in copies(0, 0):
            copy.start()

    @pl.when(step + 1 < steps)
    def _():
        for copy in copies(step + 1, 1 - now):
            copy.start()

    for copy in copies(step, now):
        copy.wait()
    return [target.at[now] for _, target in pairs]


HBM_SPEC = pl.BlockSpec(memory_space=pltpu.HBM)


def in_hbm(*arrays):
    return [pltpu.with_memory_space_constraint(array, pltpu.HBM) for array in arrays]


def at(start, size):
    return pl.ds(pl.multiple_of(start, 16), size)


VMEM_SPEC = pl.BlockSpec(memory_space=pltpu.VMEM)


def pack_first_kernel(idx_ref, wq_ref, *refs):
    vectors, first_ref, small_ref = refs[:-2], refs[-2], refs[-1]
    part = wq_ref.shape[0]
    small_ref[...] = jnp.zeros_like(small_ref)
    for k, ref in enumerate(vectors):
        size = ref.shape[0]
        small_ref[k : k + 1, :size] = ref[...].reshape(1, size)
    first_ref[:part, :] = wq_ref[...]
    first_ref[part:, :] = jnp.zeros((16, first_ref.shape[1]), BF16)
    first_ref[part : part + 8, : small_ref.shape[1]] = small_ref[...]


def pack_second_kernel(idx_ref, wo_ref, w1_ref, w2_ref, second_ref):
    part, width = wo_ref.shape
    hidden = w1_ref.shape[1]
    second_ref[:, :width] = wo_ref[...]
    second_ref[:, width : width + hidden] = w1_ref[...]
    for k in range(hidden // width):
        second_ref[:, width + hidden + k * width : width + hidden + (k + 1) * width] = w2_ref[
            k * part : (k + 1) * part, :
        ]


def own_rows(rows, columns):
    return pl.BlockSpec((rows, columns), lambda i, idx: (idx[1], 0))


def run_pack_first(idx, w_qkv, vectors):
    half, wide = w_qkv.shape
    longest = max(v.shape[0] for v in vectors)
    shapes = [(half // 2 + 16, wide), (8, longest)]
    return pl.pallas_call(
        pack_first_kernel,
        grid_spec=pltpu.PrefetchScalarGridSpec(
            num_scalar_prefetch=1,
            grid=(1,),
            in_specs=[own_rows(half // 2, wide)] + [pl.BlockSpec(v.shape, lambda i, idx: (0,)) for v in vectors],
            out_specs=[VMEM_SPEC] * 2,
        ),
        out_shape=[jax.ShapeDtypeStruct(s, BF16) for s in shapes],
        compiler_params=pltpu.CompilerParams(vmem_limit_bytes=8 << 20),
        name="pack_first",
    )(idx, *in_hbm(w_qkv, *vectors))


def run_pack_second(idx, w_out, w_fc1, w_fc2):
    half, width = w_out.shape
    hidden = w_fc1.shape[1]
    part = half // 2
    shape = (part, width + 2 * hidden)
    return pl.pallas_call(
        pack_second_kernel,
        grid_spec=pltpu.PrefetchScalarGridSpec(
            num_scalar_prefetch=1,
            grid=(1,),
            in_specs=[own_rows(part, width), own_rows(part, hidden), own_rows(hidden // 4, width)],
            out_specs=VMEM_SPEC,
        ),
        out_shape=jax.ShapeDtypeStruct(shape, BF16),
        compiler_params=pltpu.CompilerParams(vmem_limit_bytes=8 << 20),
        name="pack_second",
    )(idx, *in_hbm(w_out, w_fc1, w_fc2))


def load_view(source, raw, view, sem):
    load = pltpu.make_async_copy(source, raw, sem)
    load.start()
    load.wait()
    view[...] = raw[...].astype(F32)


def prepare_images_kernel(x_hbm, low_ref, hat_ref, rstd_ref, raw, view, xs, sem):
    step = pl.program_id(0)
    width = xs.shape[1]
    seq = x_hbm.shape[0] * 128 // (width * 2 * pl.num_programs(0))

    @pl.when(step == 0)
    def _():
        xs[...] = jnp.zeros_like(xs)
        load_view(x_hbm, raw, view, sem)

    for slot in range(2):
        read_image(view, step, slot, seq, xs, slot * ROWS)
    value = xs[...]
    hat, rstd = normalize(value)
    low_ref[...] = value.astype(BF16).reshape(2, ROWS, width)
    hat_ref[...] = hat.reshape(2, ROWS, width)
    rstd_ref[...] = jnp.broadcast_to(rstd, (2 * ROWS, 128)).reshape(2, ROWS, 128)


def prepare_cotangent_kernel(x_hbm, low_ref, raw, view, xs, sem):
    step = pl.program_id(0)
    width = xs.shape[1]
    seq = x_hbm.shape[0] * 128 // (width * 2 * pl.num_programs(0))

    @pl.when(step == 0)
    def _():
        xs[...] = jnp.zeros_like(xs)
        load_view(x_hbm, raw, view, sem)

    for slot in range(2):
        read_image(view, step, slot, seq, xs, slot * ROWS)
    low_ref[...] = xs[...].astype(BF16).reshape(2, ROWS, width)


def run_prepare(kernel, view, count, width, outs):
    return pl.pallas_call(
        kernel,
        grid=(count // 2,),
        in_specs=[HBM_SPEC],
        out_specs=[per_pair(ROWS, columns) for columns, _ in outs],
        out_shape=[pltpu.HBM((count, ROWS, columns), dtype) for columns, dtype in outs],
        scratch_shapes=[
            pltpu.VMEM(view.shape, BF16), pltpu.VMEM(view.shape, F32), pltpu.VMEM((2 * ROWS, width), F32),
            pltpu.SemaphoreType.DMA,
        ],
        compiler_params=pltpu.CompilerParams(vmem_limit_bytes=14 << 20),
        cost_estimate=pl.CostEstimate(flops=1 << 28, bytes_accessed=8 << 20, transcendentals=0),
    )(*in_hbm(view))


def attention_kernel(
    seq, idx_ref, hat_hbm, w_ref, near_ref, far_ref, small_ref,
    qkv_ref, prob_ref, att_ref, whole_ref, vec_ref, b1_ref,
    kv, bias, scores, hat_buf, hat_sem,
):
    step = pl.program_id(0)
    half, wide = w_ref.shape
    width = wide // 3
    part = half // 2
    pairs = width // 128
    (hat_ref,) = fetch([(hat_hbm, hat_buf)], hat_sem, 0, step, pl.num_programs(0))

    @pl.when(step == 0)
    def _():
        kv[...] = jnp.zeros_like(kv)
        group, core = idx_ref[0], idx_ref[1]
        first, second = ordered(idx_ref, small_ref[...], near_ref[part : part + 8, : small_ref.shape[1]])
        for k, row in enumerate((4, 5, 1, 3, 6, 7)):
            vec_ref[k : k + 1, :] = joined(first, second, row, half)
        b1_ref[0:1, :] = jnp.concatenate([first[2:3, :], second[2:3, :]], axis=1)
        other = (1 - group) * half
        for pair in range(pairs):
            for kind in range(3):
                source = slice(kind * width + pair * 128, kind * width + pair * 128 + 128)
                target = slice((3 * pair + kind) * 128, (3 * pair + kind) * 128 + 128)
                whole_ref[at(group * half, half), target] = w_ref[:, source]
                whole_ref[at(other + core * part, part), target] = near_ref[:part, source]
                whole_ref[at(other + (1 - core) * part, part), target] = far_ref[:part, source]
                lanes = slice(pair * 128, pair * 128 + 128)
                piece = (first[0:1, lanes], jnp.zeros((1, 128), F32), second[0:1, lanes])[kind]
                bias[0:1, target] = piece

    hat = hat_ref[...].reshape(2 * ROWS, width)
    normed = (hat * vec_ref[0:1, :] + vec_ref[1:2, :]).astype(BF16)
    low_half = lax.broadcasted_iota(jnp.int32, (1, 128), 1) < 64
    column = lax.broadcasted_iota(jnp.int32, (1, KEYS), 1)

    def project(pair):
        lanes = slice(pair * 384, pair * 384 + 384)
        qkv = (mm(normed, whole_ref[:, lanes]) + bias[0:1, lanes]).astype(BF16)
        for slot in range(2):
            part = qkv[slot * ROWS : slot * ROWS + ROWS]
            qkv_ref[slot, :, lanes] = part
            kv[slot, :ROWS, pair * 256 : pair * 256 + 256] = part[:, 128:]

    def masked(values, head):
        mask = low_half if head % 2 == 0 else jnp.logical_not(low_half)
        return jnp.where(mask, values, jnp.zeros_like(values))

    def first_part(slot, head):
        pair = head // 2
        query = qkv_ref[slot, :, pair * 384 : pair * 384 + 128] * jnp.array(0.125, BF16)
        scores[slot, head % 2] = mm_nt(query, masked(kv[slot, :, pair * 256 : pair * 256 + 128], head))

    def second_part(slot, head):
        for r in range(0, ROWS, 16):
            value = jnp.where(column < seq, scores[slot, head % 2, r : r + 16], -1e30)
            top = jnp.max(value, axis=-1, keepdims=True)
            grown = jnp.exp(value - top)
            prob_ref[slot, head, r : r + 16] = (
                grown * (1.0 / jnp.sum(grown, axis=-1, keepdims=True))
            ).astype(BF16)

    def third_part(slot, head):
        pair = head // 2
        values = kv[slot, :, pair * 256 + 128 : pair * 256 + 256]
        if head % 2 == 1:
            total = mm(prob_ref[slot, head - 1], masked(values, 0)) + mm(prob_ref[slot, head], masked(values, 1))
            att_ref[slot, :, pair * 128 : pair * 128 + 128] = total.astype(BF16)

    project(0)
    for k in range(HEADS + 2):
        for slot in range(2):
            if k < HEADS:
                first_part(slot, k)
            if k >= 2:
                third_part(slot, k - 2)
            if slot == 0 and k % 2 == 0 and k // 2 + 1 < pairs:
                project(k // 2 + 1)
            if 1 <= k <= HEADS:
                second_part(slot, k - 1)


def mlp_kernel(
    idx_ref, count_ref, x_hbm, cot_hbm, att_hbm, wo_ref, w1_ref, w2_ref, near_ref, far_ref, vec, b1,
    act_ref, middle_ref, dx_ref, datt_ref, w2, keep_ref, send_ref,
    acts, dpres, pres, dacts, wo, w1, wot, w1t, w2t, dn_half,
    gw1, gw2, gwo, gsmall, x_buf, cot_buf, att_buf, sem,
):
    step = pl.program_id(0)
    last = pl.num_programs(0) - 1
    half, width = wo_ref.shape
    hidden = w1_ref.shape[1]
    part = half // 2
    rows = 2 * ROWS
    core = idx_ref[1]

    @pl.when(step == 0)
    def _():
        for ref in (gw1, gw2, gwo, gsmall):
            ref[...] = jnp.zeros_like(ref)
        group = idx_ref[0]
        wo[at(group * half, half), :] = wo_ref[...]
        w1[at(group * half, half), :] = w1_ref[...]
        w2[at(group * (hidden // 2), hidden // 2), :] = w2_ref[...]
        other = (1 - group) * half
        for ref, which in ((near_ref, core), (far_ref, 1 - core)):
            wo[at(other + which * part, part), :] = ref[:, :width]
            w1[at(other + which * part, part), :] = ref[:, width : width + hidden]
            base = (1 - group) * (hidden // 2) + which * (hidden // 4)
            for k in range(hidden // width):
                w2[at(base + k * part, part), :] = ref[:, width + hidden + k * width : width + hidden + (k + 1) * width]
        wot[...] = wo[...].T
        w1t[...] = w1[...].T
        w2t[...] = w2[...].T

    x_ref, cot_ref, att_ref = fetch(
        [(x_hbm, x_buf), (cot_hbm, cot_buf), (att_hbm, att_buf)], sem, 0, step, last + 1
    )
    second_valid = (1 < count_ref[step, 0]).astype(F32)
    row = lax.broadcasted_iota(jnp.int32, (rows, 1), 0)
    valid = jnp.where(row < ROWS, 1.0, second_valid)
    att = att_ref[...].reshape(rows, width)
    middle = x_ref[...].reshape(rows, width).astype(F32) + mm(att, wo[...]) + vec[2:3, :]
    hat, rstd = normalize(middle)
    gain = vec[4:5, :]
    normed = (hat * gain + vec[5:6, :]).astype(BF16)
    d_out = cot_ref[...].reshape(rows, width).astype(F32) * valid
    d_mlp = d_out.astype(BF16)
    normed_t = jnp.concatenate([normed.T, jnp.ones((16, rows), BF16)], axis=0)
    d_mlp_t = d_mlp.T
    chunks = hidden // 256
    middle_of = hidden // 2

    def first_part(c):
        cols = slice(c * 256, c * 256 + 256)
        pres[c % 2] = mm(normed, w1[:, cols])
        dacts[c % 2] = mm(d_mlp, w2t[:, cols])

    def second_part(c):
        cols = slice(c * 256, c * 256 + 256)
        bias = b1[0:1, cols]
        for r in range(0, rows, 32):
            act, d_pre = gelu_parts(pres[c % 2, r : r + 32] + bias, dacts[c % 2, r : r + 32])
            acts[r : r + 32, cols] = act
            act_ref[r // ROWS, r % ROWS : r % ROWS + 16, cols] = act[:16]
            act_ref[(r + 16) // ROWS, (r + 16) % ROWS : (r + 16) % ROWS + 16, cols] = act[16:]
            dpres[r : r + 32, cols] = d_pre

    def third_part(c):
        cols = slice(c * 256, c * 256 + 256)
        gw1[:, cols] += mm(normed_t, dpres[:, cols])
        gw2[:, cols] += mm(d_mlp_t, acts[:, cols])

    for k in range(chunks + 2):
        if k < chunks:
            first_part(k)
        if k >= 2:
            third_part(k - 2)
        if k == chunks // 2 + 1:
            dn_half[...] = mm(dpres[:, :middle_of], w1t[:middle_of, :])
        if 1 <= k <= chunks:
            second_part(k - 1)

    middle_ref[...] = middle.reshape(2, ROWS, width)
    d_normed = dn_half[...] + mm(dpres[:, middle_of:], w1t[middle_of:, :])
    dx = d_out + norm_back(d_normed, hat, rstd, gain)
    d_attn = dx.astype(BF16)
    dx_ref[...] = d_attn.reshape(2, ROWS, width)
    datt_ref[...] = mm(d_attn, wot[...]).astype(BF16).reshape(2, ROWS, width)
    gwo[...] += mm_tn(att, d_attn)

    def fold(values):
        return jnp.sum(values.reshape(rows // 8, 8, width), axis=0)

    gsmall[0] += fold(d_out)
    gsmall[1] += fold(d_attn.astype(F32))
    gsmall[2] += fold(d_normed * hat)
    gsmall[3] += fold(d_normed)

    @pl.when(step == last)
    def _():
        quarter = half // 4
        wide = hidden // 8
        gw2_t = gw2[...].astype(BF16).T
        small_rows = [jnp.sum(gsmall[k], axis=0, keepdims=True) for k in range(4)]

        def emit(group, quad, ref, side):
            base = group * half + quad * quarter
            top = 0
            for col in range(hidden // width):
                ref[group, side, top : top + quarter, :] = gw1[
                    base : base + quarter, col * width : (col + 1) * width
                ].astype(BF16)
                top += quarter
            start = group * (hidden // 2) + quad * wide
            ref[group, side, top : top + wide, :] = gw2_t[start : start + wide]
            top += wide
            ref[group, side, top : top + quarter, :] = gwo[base : base + quarter, :].astype(BF16)
            top += quarter
            if quad < 2:
                start = group * (hidden // 2) + quad * width
                value = gw1[width : width + 1, start : start + width]
            else:
                own = slice(group * half, group * half + half)
                value = jnp.concatenate(
                    [small_rows[2 * quad - 4][:, own], small_rows[2 * quad - 3][:, own]], axis=1
                )
            ref[group, side, top : top + 16, :] = jnp.broadcast_to(value, (16, width)).astype(BF16)

        split_quads(core, emit, keep_ref, send_ref)


def split_quads(core, emit, keep_ref, send_ref):
    for mine in range(2):

        @pl.when(core == mine)
        def _():
            for group in range(2):
                for side in range(2):
                    emit(group, 2 * mine + side, keep_ref, side)
                    emit(group, 2 * (1 - mine) + side, send_ref, side)


def attention_back_kernel(
    first_micro, last, idx_ref, hat_hbm, qkv_hbm, prob_hbm, att_hbm, datt_hbm, w_ref, vec_ref, *refs
):
    carried = 0 if first_micro == 0 else 3
    dqkv_ref, total_ref, sums_ref = refs[carried : carried + 3]
    kv, hat_t, d_probs, d_scores = refs[-10:-6]
    buffers, sem = refs[-6:-1], refs[-1]
    step = pl.program_id(0)
    width = w_ref.shape[0]
    pairs = width // 128
    sources = (hat_hbm, datt_hbm, qkv_hbm, att_hbm, prob_hbm)
    hat_ref, datt_ref, qkv_ref, att_ref, prob_ref = fetch(
        list(zip(sources, buffers)), sem, first_micro, step, pl.num_programs(0)
    )

    @pl.when(step == 0)
    def _():
        kv[...] = jnp.zeros_like(kv)
        if not carried:
            total_ref[...] = jnp.zeros_like(total_ref)
            sums_ref[...] = jnp.zeros_like(sums_ref)

    hat_t[...] = hat_ref[...].reshape(2 * ROWS, width).astype(BF16).T
    for pair in range(pairs):
        kv[:, :ROWS, pair * 256 : pair * 256 + 256] = qkv_ref[:, :, pair * 384 + 128 : pair * 384 + 384]
    low_half = lax.broadcasted_iota(jnp.int32, (1, 128), 1) < 64

    def masked(values, head):
        mask = low_half if head % 2 == 0 else jnp.logical_not(low_half)
        return jnp.where(mask, values, jnp.zeros_like(values))

    def lanes(head):
        return slice(head // 2 * 128, head // 2 * 128 + 128)

    def first_part(slot, head):
        pair = head // 2
        d_probs[slot, head % 2] = mm_nt(
            datt_ref[slot, :, lanes(head)], masked(kv[slot, :, pair * 256 + 128 : pair * 256 + 256], head)
        )

    def second_part(slot, head):
        for r in range(0, ROWS, 16):
            rows = slice(r, r + 16)
            product = datt_ref[slot, rows, lanes(head)].astype(F32) * att_ref[slot, rows, lanes(head)].astype(F32)
            delta = jnp.sum(masked(product, head), axis=-1, keepdims=True)
            d_scores[slot, head % 4, rows] = (
                prob_ref[slot, head, rows].astype(F32) * (d_probs[slot, head % 2, rows] - delta)
            ).astype(BF16)

    def third_part(slot, pair):
        query = qkv_ref[slot, :, pair * 384 : pair * 384 + 128] * jnp.array(0.125, BF16)
        keys = kv[slot, :, pair * 256 : pair * 256 + 128] * jnp.array(0.125, BF16)
        d_att = datt_ref[slot, :, pair * 128 : pair * 128 + 128]
        dq = dk = dv = 0.0
        for head in (2 * pair, 2 * pair + 1):
            d_score = d_scores[slot, head % 4]
            dv = dv + mm_tn(prob_ref[slot, head], masked(d_att, head))
            dk = dk + mm_tn(d_score, masked(query, head))
            dq = dq + mm(d_score, masked(keys, head))
        top = pair * 384
        dqkv_ref[slot, :, top : top + 128] = dq.astype(BF16)
        dqkv_ref[slot, :, top + 128 : top + 256] = dk[:ROWS].astype(BF16)
        dqkv_ref[slot, :, top + 256 : top + 384] = dv[:ROWS].astype(BF16)

    def fourth_part(pair):
        columns = slice(pair * 384, pair * 384 + 384)
        joined_back = dqkv_ref[:, :, columns].reshape(2 * ROWS, 384)
        total_ref[:, columns] += mm(hat_t[...], joined_back)
        sums_ref[:, columns] += jnp.sum(joined_back.astype(F32).reshape(ROWS // 4, 8, 384), axis=0)

    for k in range(HEADS + 3):
        for slot in range(2):
            if k < HEADS:
                first_part(slot, k)
            if k >= 3 and k % 2 == 1:
                third_part(slot, k // 2 - 1)
            if slot == 0 and k >= 4 and k % 2 == 0:
                fourth_part(k // 2 - 2)
            if 1 <= k <= HEADS:
                second_part(slot, k - 1)

    if last:
        keep_ref, send_ref = refs[carried + 3 : carried + 5]

        @pl.when(step == pl.num_programs(0) - 1)
        def _():
            half = width // 2
            quarter = half // 4
            total_sums = jnp.sum(sums_ref[...], axis=0, keepdims=True)
            weights = w_ref[...].astype(F32)
            d_gain = jnp.sum((weights * total_ref[...]).reshape(width, 3 * width), axis=1, keepdims=True)
            d_shift = jnp.sum(weights * total_sums, axis=1, keepdims=True)
            columns = jnp.concatenate([vec_ref[...], jnp.zeros((120, width), F32)], axis=0).T
            gain, shift = columns[:, 0:1], columns[:, 1:2]
            total_ref[...] = total_ref[...] * gain + shift * total_sums
            lane = lax.broadcasted_iota(jnp.int32, (1, 128), 1)
            both = jnp.where(lane == 0, d_gain, jnp.where(lane == 1, d_shift, 0.0)).T

            def emit(group, quad, ref, side):
                base = group * half + quad * quarter
                for kind in range(3):
                    for pair in range(pairs):
                        source = slice((3 * pair + kind) * 128, (3 * pair + kind) * 128 + 128)
                        ref[group, side, kind * quarter : (kind + 1) * quarter, pair * 128 : pair * 128 + 128] = (
                            total_ref[base : base + quarter, source].astype(BF16)
                        )
                if quad == 0:
                    kind = 2 * group
                    value = jnp.concatenate(
                        [total_sums[:, (3 * p + kind) * 128 : (3 * p + kind) * 128 + 128] for p in range(pairs)], axis=1
                    )
                else:
                    own = slice(group * half, group * half + half)
                    value = jnp.concatenate([both[0:1, own], both[1:2, own]], axis=1)
                ref[group, side, 3 * quarter : 3 * quarter + 16, :] = jnp.broadcast_to(value, (16, width)).astype(BF16)

            split_quads(idx_ref[1], emit, keep_ref, send_ref)


def input_grad_kernel(hat_hbm, rstd_hbm, dqkv_hbm, dx_hbm, w_ref, vec_ref, din_ref, outs, wt, *refs):
    step = pl.program_id(0)
    width = w_ref.shape[0]
    micros = pl.num_programs(0)
    seq = din_ref.shape[0] * 128 // (width * 2 * micros)
    rows = 2 * ROWS
    sources = (hat_hbm, rstd_hbm, dqkv_hbm, dx_hbm)
    hat_ref, rstd_ref, dqkv_ref, dx_ref = fetch(list(zip(sources, refs[:-1])), refs[-1], 0, step, micros)

    @pl.when(step == 0)
    def _():
        wt[...] = w_ref[...].T

    d_normed = mm(dqkv_ref[...].reshape(rows, 3 * width), wt[...])
    hat = hat_ref[...].reshape(rows, width)
    rstd = rstd_ref[...].reshape(rows, 128)[:, 0:1]
    d_in = dx_ref[...].reshape(rows, width).astype(F32) + norm_back(d_normed, hat, rstd, vec_ref[0:1, :])
    for slot in range(2):
        write_image(outs, step, slot, seq, d_in[slot * ROWS : slot * ROWS + ROWS])

    @pl.when(step == micros - 1)
    def _():
        din_ref[...] = outs[...].astype(BF16)


def outputs_kernel(count_ref, act_hbm, middle_hbm, w2_ref, vec_ref, out_ref, outs, act_buf, middle_buf, sem):
    step = pl.program_id(0)
    hidden, width = w2_ref.shape
    micros = pl.num_programs(0)
    seq = out_ref.shape[0] * 128 // (width * 2 * micros)
    rows = 2 * ROWS
    act_ref, middle_ref = fetch([(act_hbm, act_buf), (middle_hbm, middle_buf)], sem, 0, step, micros)
    row = lax.broadcasted_iota(jnp.int32, (rows, 1), 0)
    valid = jnp.where(row < ROWS, 1.0, (1 < count_ref[step, 0]).astype(F32))
    mlp = mm(act_ref[...].reshape(rows, hidden), w2_ref[...]) + vec_ref[3:4, :]
    result = (middle_ref[...].reshape(rows, width) + mlp) * valid
    for slot in range(2):
        write_image(outs, step, slot, seq, result[slot * ROWS : slot * ROWS + ROWS])

    @pl.when(step == micros - 1)
    def _():
        out_ref[...] = outs[...].astype(BF16)


def per_pair(*shape):
    return pl.BlockSpec((2, *shape), lambda i: (i,) + (0,) * len(shape))


SMEM_SPEC = pl.BlockSpec(memory_space=pltpu.SMEM)


def run_attention(seq, idx, hat, w_qkv, near, far, small):
    count = hat.shape[0]
    width = w_qkv.shape[1] // 3
    return pl.pallas_call(
        partial(attention_kernel, seq),
        grid=(count // 2,),
        in_specs=[SMEM_SPEC, HBM_SPEC] + [VMEM_SPEC] * 4,
        out_specs=[
            per_pair(ROWS, 3 * width), per_pair(HEADS, ROWS, KEYS), per_pair(ROWS, width),
            VMEM_SPEC, VMEM_SPEC, VMEM_SPEC,
        ],
        out_shape=[
            pltpu.HBM((count, ROWS, 3 * width), BF16),
            pltpu.HBM((count, HEADS, ROWS, KEYS), BF16),
            pltpu.HBM((count, ROWS, width), BF16),
            jax.ShapeDtypeStruct((width, 3 * width), BF16),
            jax.ShapeDtypeStruct((8, width), F32),
            jax.ShapeDtypeStruct((8, 2 * small.shape[1]), F32),
        ],
        scratch_shapes=[
            pltpu.VMEM((2, KEYS, 2 * width), BF16),
            pltpu.VMEM((8, 3 * width), F32),
            pltpu.VMEM((2, 2, ROWS, KEYS), F32),
            pltpu.VMEM((2, 2, ROWS, width), F32),
            pltpu.SemaphoreType.DMA((1, 2)),
        ],
        compiler_params=pltpu.CompilerParams(vmem_limit_bytes=22 << 20),
        cost_estimate=pl.CostEstimate(flops=5 << 30, bytes_accessed=20 << 20, transcendentals=0),
        name="attention_fwd",
    )(idx, *in_hbm(hat), w_qkv, near, far, small)


def run_mlp(idx, counts, images, cot, att, wo, w1, w2, near, far, vec, b1):
    width = wo.shape[1]
    hidden = w1.shape[1]
    micro = counts.shape[0]
    rows = 2 * ROWS
    packed = width // 8 * (hidden // width) + hidden // 8 + width // 8 + 16
    two = pl.BlockSpec((2, ROWS, width), lambda i: (i, 0, 0))
    return pl.pallas_call(
        mlp_kernel,
        grid=(micro,),
        in_specs=[SMEM_SPEC, SMEM_SPEC, HBM_SPEC, HBM_SPEC, HBM_SPEC] + [VMEM_SPEC] * 7,
        out_specs=[per_pair(ROWS, hidden), two, two, two, VMEM_SPEC, VMEM_SPEC, VMEM_SPEC],
        out_shape=[
            pltpu.HBM((2 * micro, ROWS, hidden), BF16),
            pltpu.HBM(att.shape, F32),
            pltpu.HBM(att.shape, BF16),
            pltpu.HBM(att.shape, BF16),
            jax.ShapeDtypeStruct((hidden, width), BF16),
            jax.ShapeDtypeStruct((2, 2, packed, width), BF16),
            jax.ShapeDtypeStruct((2, 2, packed, width), BF16),
        ],
        scratch_shapes=[
            pltpu.VMEM((rows, hidden), BF16),
            pltpu.VMEM((rows, hidden), BF16),
            pltpu.VMEM((2, rows, 256), F32),
            pltpu.VMEM((2, rows, 256), F32),
            pltpu.VMEM((width, width), BF16),
            pltpu.VMEM((width, hidden), BF16),
            pltpu.VMEM((width, width), BF16),
            pltpu.VMEM((hidden, width), BF16),
            pltpu.VMEM((width, hidden), BF16),
            pltpu.VMEM((rows, width), F32),
            pltpu.VMEM((width + 16, hidden), F32),
            pltpu.VMEM((width, hidden), F32),
            pltpu.VMEM((width, width), F32),
            pltpu.VMEM((4, 8, width), F32),
            pltpu.VMEM((2, 2, ROWS, width), BF16),
            pltpu.VMEM((2, 2, ROWS, width), BF16),
            pltpu.VMEM((2, 2, ROWS, width), BF16),
            pltpu.SemaphoreType.DMA((3, 2)),
        ],
        compiler_params=pltpu.CompilerParams(vmem_limit_bytes=40 << 20),
        cost_estimate=pl.CostEstimate(flops=12 << 30, bytes_accessed=20 << 20, transcendentals=0),
        name="mlp_fwd_bwd",
    )(idx, counts, *in_hbm(images, cot, att), wo, w1, w2, near, far, vec, b1)


def run_attention_back(begin, end, idx, hat, qkv, prob, att, datt, w_qkv, vec, carried):
    count = qkv.shape[0]
    width = w_qkv.shape[0]
    packed = width // 8 * 3 + 16
    last = 2 * end == count
    block = pl.BlockSpec((2, ROWS, 3 * width), lambda i: (i + begin, 0, 0))
    two = lambda *shape: pltpu.VMEM((2, 2, *shape), BF16)
    return pl.pallas_call(
        partial(attention_back_kernel, begin, last),
        grid=(end - begin,),
        in_specs=[SMEM_SPEC] + [HBM_SPEC] * 5 + [VMEM_SPEC] * 2
        + ([HBM_SPEC, VMEM_SPEC, VMEM_SPEC] if carried else []),
        out_specs=[block, VMEM_SPEC, VMEM_SPEC] + ([VMEM_SPEC] * 2 if last else []),
        out_shape=[
            pltpu.HBM((count, ROWS, 3 * width), BF16),
            jax.ShapeDtypeStruct((width, 3 * width), F32),
            jax.ShapeDtypeStruct((8, 3 * width), F32),
        ]
        + [jax.ShapeDtypeStruct((2, 2, packed, width), BF16)] * (2 if last else 0),
        scratch_shapes=[
            pltpu.VMEM((2, KEYS, 2 * width), BF16),
            pltpu.VMEM((width, 2 * ROWS), BF16),
            pltpu.VMEM((2, 2, ROWS, KEYS), F32),
            pltpu.VMEM((2, 4, ROWS, KEYS), BF16),
            pltpu.VMEM((2, 2, ROWS, width), F32),
            two(ROWS, width), two(ROWS, 3 * width), two(ROWS, width), two(HEADS, ROWS, KEYS),
            pltpu.SemaphoreType.DMA((5, 2)),
        ],
        input_output_aliases={8: 0, 9: 1, 10: 2} if carried else {},
        compiler_params=pltpu.CompilerParams(vmem_limit_bytes=18 << 20),
        cost_estimate=pl.CostEstimate(flops=(end - begin) << 31, bytes_accessed=20 << 20, transcendentals=0),
    )(idx, *in_hbm(hat, qkv, prob, att, datt), w_qkv, vec, *in_hbm(*carried[:1]), *carried[1:])


def run_input_grad(view_shape, hat, rstd, dqkv, dx, w_qkv, vec):
    count = dqkv.shape[0]
    width = w_qkv.shape[0]
    two = lambda dtype, *shape: pltpu.VMEM((2, 2, *shape), dtype)
    return pl.pallas_call(
        input_grad_kernel,
        grid=(count // 2,),
        in_specs=[HBM_SPEC] * 4 + [VMEM_SPEC] * 2,
        out_specs=VMEM_SPEC,
        out_shape=jax.ShapeDtypeStruct(view_shape, BF16),
        scratch_shapes=[
            pltpu.VMEM(view_shape, F32),
            pltpu.VMEM((3 * width, width), BF16),
            two(F32, ROWS, width), two(F32, ROWS, 128), two(BF16, ROWS, 3 * width), two(BF16, ROWS, width),
            pltpu.SemaphoreType.DMA((4, 2)),
        ],
        compiler_params=pltpu.CompilerParams(vmem_limit_bytes=14 << 20),
        cost_estimate=pl.CostEstimate(flops=2 << 30, bytes_accessed=20 << 20, transcendentals=0),
        name="input_grad",
    )(*in_hbm(hat, rstd, dqkv, dx), w_qkv, vec)


def run_outputs(view_shape, counts, act, middle, w2, vec):
    count, _, hidden = act.shape
    width = w2.shape[1]
    return pl.pallas_call(
        outputs_kernel,
        grid=(count // 2,),
        in_specs=[SMEM_SPEC] + [HBM_SPEC] * 2 + [VMEM_SPEC] * 2,
        out_specs=VMEM_SPEC,
        out_shape=jax.ShapeDtypeStruct(view_shape, BF16),
        scratch_shapes=[
            pltpu.VMEM(view_shape, F32),
            pltpu.VMEM((2, 2, ROWS, hidden), BF16), pltpu.VMEM((2, 2, ROWS, width), F32),
            pltpu.SemaphoreType.DMA((2, 2)),
        ],
        compiler_params=pltpu.CompilerParams(vmem_limit_bytes=14 << 20),
        cost_estimate=pl.CostEstimate(flops=2 << 30, bytes_accessed=20 << 20, transcendentals=0),
        name="layer_outputs",
    )(counts, *in_hbm(act, middle), w2, vec)


def merge_kernel(which, idx_ref, a_ref, b_ref, own_ref, other_ref):
    mine = idx_ref[which]
    own_ref[...] = a_ref[mine] + b_ref[mine]
    other_ref[...] = a_ref[1 - mine] + b_ref[1 - mine]


def merge(idx, which, a, b):
    return pl.pallas_call(
        partial(merge_kernel, which),
        in_specs=[SMEM_SPEC, VMEM_SPEC, VMEM_SPEC],
        out_specs=[VMEM_SPEC, VMEM_SPEC],
        out_shape=[jax.ShapeDtypeStruct(a.shape[1:], BF16)] * 2,
        compiler_params=pltpu.CompilerParams(vmem_limit_bytes=4 << 20),
    )(idx, a, b)


def flip(value, axis, size, bit):
    return lax.ppermute(value, axis, [(i, i ^ bit) for i in range(size)])


def exchange(own, replicas, bit):
    while bit < replicas:
        got = flip(own, "replica", replicas, bit)
        own = own + got
        bit *= 2
    return own


def reduce_grads(idx, keep, send, replicas):
    own, other = merge(idx, 0, keep, flip(send, "replica", replicas, 1))
    own, other = merge(idx, 2, own, flip(other, "group", 2, 1))
    got = flip(other, "replica", replicas, 2)
    own = own + got
    own = exchange(own, replicas, 4)
    side = flip(own, "replica", replicas, 2)
    far_own = flip(own, "replica", replicas, 1)
    return own, side, far_own, flip(side, "replica", replicas, 1)


def reduce_large_grads(idx, keep, send, replicas):
    own, other = merge(idx, 0, keep, flip(send, "replica", replicas, 1))
    own, other = merge(idx, 2, own, flip(other, "group", 2, 1))
    halves = (2, own.shape[0] // 2, own.shape[1])
    got = flip(other, "replica", replicas, 2)
    own, other = merge(idx, 3, own.reshape(halves), got.reshape(halves))
    got = flip(other, "replica", replicas, 4)
    own = own + got
    own = exchange(own, replicas, 8)
    next_own = flip(own, "replica", replicas, 4)
    side = flip(own, "replica", replicas, 2)
    next_side = flip(next_own, "replica", replicas, 2)
    parts = (own, next_own, side, next_side)
    far = [flip(part, "replica", replicas, 1) for part in parts]
    return (*parts, *far)


def places(idx_ref):
    core, side = idx_ref[1], idx_ref[2]
    return 2 * core + side, 2 * core + 1 - side, 2 * (1 - core) + side, 2 * (1 - core) + 1 - side


def unpack_mlp_kernel(idx_ref, *refs):
    ins, outs, mlp = refs[:8], refs[8:16], refs[16]
    low = idx_ref[3]
    lines = ins[0].shape[0]
    for k, place in enumerate(places(idx_ref)):
        mlp[place, at(low * lines, lines)] = ins[2 * k][...].astype(F32)
        mlp[place, at((1 - low) * lines, lines)] = ins[2 * k + 1][...].astype(F32)
    g_out, g_bout, g_fc1, g_bfc1, g_fc2, g_bfc2, g_gtwo, g_stwo = outs
    half, width = g_out.shape
    hidden = g_fc1.shape[1]
    quarter = half // 4
    wide = hidden // 8
    for quad in range(4):
        rows = slice(quad * quarter, (quad + 1) * quarter)
        top = 0
        for col in range(hidden // width):
            g_fc1[rows, col * width : (col + 1) * width] = mlp[quad, top : top + quarter]
            top += quarter
        g_fc2[quad * wide : (quad + 1) * wide] = mlp[quad, top : top + wide]
        top += wide
        g_out[rows] = mlp[quad, top : top + quarter]
        top += quarter
        value = mlp[quad, top : top + 1]
        if quad < 2:
            g_bfc1[quad * width : (quad + 1) * width] = value.reshape(width)
        elif quad == 2:
            g_bfc2[...] = value[:, :half].reshape(half)
            g_bout[...] = value[:, half:].reshape(half)
        else:
            g_gtwo[...] = value[:, :half].reshape(half)
            g_stwo[...] = value[:, half:].reshape(half)


def unpack_attention_kernel(idx_ref, *refs):
    ins, outs, att = refs[:4], refs[4:8], refs[8]
    for k, place in enumerate(places(idx_ref)):
        att[place] = ins[k][...].astype(F32)
    g_qkv, g_bqv, g_gone, g_sone = outs
    half = g_qkv.shape[0]
    width = 2 * half
    quarter = half // 4
    for quad in range(4):
        rows = slice(quad * quarter, (quad + 1) * quarter)
        for col in range(3):
            g_qkv[rows, col * width : (col + 1) * width] = att[quad, col * quarter : (col + 1) * quarter]
        value = att[quad, 3 * quarter : 3 * quarter + 1]
        if quad == 0:
            g_bqv[...] = value.reshape(width)
        elif quad == 1:
            g_gone[...] = value[:, :half].reshape(half)
            g_sone[...] = value[:, half:].reshape(half)


def run_unpack(kernel, idx, parts, shapes):
    return pl.pallas_call(
        kernel,
        in_specs=[SMEM_SPEC] + [VMEM_SPEC] * len(parts),
        out_specs=[VMEM_SPEC] * len(shapes),
        out_shape=[jax.ShapeDtypeStruct(s, F32) for s in shapes],
        scratch_shapes=[pltpu.VMEM((4, parts[0].shape[0] * len(parts) // 4, parts[0].shape[1]), F32)],
        compiler_params=pltpu.CompilerParams(vmem_limit_bytes=8 << 20),
    )(idx, *parts)


def interleaved(images):
    micro, slots, seq, width = images.shape
    blocks = images.reshape(micro, slots, seq, width // 128, 128)
    blocks = with_layout_constraint(blocks, Layout(major_to_minor=(0, 2, 3, 1, 4)))
    return blocks.transpose(0, 2, 3, 1, 4).reshape(-1, 128)


def separated(rows, shape):
    micro, slots, seq, width = shape
    blocks = rows.reshape(micro, seq, width // 128, slots, 128).transpose(0, 1, 3, 2, 4)
    return blocks.reshape(micro, seq, slots, width).transpose(0, 2, 1, 3)


SPLITS = ((0, 1), (1, 4))


def local(
    replicas,
    images, image_count, cotangent, w_qkv, b_qv, w_out, b_out, w_fc1, b_fc1, w_fc2, b_fc2,
    gain_one, shift_one, gain_two, shift_two,
):
    replica = lax.axis_index("replica")
    idx = jnp.stack([lax.axis_index("group"), replica & 1, (replica >> 1) & 1, (replica >> 2) & 1]).astype(jnp.int32)
    count = images.shape[0] * images.shape[1]
    width = images.shape[3]
    vectors = (b_qv, b_out, b_fc1, b_fc2, gain_one, shift_one, gain_two, shift_two)
    first, small = run_pack_first(idx, w_qkv, vectors)
    second = run_pack_second(idx, w_out, w_fc1, w_fc2)
    near_first = flip(first, "group", 2, 1)
    near_second = flip(second, "group", 2, 1)
    far_first = flip(near_first, "replica", replicas, 1)
    far_second = flip(near_second, "replica", replicas, 1)
    view = interleaved(images)
    image_rows, hat, rstd = run_prepare(
        prepare_images_kernel, view, count, width, ((width, BF16), (width, F32), (128, F32))
    )
    (cot_rows,) = run_prepare(prepare_cotangent_kernel, interleaved(cotangent), count, width, ((width, BF16),))
    qkv, prob, att, w_all, vec, b1 = run_attention(
        images.shape[2], idx, hat, w_qkv, near_first, far_first, small
    )
    act, middle, dx, datt, w_two, keep_b, send_b = run_mlp(
        idx, image_count, image_rows, cot_rows, att, w_out, w_fc1, w_fc2, near_second, far_second, vec, b1
    )
    carried = ()
    for begin, end in SPLITS:
        carried = run_attention_back(begin, end, idx, hat, qkv, prob, att, datt, w_all, vec, carried)
    dqkv, _, _, keep_c, send_c = carried
    din = run_input_grad(view.shape, hat, rstd, dqkv, dx, w_all, vec)
    out = run_outputs(view.shape, image_count, act, middle, w_two, vec)
    mlp = reduce_large_grads(idx, keep_b, send_b, replicas)
    attention = reduce_grads(idx, keep_c, send_c, replicas)
    shape_of = lambda *arrays: [v.shape for v in arrays]
    g_out, g_bout, g_fc1, g_bfc1, g_fc2, g_bfc2, g_gtwo, g_stwo = run_unpack(
        unpack_mlp_kernel, idx, mlp,
        shape_of(w_out, b_out, w_fc1, b_fc1, w_fc2, b_fc2, gain_two, shift_two),
    )
    g_qkv, g_bqv, g_gone, g_sone = run_unpack(
        unpack_attention_kernel, idx, attention, shape_of(w_qkv, b_qv, gain_one, shift_one)
    )
    return (
        separated(out, images.shape), separated(din, images.shape),
        g_qkv, g_bqv, g_out, g_bout, g_fc1, g_bfc1, g_fc2, g_bfc2, g_gone, g_sone, g_gtwo, g_stwo,
    )


def step(replicas, *args):
    return local(replicas, *args)


def solution(mesh):
    split = P(None, ("group", "replica"), None, None)
    matrix, vector = P("group", None), P("group")
    return jax.shard_map(
        partial(step, mesh.shape["replica"]),
        mesh=mesh,
        in_specs=(split, P(None, ("group", "replica")), split)
        + (matrix, vector) * 4
        + (vector,) * 4,
        out_specs=(split, split) + (matrix, vector) * 4 + (vector,) * 4,
        check_vma=False,
    )
```
